32 devices in a mesh: frame: 4 (over y, core), row: 8 (over z, x).
Axes of the slice: x: 2, y: 2, z: 4, core: 2. Of those that a mesh axis runs over, the one named last changes fastest.
Arguments:
- tokens: bfloat16 [2, 8, 8, 32, 1536], P(None, 'frame', 'row'), may hold values from -6 to 6
- w_query: bfloat16 [1536, 1536], P(('frame', 'row')), may hold values from -0.15625 to 0.15625
- w_key: bfloat16 [1536, 1536], P(('frame', 'row')), may hold values from -0.15625 to 0.15625
- w_value: bfloat16 [1536, 1536], P(('frame', 'row')), may hold values from -0.15625 to 0.15625
- w_out: bfloat16 [1536, 1536], P(('frame', 'row')), may hold values from -0.15625 to 0.15625
- w_gate: bfloat16 [1536, 4096], P(('frame', 'row')), may hold values from -0.15625 to 0.15625
- w_up: bfloat16 [1536, 4096], P(('frame', 'row')), may hold values from -0.15625 to 0.15625
- w_down: bfloat16 [4096, 1536], P(('frame', 'row')), may hold values from -0.09375 to 0.09375
- w_cap_key: bfloat16 [1536, 1536], P(None, ('frame', 'row')), may hold values from -0.15625 to 0.15625
- w_cap_value: bfloat16 [1536, 1536], P(None, ('frame', 'row')), may hold values from -0.15625 to 0.15625
- w_mod: bfloat16 [1536, 6144], P(None, ('frame', 'row')), may hold values from -0.3125 to 0.3125
- norm_gains: float32 [7, 1536], replicated, may hold values from 0.1 to 1.9
- mix_coefs: float32 [3, 1536], replicated, may hold values from -0.9 to 0.9
- caption: bfloat16 [2, 256, 1536], replicated, may hold values from -6 to 6
- cap_len: int32 [2], replicated, may hold values from 64 to 256, as said below
- cap_mask: int32 [2, 256], replicated, may hold values from 0 to 1, as said below
- timesteps: int32 [2], replicated, may hold values from 0 to 999
- frame_pos: int32 [2, 8], P(None, 'frame'), may hold values from 0 to 63
- row_pos: int32 [8], P('row'), may hold values from 0 to 63
- col_pos: int32 [32], replicated, may hold values from 0 to 63
- grad_out: bfloat16 [2, 8, 8, 32, 1536], P(None, 'frame', 'row'), may hold values from -6 to 6
Outputs:
- output: bfloat16 [2, 8, 8, 32, 1536], P(None, 'frame', 'row')
- grad_tokens: float32 [2, 8, 8, 32, 1536], P(None, 'frame', 'row')
- d_w_query: float32 [1536, 1536], P('row', 'frame')
- d_w_key: float32 [1536, 1536], P('row', 'frame')
- d_w_value: float32 [1536, 1536], P('row', 'frame')
- d_w_out: float32 [1536, 1536], P('row', 'frame')
- d_w_gate: float32 [1536, 4096], P('row', 'frame')
- d_w_up: float32 [1536, 4096], P('row', 'frame')
- d_w_down: float32 [4096, 1536], P('row', 'frame')
- d_w_cap_key: float32 [1536, 1536], P(None, ('frame', 'row'))
- d_w_cap_value: float32 [1536, 1536], P(None, ('frame', 'row'))
- d_w_mod: float32 [1536, 6144], P(None, ('frame', 'row'))
- d_norm_gains: float32 [7, 1536], P(None, ('frame', 'row'))
- d_mix_coefs: float32 [3, 1536], P(None, ('frame', 'row'))
The draws below stay inside these ranges and needn't reach their ends.
Inputs may be any that keep to these rules, and one draw needn't show every extreme that they name: `cap_len`: every clip has 64 to 256 caption tokens, and some clip has all 256. `cap_mask`: the first caption token of every clip is kept.
All inputs are finite; a program needn't handle non-finite values.
Results may differ from the reference program's by a relative error of at most 0.023.
Values may be sent and summed in bfloat16 or wider, within the bound.
No kernel may reach another device: no remote copies, remote signals or barrier semaphores. Data moves between devices by JAX's collectives and lax.ppermute only.
A program may use at most 704 MiB of HBM per device.

```python
import math
import jax
import jax.numpy as jnp
from jax import lax

D = 1536
HEADS = 24
HDIM = 64
FF = 4096
CAP = 256
CLIPS = 2
COLS = 32
FRAMES = 8
ROWS = 8
SEQ = 2048


def draw_cap_len(key, part):
    key_len, key_pick = jax.random.split(key)
    lengths = jax.random.randint(key_len, (CLIPS,), CAP // 4, CAP + 1)
    chosen = jax.random.randint(key_pick, (), 0, CLIPS)
    return jnp.where(jnp.arange(CLIPS) == chosen, CAP, lengths).astype(jnp.int32)


def draw_cap_mask(key, part):
    coin_draw = jax.random.randint(key, (CLIPS, CAP), 0, 4)
    kept_mask = jnp.where(coin_draw > 0, 1, 0)
    return jnp.where(jnp.arange(CAP)[None, :] == 0, 1, kept_mask).astype(jnp.int32)


def set_ends(values, stream_key, smallest, largest):
    longest = values.shape.index(max(values.shape))
    spots = []
    for shift in (0, 1):
        where = [jax.random.randint(jax.random.fold_in(stream_key, axis), (), 0, length) for axis, length in enumerate(values.shape)]
        where[longest] = (where[longest] + shift) % values.shape[longest]
        spots.append(tuple(where))
    return values.at[spots[0]].set(smallest).at[spots[1]].set(largest)


def levels(own_key, extent, shards, smallest, largest):
    loudness, own = 1.0, jax.random.fold_in(own_key, 6)
    for position, blocks in shards:
        heights = jnp.exp(jax.random.uniform(jax.random.fold_in(own, position), (blocks,), jnp.float32, smallest / len(shards), largest / len(shards)))
        loudness = loudness * jnp.repeat(heights, extent[position] // blocks).reshape([-1 if axis == position else 1 for axis in range(len(extent))])
    return loudness


def noise(key, dims, width, reach, shards=(), kind=jnp.bfloat16):
    drawn = width * jax.random.normal(key, dims, jnp.float32)
    if shards:
        drawn = drawn * levels(key, dims, shards, -0.22, 0.18)
    return jnp.clip(drawn, -reach, reach).astype(kind)


def setup_inputs(seed: int = 0) -> dict:
    streams_of = jax.random.split(jax.random.key(seed), 22)
    tokens = noise(streams_of[0], (CLIPS, FRAMES, ROWS, COLS, D), 1.0, 6.0, ((1, 4), (2, 8)))
    w_query = noise(streams_of[1], (D, D), D ** -0.5, 0.15625, ((0, 32),))
    w_key = noise(streams_of[2], (D, D), D ** -0.5, 0.15625, ((0, 32),))
    w_value = noise(streams_of[3], (D, D), D ** -0.5, 0.15625, ((0, 32),))
    w_out = noise(streams_of[4], (D, D), D ** -0.5, 0.15625, ((0, 32),))
    w_gate = noise(streams_of[5], (D, FF), D ** -0.5, 0.15625, ((0, 32),))
    w_up = noise(streams_of[6], (D, FF), D ** -0.5, 0.15625, ((0, 32),))
    w_down = noise(streams_of[7], (FF, D), FF ** -0.5, 0.09375, ((0, 32),))
    w_cap_key = noise(streams_of[8], (D, D), D ** -0.5, 0.15625, ((1, 32),))
    w_cap_value = noise(streams_of[9], (D, D), D ** -0.5, 0.15625, ((1, 32),))
    w_mod = noise(streams_of[10], (D, 4 * D), (D // 4) ** -0.5, 0.3125, ((1, 32),))
    norm_gains = jnp.clip(1.0 + 0.18 * jax.random.normal(streams_of[11], (7, D), jnp.float32), 0.1, 1.9)
    mix_coefs = jnp.clip(jax.random.uniform(streams_of[12], (3, D), jnp.float32, -0.9, 0.9), -0.9, 0.9)
    caption = noise(streams_of[13], (CLIPS, CAP, D), 1.0, 6.0)
    cap_len = draw_cap_len(jax.random.fold_in(streams_of[21], 71), 0)
    cap_mask = draw_cap_mask(jax.random.fold_in(streams_of[21], 71), 0)
    timesteps = jax.random.randint(streams_of[16], (CLIPS,), 0, 1000).astype(jnp.int32)
    frame_pos = set_ends(jax.random.randint(streams_of[17], (CLIPS, FRAMES), 0, 64), jax.random.fold_in(streams_of[17], 1), 0, 63).astype(jnp.int32)
    row_pos = set_ends(jax.random.randint(streams_of[18], (ROWS,), 0, 64), jax.random.fold_in(streams_of[18], 1), 0, 63).astype(jnp.int32)
    col_pos = set_ends(jax.random.randint(streams_of[19], (COLS,), 0, 64), jax.random.fold_in(streams_of[19], 1), 0, 63).astype(jnp.int32)
    grad_out = noise(streams_of[20], (CLIPS, FRAMES, ROWS, COLS, D), 1.0, 6.0, ((1, 4), (2, 8)))
    return dict(tokens=tokens, w_query=w_query, w_key=w_key, w_value=w_value, w_out=w_out, w_gate=w_gate, w_up=w_up, w_down=w_down, w_cap_key=w_cap_key, w_cap_value=w_cap_value, w_mod=w_mod, norm_gains=norm_gains, mix_coefs=mix_coefs, caption=caption, cap_len=cap_len, cap_mask=cap_mask, timesteps=timesteps, frame_pos=frame_pos, row_pos=row_pos, col_pos=col_pos, grad_out=grad_out)


EPS = 1e-05
THETA = 10000.0
NEG = -1000000000.0
HIGH = lax.Precision.HIGHEST

@jax.custom_vjp
def low(v):
    return lax.optimization_barrier(v.astype(jnp.bfloat16)).astype(jnp.float32)

@jax.custom_vjp
def low_back(v):
    return v

def low_keep(v):
    return (low(v), None)

def low_pass(kept, grad):
    return (grad,)

def back_keep(v):
    return (v, None)

def back_low(kept, grad):
    return (low(grad),)
low.defvjp(low_keep, low_pass)
low_back.defvjp(back_keep, back_low)

def rms_norm(tensor, gain):
    return tensor * lax.rsqrt(lax.optimization_barrier(jnp.mean(tensor * tensor, axis=-1, keepdims=True)) + EPS) * gain

def freq_table(size):
    return jnp.exp(-math.log(THETA) * 2.0 * jnp.arange(size // 2, dtype=jnp.float32) / size)

def rotary_tables(pos_frame, pos_row, pos_col, head_dim):
    leading = head_dim // 4
    remain = (head_dim - leading) // 2
    angles = jnp.concatenate([pos_frame[..., None] * freq_table(leading), pos_row[..., None] * freq_table(remain), pos_col[..., None] * freq_table(remain)], axis=-1)
    return (jnp.cos(angles), jnp.sin(angles))

def rotate(tensor, cosine, sine_table):
    head_dim = tensor.shape[-1]
    leading = head_dim // 4
    remain = (head_dim - leading) // 2
    bounds = [(0, leading), (leading, leading + remain), (leading + remain, head_dim)]
    lower_half = jnp.concatenate([tensor[..., a:a + (b - a) // 2] for a, b in bounds], axis=-1)
    upper_half = jnp.concatenate([tensor[..., a + (b - a) // 2:b] for a, b in bounds], axis=-1)
    turned_low = lower_half * cosine - upper_half * sine_table
    turned_high = lower_half * sine_table + upper_half * cosine
    pieces = []
    offset = 0
    for a, b in bounds:
        size_half = (b - a) // 2
        pieces.append(turned_low[..., offset:offset + size_half])
        pieces.append(turned_high[..., offset:offset + size_half])
        offset = offset + size_half
    return jnp.concatenate(pieces, axis=-1)

def project(tensor, weight):
    return jnp.dot(tensor, weight, precision=HIGH, preferred_element_type=jnp.float32)

def attention(query_rot, query_cap, key_rot, value_self, key_cap, value_cap, usable):
    score_scale = HDIM ** (-0.5)
    blocks = SEQ // 512

    def per_clip(inputs):
        q_rot, q_cap, k_rot, v_self, k_cap, v_cap, kept_keys = inputs

        def per_block(pair):
            block_rot, block_cap = pair
            scores = low_back(jnp.einsum('qhd,khd->qhk', block_rot, k_rot, precision=HIGH) * score_scale)
            probs = jax.nn.softmax(scores, axis=-1)
            out_self = jnp.einsum('qhk,khd->qhd', low(probs), v_self, precision=HIGH)
            cross = low_back(jnp.einsum('qhd,khd->qhk', block_cap, k_cap, precision=HIGH) * score_scale)
            cross = jnp.where(kept_keys[None, None, :], cross, NEG)
            cross_probs = jax.nn.softmax(cross, axis=-1)
            out_cross = jnp.einsum('qhk,khd->qhd', low(cross_probs), v_cap, precision=HIGH)
            return (out_self.reshape(512, D), out_cross.reshape(512, D))
        pairs = (q_rot.reshape(blocks, 512, HEADS, HDIM), q_cap.reshape(blocks, 512, HEADS, HDIM))
        out_self, out_cross = lax.map(jax.checkpoint(per_block), pairs)
        return (out_self.reshape(SEQ, D), out_cross.reshape(SEQ, D))
    return lax.map(per_clip, (query_rot, query_cap, key_rot, value_self, key_cap, value_cap, usable))

def reference(tokens, w_query, w_key, w_value, w_out, w_gate, w_up, w_down, w_cap_key, w_cap_value, w_mod, norm_gains, mix_coefs, caption, cap_len, cap_mask, timesteps, frame_pos, row_pos, col_pos, grad_out):
    ftype = jnp.float32
    half_width = D // 2
    frequencies = jnp.exp(-math.log(THETA) * jnp.arange(half_width, dtype=ftype) / half_width)
    phases = timesteps.astype(ftype)[:, None] * frequencies[None, :]
    step_embed = low(jax.nn.silu(jnp.concatenate([jnp.cos(phases), jnp.sin(phases)], axis=1)))
    grid_shape = (CLIPS, FRAMES, ROWS, COLS)
    pos_frame = jnp.broadcast_to((frame_pos + cap_len[:, None]).astype(ftype)[:, :, None, None], grid_shape).reshape(CLIPS, SEQ)
    pos_row = jnp.broadcast_to(row_pos.astype(ftype)[None, None, :, None], grid_shape).reshape(CLIPS, SEQ)
    pos_col = jnp.broadcast_to(col_pos.astype(ftype)[None, None, None, :], grid_shape).reshape(CLIPS, SEQ)
    cosine, sine_table = rotary_tables(pos_frame, pos_row, pos_col, HDIM)
    cosine = cosine[:, :, None, :]
    sine_table = sine_table[:, :, None, :]
    usable = (jnp.arange(CAP)[None, :] < cap_len[:, None]) & (cap_mask > 0)
    cap_float = caption.astype(ftype)

    def forward(x_in, wq, wk, wv, wo, w_one, w_three, w_two, wkc, wvc, wmod, gains, mixes):
        modulate = low(low_back(project(step_embed, wmod)))
        scale_a = modulate[:, :D]
        gate_a = modulate[:, D:2 * D]
        scale_f = modulate[:, 2 * D:3 * D]
        gate_f = modulate[:, 3 * D:]
        x_flat = x_in.reshape(CLIPS, SEQ, D)
        h_in = low(rms_norm(x_flat, gains[0]) * (1.0 + scale_a[:, None, :]))
        q_zero = low_back(project(h_in, wq))
        k_zero = low_back(project(h_in, wk))
        v_self = low(low_back(project(h_in, wv)))
        q_norm = rms_norm(q_zero, gains[4])
        k_norm = rms_norm(k_zero, gains[5])
        q_rot = low(rotate(q_norm.reshape(CLIPS, SEQ, HEADS, HDIM), cosine, sine_table))
        k_rot = low(rotate(k_norm.reshape(CLIPS, SEQ, HEADS, HDIM), cosine, sine_table))
        q_cap = low(q_norm).reshape(CLIPS, SEQ, HEADS, HDIM)
        k_cap = low(rms_norm(low_back(project(cap_float, wkc)), gains[6])).reshape(CLIPS, CAP, HEADS, HDIM)
        v_cap = low(low_back(project(cap_float, wvc))).reshape(CLIPS, CAP, HEADS, HDIM)
        out_self, out_cross = attention(q_rot, q_cap, k_rot, v_self.reshape(CLIPS, SEQ, HEADS, HDIM), k_cap, v_cap, usable)
        out_self = low_back(out_self)
        out_cross = low_back(out_cross)
        attn_mix = low(out_self + jnp.tanh(mixes[0]) * out_cross)
        y_one = low_back(project(attn_mix, wo))
        h_mid = x_flat + jnp.tanh(gate_a)[:, None, :] * rms_norm(y_one, gains[1])
        f_in = low(rms_norm(h_mid, gains[2]) * (1.0 + scale_f[:, None, :]))
        gate_pre = low_back(project(f_in, w_one))
        up_proj = low_back(project(f_in, w_three))
        hidden = low(jax.nn.silu(gate_pre) * up_proj)
        z_out = low_back(project(hidden, w_two))
        y_all = h_mid + jnp.tanh(gate_f)[:, None, :] * rms_norm(z_out, gains[3])
        y_all = y_all.reshape(CLIPS, FRAMES, ROWS, COLS, D)
        zero_row = jnp.zeros_like(y_all[:, :, :1])
        above = jnp.concatenate([zero_row, y_all[:, :, :-1]], axis=2)
        below = jnp.concatenate([y_all[:, :, 1:], zero_row], axis=2)
        return y_all + mixes[1] * above + mixes[2] * below
    primals = (tokens.astype(ftype), w_query.astype(ftype), w_key.astype(ftype), w_value.astype(ftype), w_out.astype(ftype), w_gate.astype(ftype), w_up.astype(ftype), w_down.astype(ftype), w_cap_key.astype(ftype), w_cap_value.astype(ftype), w_mod.astype(ftype), norm_gains.astype(ftype), mix_coefs.astype(ftype))
    result, pullback = jax.vjp(forward, *primals)
    grads = pullback(grad_out.astype(ftype))
    return (result.astype(jnp.bfloat16), grads[0], grads[1], grads[2], grads[3], grads[4], grads[5], grads[6], grads[7], grads[8], grads[9], grads[10], grads[11], grads[12])
```

```python
import functools
import math

import jax
import jax.numpy as jnp
from jax import lax
from jax.experimental import pallas as pl
from jax.experimental.pallas import tpu as pltpu
from jax.sharding import Mesh
from jax.sharding import PartitionSpec as P

HDIM = 64
EPS = 1e-05
THETA = 10000.0
NEG = -1000000000.0
F32 = jnp.float32
BF16 = jnp.bfloat16
RING = 8
ROW = ("far", "row")
ALL = ("frame", "far", "row")


def swap(value, bits):
    return lax.ppermute(value, "frame", [(i, i ^ bits) for i in range(lax.axis_size("frame"))])


def frame_sum(value):
    value = value + swap(value, 1)
    return value + swap(value, 2)


def token_sum(value):
    blocks = value.reshape(value.shape[0], 4, -1)
    got = swap(blocks, 1).reshape(value.shape[0], 2, 2, -1)
    blocks = blocks + got[:, :, ::-1].reshape(blocks.shape)
    got = swap(blocks, 2)
    blocks = blocks + jnp.concatenate([got[:, 2:], got[:, :2]], axis=1)
    return blocks.reshape(value.shape)


def frame_gather(value):
    over = swap(value, 2)
    pair = swap(jnp.stack([value, over]), 1)
    return jnp.stack([value, pair[0], over, pair[1]])


def frame_scatter(terms):
    low = terms.astype(BF16)
    got = swap(jnp.stack([low[1], low[3]]), 1).astype(F32)
    far = (terms[2] + got[1]).astype(BF16)
    return terms[0] + got[0] + swap(far, 2).astype(F32)


def row_neighbours(block):
    count = lax.axis_size(ROW)
    forward = [(i, i + 1) for i in range(count - 1)]
    above = lax.ppermute(block, ROW, forward)
    below = lax.ppermute(block, ROW, [(b, a) for a, b in forward])
    return above, below


def row_gather(block):
    return lax.all_gather(block, ROW, axis=0, tiled=True)


def row_scatter(terms):
    return lax.psum_scatter(terms, ROW, scatter_dimension=0, tiled=True)


def to_owner(block):
    frames, rows = lax.axis_size("frame"), lax.axis_size(ROW)
    part = rows // frames
    pairs = []
    for f in range(frames):
        for c in range(frames):
            for h in range(part):
                pairs.append((f * rows + c * part + h, c * rows + f * part + h))
    return lax.ppermute(block, ALL, pairs)


def owners(pair):
    j, k = divmod(pair, 3)
    if k == 1:
        return [(2 * j, 1, (0, 1)), (2 * j + 1, 1, (2, 3))]
    return [(2 * j + k // 2, 0, (0, 1, 2, 3))]


def q_rows(slot, chunk):
    if slot == 0:
        return 64 * (chunk % 2), chunk // 2
    return 128, chunk % 2


def lanes(shape):
    return lax.broadcasted_iota(jnp.int32, shape, len(shape) - 1)


def half(value, source, target):
    return value if source == target else pltpu.roll(value, 64, 1)


def partner(value):
    lane = lanes(value.shape) % 64
    up8, dn8 = pltpu.roll(value, 120, 1), pltpu.roll(value, 8, 1)
    up12, dn12 = pltpu.roll(value, 116, 1), pltpu.roll(value, 12, 1)
    lower = ((lane >= 16) & (lane < 28)) | ((lane >= 40) & (lane < 52))
    return jnp.where(lane < 8, up8, jnp.where(lane < 16, dn8, jnp.where(lower, up12, dn12)))


def store_queries(out_ref, base, tile, clip, pair_of_heads):
    lane = lanes((64, 128))
    for e in range(2):
        pair = 6 * clip + 2 * pair_of_heads + e
        chunk = [tile[128 * k + 64 * clip : 128 * k + 64 * clip + 64] for k in range(4)]
        for dev, slot, chunks in owners(pair):
            for lo in chunks[: len(chunks) // 2]:
                row, _ = q_rows(slot, lo)
                hi = lo + len(chunks) // 2
                value = jnp.where(lane < 64, half(chunk[lo], e, 0), half(chunk[hi], e, 1))
                out_ref[dev, base + row : base + row + 64, :] = value.astype(out_ref.dtype)


def load_queries(in_ref, base, clip, pair_of_heads):
    lane = lanes((64, 128))
    parts = []
    for e in range(2):
        pair = 6 * clip + 2 * pair_of_heads + e
        found = [None] * 4
        for dev, slot, chunks in owners(pair):
            for c in chunks:
                row, source = q_rows(slot, c)
                value = in_ref[dev, base + row : base + row + 64, :].astype(F32)
                found[c] = half(value, source, e)
        parts.append(found)
    return [jnp.where(lane < 64, a, b) for a, b in zip(*parts)]


def send_kernel(qkv_ref, rs_ref, gain_ref, cos_ref, sin_ref, send_ref, qc_ref):
    lane = lanes((64, 128))
    cosine, sine = cos_ref[...], sin_ref[...]
    rq, rk = rs_ref[:, 0:1], rs_ref[:, 1:2]
    width = 384
    for hp in range(3):
        cut = slice(128 * hp, 128 * hp + 128)
        qn = qkv_ref[:, cut] * rq * gain_ref[0:1, cut]
        kn = qkv_ref[:, width + 128 * hp : width + 128 * hp + 128] * rk * gain_ref[1:2, cut]
        vv = qkv_ref[:, 2 * width + 128 * hp : 2 * width + 128 * hp + 128]
        qc_ref[:, cut] = qn.astype(BF16)
        qr = qn * cosine + partner(qn) * sine
        kr = kn * cosine + partner(kn) * sine
        for clip in range(2):
            store_queries(send_ref, 512, qr, clip, hp)
            for e in range(2):
                for k in range(4):
                    row = 128 * k + 64 * clip
                    kc, vc = kr[row : row + 64], vv[row : row + 64]
                    value = jnp.where(lane < 64, half(kc, e, 0), half(vc, e, 1)).astype(BF16)
                    for dev, slot, _ in owners(6 * clip + 2 * hp + e):
                        at = 256 * slot + 64 * k
                        send_ref[dev, at : at + 64, :] = value


def mix_kernel(o_ref, oc_ref, gate_ref, attn_ref):
    for hp in range(3):
        cut = slice(128 * hp, 128 * hp + 128)
        gate = gate_ref[0:1, cut]
        for clip in range(2):
            for k, chunk in enumerate(load_queries(o_ref, 0, clip, hp)):
                rows = slice(128 * k + 64 * clip, 128 * k + 64 * clip + 64)
                attn_ref[rows, cut] = (chunk + gate * oc_ref[rows, cut]).astype(BF16)


def split_kernel(d_ref, gate_ref, do_ref, doc_ref):
    for hp in range(3):
        cut = slice(128 * hp, 128 * hp + 128)
        tile = d_ref[:, cut]
        doc_ref[:, cut] = (tile * gate_ref[0:1, cut]).astype(BF16)
        for clip in range(2):
            store_queries(do_ref, 0, tile, clip, hp)


def back_kernel(d_ref, dqc_ref, cos_ref, sin_ref, dqn_ref, dkn_ref, dv_ref):
    lane = lanes((64, 128))
    for hp in range(3):
        cut = slice(128 * hp, 128 * hp + 128)
        for clip in range(2):
            queries = load_queries(d_ref, 512, clip, hp)
            for k in range(4):
                rows = slice(128 * k + 64 * clip, 128 * k + 64 * clip + 64)
                cosine, sine = cos_ref[rows, :], sin_ref[rows, :]
                heads = []
                for e in range(2):
                    total = None
                    for dev, slot, _ in owners(6 * clip + 2 * hp + e):
                        at = 256 * slot + 64 * k
                        term = d_ref[dev, at : at + 64, :].astype(F32)
                        total = term if total is None else total + term
                    heads.append(total)
                dk = jnp.where(lane < 64, heads[0], half(heads[1], 0, 1))
                dv = jnp.where(lane < 64, half(heads[0], 1, 0), heads[1])
                dq = queries[k]
                dqn_ref[rows, cut] = dq * cosine + partner(dq * sine) + dqc_ref[rows, cut]
                dkn_ref[rows, cut] = dk * cosine + partner(dk * sine)
                dv_ref[rows, cut] = dv.astype(BF16)


def dot_nt(a, b):
    return lax.dot_general(a, b, (((1,), (1,)), ((), ())), preferred_element_type=F32)


def dot_nn(a, b):
    return lax.dot_general(a, b, (((1,), (0,)), ((), ())), preferred_element_type=F32)


def dot_tn(a, b):
    return lax.dot_general(a, b, (((0,), (0,)), ((), ())), preferred_element_type=F32)


def query_block(ref, slot, i, base):
    if slot == 0:
        return ref[pl.ds(i, 1), base : base + 128, :].reshape(128, 128).astype(F32)
    return ref[pl.ds(2 * i, 2), base + 128 : base + 192, :].reshape(128, 128).astype(F32)


def put_block(ref, slot, i, base, value):
    if slot == 0:
        ref[pl.ds(i, 1), base : base + 128, :] = value.reshape(1, 128, 128).astype(ref.dtype)
    else:
        ref[pl.ds(2 * i, 2), base + 128 : base + 192, :] = value.reshape(2, 64, 128).astype(ref.dtype)


def self_kernel(kv_ref, q_ref, o_ref, ot_ref, lse_ref):
    lane = lanes((128, 128))
    for slot in range(2):
        kv = kv_ref[:, 256 * slot : 256 * slot + 256, :].reshape(-1, 128)
        kvt = kv.astype(F32).T.astype(BF16)

        def step(i, carry):
            q = query_block(q_ref, slot, i, 512) * (HDIM ** (-0.5))
            qa = jnp.where(lane < 64, q, 0.0)
            qb = jnp.where(lane < 64, pltpu.roll(q, 64, 1), 0.0)
            q2 = jnp.concatenate([qa, qb], axis=0).astype(BF16)
            s = dot_nt(kv, q2)
            top = jnp.max(s, axis=0, keepdims=True)
            p = jnp.exp(s - top)
            total = jnp.sum(p, axis=0, keepdims=True)
            ot = dot_nn(kvt, p.astype(BF16)) / total
            o = ot.T
            packed = jnp.where(lane < 64, pltpu.roll(o[:128], 64, 1), o[128:])
            put_block(o_ref, slot, i, 0, packed)
            ot_ref[pl.ds(8 * slot + i, 1)] = ot[64:].reshape(1, 64, 256)
            lse_ref[pl.ds(8 * slot + i, 1)] = (top + jnp.log(total)).reshape(1, 1, 256)
            return carry

        lax.fori_loop(0, 8 if slot == 0 else 4, step, 0)


def self_back_kernel(merged, kv_ref, q_ref, do_ref, ot_ref, lse_ref, *rest):
    if merged:
        dkv_ref, acc_ref = rest
        dq_ref, base = dkv_ref, 512
    else:
        dkv_ref, dq_ref, acc_ref = rest
        base = 0
    lane = lanes((128, 128))
    for slot in range(2):
        kv = kv_ref[:, 256 * slot : 256 * slot + 256, :].reshape(-1, 128)
        kvt = kv.astype(F32).T.astype(BF16)
        acc_ref[...] = jnp.zeros_like(acc_ref)

        def step(i, carry):
            q = query_block(q_ref, slot, i, 512) * (HDIM ** (-0.5))
            d = query_block(do_ref, slot, i, 0)
            qa = jnp.where(lane < 64, q, 0.0)
            qb = jnp.where(lane < 64, pltpu.roll(q, 64, 1), 0.0)
            q2 = jnp.concatenate([qa, qb], axis=0).astype(BF16)
            da = jnp.where(lane < 64, 0.0, pltpu.roll(d, 64, 1))
            db = jnp.where(lane < 64, 0.0, d)
            d2 = jnp.concatenate([da, db], axis=0)
            delta = jnp.sum(d2.T[64:] * ot_ref[pl.ds(8 * slot + i, 1)].reshape(64, 256), axis=0, keepdims=True)
            d2 = d2.astype(BF16)
            s = dot_nt(kv, q2)
            p = jnp.exp(s - lse_ref[pl.ds(8 * slot + i, 1)].reshape(1, 256))
            dp = dot_nt(kv, d2)
            ds = (p * (dp - delta)).astype(BF16)
            acc_ref[...] += dot_nn(ds, q2) + dot_nn(p.astype(BF16), d2)
            dq = dot_nn(kvt, ds).T * (HDIM ** (-0.5))
            packed = jnp.where(lane < 64, dq[:128], pltpu.roll(dq[128:], 64, 1))
            put_block(dq_ref, slot, i, base, packed)
            return carry

        lax.fori_loop(0, 8 if slot == 0 else 4, step, 0)
        dkv_ref[:, 256 * slot : 256 * slot + 256, :] = (
            acc_ref[...].reshape(-1, 256, 128).astype(dkv_ref.dtype)
        )


def cross_probs(kc, q, bias, lane, e):
    qm = jnp.where((lane < 64) == (e == 0), q, jnp.zeros_like(q))
    s = jnp.where(bias > 0.0, dot_nt(kc, qm) * (HDIM ** (-0.5)), NEG)
    p = jnp.exp(s - jnp.max(s, axis=0, keepdims=True))
    return p / jnp.sum(p, axis=0, keepdims=True), qm


def cross_kernel(q_ref, kc_ref, vc_ref, bias_ref, o_ref):
    q = q_ref[...].reshape(256, 128)
    lane = lanes((256, 128))
    bias = bias_ref[...]
    outs = []
    for e in range(2):
        p, _ = cross_probs(kc_ref[...], q, bias, lane, e)
        outs.append(dot_tn(p.astype(BF16), vc_ref[...]))
    o_ref[...] = jnp.where(lane < 64, outs[0], outs[1]).reshape(4, 1, 64, 128)


def cross_back_kernel(q_ref, kc_ref, vc_ref, bias_ref, do_ref, dq_ref, dk_ref, dv_ref):
    q = q_ref[...].reshape(256, 128)
    d = do_ref[...].reshape(256, 128)
    lane = lanes((256, 128))
    bias = bias_ref[...]
    kc, vc = kc_ref[...], vc_ref[...]
    dqs, dk, dv = [], 0.0, 0.0
    for e in range(2):
        p, qm = cross_probs(kc, q, bias, lane, e)
        dm = jnp.where((lane < 64) == (e == 0), d, jnp.zeros_like(d))
        dp = dot_nt(vc, dm)
        dt = (p * (dp - jnp.sum(p * dp, axis=0, keepdims=True))).astype(BF16)
        dqs.append(dot_tn(dt, kc))
        dk = dk + lax.dot_general(qm, dt, (((0,), (1,)), ((), ())), preferred_element_type=F32)
        dv = dv + lax.dot_general(
            dm, p.astype(BF16), (((0,), (1,)), ((), ())), preferred_element_type=F32
        )
    dq = jnp.where(lane < 64, dqs[0], dqs[1]) * (HDIM ** (-0.5))
    dq_ref[...] = dq.reshape(4, 1, 64, 128)
    dk_ref[...] = dk * (HDIM ** (-0.5))
    dv_ref[...] = dv


def call(kernel, outs, *args, scratch=(), flops=0):
    size = sum(math.prod(a.shape) * a.dtype.itemsize for a in (*args, *outs))
    spec = pl.BlockSpec(memory_space=pltpu.VMEM)
    return pl.pallas_call(
        kernel,
        out_shape=outs,
        in_specs=[spec] * len(args),
        out_specs=[spec] * len(outs),
        scratch_shapes=list(scratch),
        compiler_params=pltpu.CompilerParams(vmem_limit_bytes=56 << 20),
        cost_estimate=pl.CostEstimate(flops=flops, bytes_accessed=size, transcendentals=flops // 256),
    )(*args)


def cross_call(kernel, outs, specs, *args):
    token = pl.BlockSpec((4, 1, 64, 128), lambda c, h: (0, c, 0, h))
    key = pl.BlockSpec((256, 128), lambda c, h: (c, h))
    bias = pl.BlockSpec((256, 1), lambda c, h: (c, 0))
    back = pl.BlockSpec((128, 256), lambda c, h: (h, c))
    kinds = {"t": token, "k": key, "b": bias, "o": back}
    return pl.pallas_call(
        kernel,
        grid=(2, 3),
        out_shape=outs,
        in_specs=[kinds[c] for c in specs[0]],
        out_specs=[kinds[c] for c in specs[1]],
        compiler_params=pltpu.CompilerParams(vmem_limit_bytes=40 << 20),
        cost_estimate=pl.CostEstimate(
            flops=12 * len(args) * 256 * 256 * 128, bytes_accessed=4 << 20, transcendentals=12 << 16
        ),
    )(*args)


def shaped(shape, dtype=F32):
    return jax.ShapeDtypeStruct(shape, dtype)


def rms_norm(tensor, gain):
    return tensor * lax.rsqrt(jnp.mean(tensor * tensor, axis=-1, keepdims=True) + EPS) * gain


def rotary_lanes():
    parts = ((0, 16), (1, 24), (2, 24))
    freqs = [[], [], []]
    signs = []
    for which, size in parts:
        for upper in range(2):
            for i in range(size // 2):
                for p in range(3):
                    freqs[p].append(math.exp(-math.log(THETA) * 2.0 * i / size) if p == which else 0.0)
                signs.append(1.0 if upper else -1.0)
    return [jnp.array(f, F32) for f in freqs], jnp.array(signs, F32)


def mm(a, b):
    return jnp.dot(a, b, preferred_element_type=F32)


def body(
    tokens,
    w_query,
    w_key,
    w_value,
    w_out,
    w_gate,
    w_up,
    w_down,
    w_cap_key,
    w_cap_value,
    w_mod,
    norm_gains,
    mix_coefs,
    caption,
    cap_len,
    cap_mask,
    timesteps,
    frame_pos,
    row_pos,
    col_pos,
    grad_out,
):
    clips, frames, rows_here, cols, width = tokens.shape
    local = frames * rows_here * cols
    group = lax.axis_size("frame")
    n_rows = lax.axis_size(ROW)
    n_far = lax.axis_size("far")
    n_all = group * n_rows
    me = lax.axis_index("frame")
    my_row = lax.axis_index(ROW)
    heads_w = width // group
    ff_w = w_gate.shape[1] // group
    count = group * clips * local
    caps = caption.shape[1]
    share = width // n_all

    def by_columns(parts):
        rows = parts[0].shape[0]
        cut = jnp.concatenate([w.reshape(rows, group, -1) for w in parts], axis=2)
        cut = lax.all_to_all(cut.transpose(1, 0, 2), "frame", 0, 0)
        full = row_gather(cut.reshape(group * rows, -1))
        full = full.reshape(n_rows, group, rows, -1).transpose(1, 0, 2, 3)
        return full.reshape(n_rows * group * rows, -1)

    w_qkv = by_columns([w_query, w_key, w_value])
    stack = jnp.concatenate([w_cap_key.T, w_cap_value.T, w_out], axis=0)
    stack = row_gather(stack).reshape(n_rows, 3, -1, width).transpose(1, 0, 2, 3)
    w_ck, w_cv, w_o = stack.reshape(3, heads_w, width)
    w_gu = by_columns([w_gate, w_up])
    w_dn = row_gather(w_down)

    half_width = width // 2
    frequencies = jnp.exp(-math.log(THETA) * jnp.arange(half_width, dtype=F32) / half_width)
    phases = timesteps.astype(F32)[:, None] * frequencies[None, :]
    step_embed = jax.nn.silu(jnp.concatenate([jnp.cos(phases), jnp.sin(phases)], axis=1)).astype(BF16)
    mod_local = mm(step_embed, w_mod).astype(BF16).astype(F32)
    mod_cols = mod_local.shape[1]
    note = jnp.concatenate([mod_local.reshape(-1), frame_pos.astype(F32).reshape(-1)])
    used = note.shape[0]
    note = jnp.pad(note, (0, -used % 512)).reshape(1, -1, 128)
    note = lax.all_to_all(jnp.broadcast_to(note, (n_all,) + note.shape[1:]), ALL, 0, 0)
    note = note.reshape(n_all, -1)
    mod_full = note[:, : clips * mod_cols].reshape(n_all, clips, mod_cols)
    mod_full = mod_full.transpose(1, 0, 2).reshape(clips, 4, width)
    scale_a, gate_a, scale_f, gate_f = (mod_full[:, i] for i in range(4))
    positions = note[:, clips * mod_cols : used].reshape(group, n_rows, clips, frames)[:, 0]
    order = jnp.arange(group)
    pick = (order[None, :] == (me ^ order)[:, None]).astype(F32)
    positions = jnp.sum(pick[:, :, None, None] * positions[None], axis=1)

    above_g, below_g = row_neighbours(grad_out)
    gains = norm_gains
    own_gains = lax.dynamic_slice(gains, (4, me * heads_w), (3, heads_w))
    own_gate = jnp.tanh(lax.dynamic_slice(mix_coefs, (0, me * heads_w), (1, heads_w)))

    full = (group, clips, frames, cols)
    pos_a = jnp.broadcast_to((positions + cap_len.astype(F32)[None, :, None])[..., None], full)
    pos_b = jnp.broadcast_to(row_pos.astype(F32)[0], full)
    pos_e = jnp.broadcast_to(col_pos.astype(F32), full)
    (fa, fb, fe), sign = rotary_lanes()
    angle = (
        pos_a.reshape(count, 1) * fa + pos_b.reshape(count, 1) * fb + pos_e.reshape(count, 1) * fe
    )
    cosine = jnp.tile(jnp.cos(angle), (1, 2))
    sine = jnp.tile(jnp.sin(angle) * sign, (1, 2))

    x_own = tokens.reshape(clips, local, width)
    x_flat = x_own.astype(F32)
    x_group = frame_gather(x_own)

    def pre_piece(x_in, gain, scale_in):
        return rms_norm(x_in, gain) * (1.0 + scale_in[:, None, :])

    h_in = pre_piece(x_group.astype(F32), gains[0], scale_a).astype(BF16).reshape(count, width)
    _, pre_back = jax.vjp(pre_piece, x_flat, gains[0], scale_a)
    qkv = mm(h_in, w_qkv)
    q_zero, k_zero = qkv[:, :heads_w], qkv[:, heads_w : 2 * heads_w]
    squares = jnp.stack([jnp.sum(q_zero * q_zero, axis=1), jnp.sum(k_zero * k_zero, axis=1)])
    rsq = lax.rsqrt(token_sum(squares) / width + EPS).T
    send, q_cap = call(
        send_kernel,
        [shaped((RING, 704, 128), BF16), shaped((count, heads_w), BF16)],
        qkv,
        rsq,
        own_gains,
        cosine,
        sine,
    )
    got = lax.all_to_all(send, "row", 0, 0)
    kv_all = got
    if n_far > 1:
        kv_all = lax.all_gather(got, "far", axis=0, tiled=True)
    keys = kv_all.shape[0] * 256
    work = 12 * keys * 256 * 128 * 2
    o_pack, o_t, lse = call(
        self_kernel,
        [shaped((RING, 192, 128), BF16), shaped((12, 64, 256)), shaped((12, 1, 256))],
        kv_all,
        got,
        flops=2 * work,
    )
    o_back = lax.all_to_all(o_pack, "row", 0, 0)

    cap2 = caption.reshape(clips * caps, width)
    usable = (jnp.arange(caps)[None, :] < cap_len[:, None]) & (cap_mask > 0)
    bias = usable.astype(F32).reshape(clips * caps, 1)
    k_pre = lax.dot_general(cap2, w_ck, (((1,), (1,)), ((), ())), preferred_element_type=F32)
    v_cap = lax.dot_general(cap2, w_cv, (((1,), (1,)), ((), ())), preferred_element_type=F32).astype(BF16)
    r_cap = lax.rsqrt(frame_sum(jnp.sum(k_pre * k_pre, axis=1)[None]) / width + EPS)
    k_cap = (k_pre * r_cap.T * own_gains[2]).astype(BF16)
    q_cap4 = q_cap.reshape(group, clips, local, heads_w)
    (out_cross,) = cross_call(
        cross_kernel, [shaped(q_cap4.shape)], ("tkkb", "t"), q_cap4, k_cap, v_cap, bias
    )
    out_cross = out_cross.reshape(count, heads_w)
    (attn_mix,) = call(mix_kernel, [shaped((count, heads_w), BF16)], o_back, out_cross, own_gate)

    y_one = frame_scatter(mm(attn_mix, w_o).reshape(group, clips, local, width))

    def mid_piece(x_in, y_in, gain_two, gate_in, gain_three, scale_in):
        h_mid = x_in + jnp.tanh(gate_in)[:, None, :] * rms_norm(y_in, gain_two)
        return (h_mid, rms_norm(h_mid, gain_three) * (1.0 + scale_in[:, None, :]))

    (h_mid, f_in32), mid_back = jax.vjp(mid_piece, x_flat, y_one, gains[1], gate_a, gains[2], scale_f)
    f_in = frame_gather(f_in32.astype(BF16)).reshape(count, width)
    gate_up = mm(f_in, w_gu)

    def act_piece(gate_in, up_in):
        return jax.nn.silu(gate_in) * up_in

    hidden32, act_back = jax.vjp(act_piece, gate_up[:, :ff_w], gate_up[:, ff_w:])
    hidden = hidden32.astype(BF16)
    z_out = frame_scatter(mm(hidden, w_dn).reshape(group, clips, local, width))

    def end_piece(h_in_mid, z_in, gain_four, gate_in):
        return h_in_mid + jnp.tanh(gate_in)[:, None, :] * rms_norm(z_in, gain_four)

    y_all, end_back = jax.vjp(end_piece, h_mid, z_out, gains[3], gate_f)
    y_grid = y_all.reshape(tokens.shape)
    above, below = (v.astype(F32) for v in row_neighbours(y_grid.astype(BF16)))
    output = (y_grid + mix_coefs[1] * above + mix_coefs[2] * below).astype(BF16)

    g_center = grad_out.astype(F32)
    d_y = g_center + mix_coefs[1] * below_g.astype(F32) + mix_coefs[2] * above_g.astype(F32)
    d_above = jnp.sum(g_center * above, axis=(0, 1, 2, 3))
    d_below = jnp.sum(g_center * below, axis=(0, 1, 2, 3))
    d_h_end, d_z, d_g_four, d_gate_f = end_back(d_y.reshape(clips, local, width))
    d_z_all = frame_gather(d_z.astype(BF16)).reshape(count, width)
    d_hidden = lax.dot_general(d_z_all, w_dn, (((1,), (1,)), ((), ())), preferred_element_type=F32)
    d_gu = jnp.concatenate([d.astype(BF16) for d in act_back(d_hidden)], axis=1)
    d_f_in = lax.dot_general(d_gu, w_gu, (((1,), (1,)), ((), ())), preferred_element_type=F32)
    d_f_in = frame_scatter(d_f_in.reshape(group, clips, local, width))

    def term(left, right):
        return lax.dot_general(left, right, (((0,), (0,)), ((), ())), preferred_element_type=F32).astype(BF16)

    def term_by_owner(left, right):
        return jnp.concatenate(
            [term(left, right[:, c * heads_w : (c + 1) * heads_w]) for c in range(group)], axis=0
        )

    sum_down = to_owner(row_scatter(term_by_owner(hidden, d_z_all)))
    sum_gu = row_scatter(term(f_in, d_gu))

    d_x_mid, d_y_one, d_g_two, d_gate_a, d_g_three, d_scale_f = mid_back((d_h_end, d_f_in))
    d_y_group = frame_gather(d_y_one.astype(BF16)).reshape(count, width)
    d_attn = lax.dot_general(d_y_group, w_o, (((1,), (1,)), ((), ())), preferred_element_type=F32)
    sum_out = to_owner(row_scatter(term_by_owner(attn_mix, d_y_group)))

    d_pack, d_cross = call(
        split_kernel, [shaped((RING, 192, 128), BF16), shaped((count, heads_w), BF16)], d_attn, own_gate
    )
    d_got = lax.all_to_all(d_pack, "row", 0, 0)
    d_mix_gate = jnp.sum(d_attn * out_cross, axis=0) * (1.0 - own_gate[0] * own_gate[0])
    d_q_cross, d_k_cap, d_v_cap = cross_call(
        cross_back_kernel,
        [shaped(q_cap4.shape), shaped((heads_w, clips * caps)), shaped((heads_w, clips * caps))],
        ("tkkbt", "too"),
        q_cap4,
        k_cap,
        v_cap,
        bias,
        d_cross.reshape(q_cap4.shape),
    )
    back_scratch = [pltpu.VMEM((keys, 128), F32)]
    if n_far == 1:
        (d_send,) = call(
            functools.partial(self_back_kernel, True),
            [shaped((RING, 704, 128), BF16)],
            kv_all,
            got,
            d_got,
            o_t,
            lse,
            scratch=back_scratch,
            flops=5 * work,
        )
    else:
        d_kv, d_q = call(
            functools.partial(self_back_kernel, False),
            [shaped((kv_all.shape[0], 512, 128), BF16), shaped((RING, 192, 128), BF16)],
            kv_all,
            got,
            d_got,
            o_t,
            lse,
            scratch=back_scratch,
            flops=5 * work,
        )
        d_kv = lax.psum_scatter(d_kv, "far", scatter_dimension=0, tiled=True)
        d_send = jnp.concatenate([d_kv, d_q], axis=1)
    d_recv = lax.all_to_all(d_send, "row", 0, 0)
    d_qn, d_kn, d_v = call(
        back_kernel,
        [shaped((count, heads_w)), shaped((count, heads_w)), shaped((count, heads_w), BF16)],
        d_recv,
        d_q_cross.reshape(count, heads_w),
        cosine,
        sine,
    )
    rq, rk = rsq[:, 0:1], rsq[:, 1:2]
    d_g_query = jnp.sum(d_qn * q_zero * rq, axis=0)
    d_g_key = jnp.sum(d_kn * k_zero * rk, axis=0)
    a_q, a_k = d_qn * own_gains[0], d_kn * own_gains[1]
    dots = token_sum(jnp.stack([jnp.sum(a_q * q_zero, axis=1), jnp.sum(a_k * k_zero, axis=1)])).T / width
    d_q_low = (rq * a_q - q_zero * (rq * rq * rq * dots[:, 0:1])).astype(BF16)
    d_k_low = (rk * a_k - k_zero * (rk * rk * rk * dots[:, 1:2])).astype(BF16)
    d_qkv = jnp.concatenate([d_q_low, d_k_low, d_v], axis=1)
    d_h_in = lax.dot_general(d_qkv, w_qkv, (((1,), (1,)), ((), ())), preferred_element_type=F32)
    d_h_in = frame_scatter(d_h_in.reshape(group, clips, local, width))
    sum_qkv = row_scatter(term(h_in, d_qkv))
    d_x_pre, d_g_zero, d_scale_a = pre_back(d_h_in)
    grad_tokens = (d_x_pre + d_x_mid).reshape(tokens.shape)

    k_pre_t = k_pre.T
    gain_cap = own_gains[2][:, None]
    cap_dot = frame_sum(jnp.sum(d_k_cap * gain_cap * k_pre_t, axis=0, keepdims=True))
    wide = heads_w // n_rows
    cap_terms = jnp.stack([d_k_cap, d_v_cap]).reshape(2, n_rows, wide, clips * caps)
    cap_terms = cap_terms.transpose(1, 0, 2, 3).reshape(n_rows, 2 * wide, clips * caps)
    extra = jnp.broadcast_to(jnp.pad(cap_dot, ((0, 7), (0, 0)))[None], (n_rows, 8, clips * caps))
    cap_terms = jnp.concatenate([cap_terms, extra], axis=1).reshape(n_rows * (2 * wide + 8), -1)
    cap_sum = row_scatter(cap_terms)
    d_k_own, d_v_own, cap_dot = cap_sum[:wide], cap_sum[wide : 2 * wide], cap_sum[2 * wide : 2 * wide + 1]
    k_own = lax.dynamic_slice(k_pre_t, (my_row * wide, 0), (wide, clips * caps))
    g_own = lax.dynamic_slice(own_gains, (2, my_row * wide), (1, wide)).T
    d_g_cap = jnp.sum(d_k_own * k_own * r_cap, axis=1)
    d_k_zero_cap = (r_cap * g_own * d_k_own - k_own * (r_cap * r_cap * r_cap * cap_dot / width)).astype(BF16)

    def cap_weight(d):
        return lax.dot_general(cap2, d, (((0,), (1,)), ((), ())), preferred_element_type=F32)

    d_w_cap_key = cap_weight(d_k_zero_cap)
    d_w_cap_value = cap_weight(d_v_own.astype(BF16))

    def spread(block):
        return lax.dynamic_update_slice(jnp.zeros((width,), F32), block, (me * heads_w,))

    d_mod = jnp.concatenate([d_scale_a, d_gate_a, d_scale_f, d_gate_f], axis=1)
    d_mod = d_mod.reshape(clips, n_all, mod_cols).transpose(1, 0, 2).reshape(n_all, -1)
    rest = jnp.stack(
        [
            d_g_zero,
            d_g_two,
            d_g_three,
            d_g_four,
            spread(d_g_query),
            spread(d_g_key),
            spread(d_mix_gate),
            d_above,
            d_below,
        ]
    )
    rest = rest.reshape(9, n_all, share).transpose(1, 0, 2).reshape(n_all, -1)
    small = jnp.concatenate([d_mod, rest], axis=1)
    small = jnp.pad(small, ((0, 0), (0, -small.shape[1] % 128))).reshape(n_all, -1, 128)
    small = jnp.sum(lax.all_to_all(small, ALL, 0, 0), axis=0).reshape(-1)
    d_mod = small[: clips * mod_cols].reshape(clips, mod_cols)
    rest = small[clips * mod_cols : clips * mod_cols + 9 * share].reshape(9, share)
    d_w_mod = lax.dot_general(
        step_embed, d_mod.astype(BF16), (((0,), (0,)), ((), ())), preferred_element_type=F32
    )
    d_gains = jnp.concatenate([rest[:6], d_g_cap[None]], axis=0)
    d_mixes = rest[6:]

    sum_qkv = sum_qkv.astype(F32)
    sum_gu = sum_gu.astype(F32)
    return (
        output,
        grad_tokens,
        sum_qkv[:, :heads_w],
        sum_qkv[:, heads_w : 2 * heads_w],
        sum_qkv[:, 2 * heads_w :],
        sum_out.astype(F32),
        sum_gu[:, :ff_w],
        sum_gu[:, ff_w:],
        sum_down.astype(F32),
        d_w_cap_key,
        d_w_cap_value,
        d_w_mod,
        d_gains,
        d_mixes,
    )


def solution(mesh):
    frame, row = mesh.shape["frame"], mesh.shape["row"]
    fine = Mesh(mesh.devices.reshape(frame, row // RING, RING), ("frame", "far", "row"))
    grid = P(None, "frame", ROW, None, None)
    rows, columns = P(ALL, None), P(None, ALL)
    tile = P(ROW, "frame")
    return jax.shard_map(
        body,
        mesh=fine,
        in_specs=(
            (grid,)
            + (rows,) * 7
            + (columns,) * 3
            + (P(),) * 6
            + (P(None, "frame"), P(ROW), P(), grid)
        ),
        out_specs=(grid, grid) + (tile,) * 7 + (columns,) * 5,
        check_vma=False,
    )
```

```python
import functools
import math

import jax
import jax.numpy as jnp
from jax import lax
from jax.experimental import pallas as pl
from jax.experimental.pallas import tpu as pltpu
from jax.sharding import Mesh
from jax.sharding import PartitionSpec as P

HDIM = 64
EPS = 1e-05
THETA = 10000.0
NEG = -1000000000.0
F32 = jnp.float32
BF16 = jnp.bfloat16
RING = 8
ROW = ("far", "row")
ALL = ("frame", "far", "row")


def swap(value, bits):
    return lax.ppermute(value, "frame", [(i, i ^ bits) for i in range(lax.axis_size("frame"))])


def frame_sum(value):
    value = value + swap(value, 1)
    return value + swap(value, 2)


def token_sum(value):
    blocks = value.reshape(value.shape[0], 4, -1)
    got = swap(blocks, 1).reshape(value.shape[0], 2, 2, -1)
    blocks = blocks + got[:, :, ::-1].reshape(blocks.shape)
    got = swap(blocks, 2)
    blocks = blocks + jnp.concatenate([got[:, 2:], got[:, :2]], axis=1)
    return blocks.reshape(value.shape)


def beside(moved, work):
    return (moved, None) if work is None else lax.optimization_barrier((moved, work))


def frame_gather(value, work=None):
    over, work = beside(swap(value, 2), work)
    pair = swap(jnp.stack([value, over]), 1)
    return jnp.stack([value, pair[0], over, pair[1]]), work


def frame_scatter(terms, work=None):
    low = terms.astype(BF16)
    got = swap(jnp.stack([low[1], low[3]]), 1).astype(F32)
    far = (terms[2] + got[1]).astype(BF16)
    far, work = beside(swap(far, 2), work)
    return terms[0] + got[0] + far.astype(F32), work


def row_neighbours(block):
    count = lax.axis_size(ROW)
    forward = [(i, i + 1) for i in range(count - 1)]
    above = lax.ppermute(block, ROW, forward)
    below = lax.ppermute(block, ROW, [(b, a) for a, b in forward])
    return above, below


def row_gather(block):
    return lax.all_gather(block, ROW, axis=0, tiled=True)


def row_scatter(terms):
    return lax.psum_scatter(terms, ROW, scatter_dimension=0, tiled=True)


def pick(blocks, index):
    return lax.dynamic_index_in_dim(blocks, index, 0, keepdims=False)


def line_scatter(terms):
    if lax.axis_size("far") > 1:
        return row_scatter(terms.reshape(-1, terms.shape[-1])).astype(F32)
    place = lax.axis_index("row")
    z, x = place // 2, place % 2
    last = RING // 2 - 1
    blocks = terms.reshape(last + 1, 2, -1, terms.shape[-1])
    mine = lax.dynamic_index_in_dim(blocks, x, 1, keepdims=False)
    other = lax.dynamic_index_in_dim(blocks, 1 - x, 1, keepdims=False)
    got = lax.ppermute(other, "row", [(i, i ^ 1) for i in range(RING)])
    both = (mine.astype(F32) + got.astype(F32)).astype(BF16)
    up = down = None
    for k in range(last, 0, -1):
        send_up = pick(both, jnp.minimum(z + k, last))
        send_down = pick(both, jnp.maximum(z - k, 0))
        if up is not None:
            send_up = (send_up.astype(F32) + up.astype(F32)).astype(BF16)
            send_down = (send_down.astype(F32) + down.astype(F32)).astype(BF16)
        up = lax.ppermute(send_up, "row", [(i, i + 2) for i in range(RING) if i // 2 + k <= last])
        down = lax.ppermute(send_down, "row", [(i, i - 2) for i in range(RING) if i // 2 - k >= 0])
    return pick(both, z).astype(F32) + up.astype(F32) + down.astype(F32)


def line_gather(block):
    if lax.axis_size("far") > 1:
        return row_gather(block)
    place = lax.axis_index("row")
    z, x = place // 2, place % 2
    last = RING // 2 - 1
    other = lax.ppermute(block, "row", [(i, i ^ 1) for i in range(RING)])
    pair = jnp.where(x == 0, jnp.stack([block, other]), jnp.stack([other, block]))
    below, above = [pair], [pair]
    for k in range(1, last + 1):
        below.append(lax.ppermute(below[-1], "row", [(i, i + 2) for i in range(RING - 2) if i // 2 >= k - 1]))
        above.append(lax.ppermute(above[-1], "row", [(i, i - 2) for i in range(2, RING) if i // 2 + k - 1 <= last]))
    line = jnp.stack(below[:0:-1] + above)
    line = lax.dynamic_slice_in_dim(line, last - z, last + 1, 0)
    return line.reshape(-1, block.shape[1])


def to_chunks(value, size):
    blocks, rows, columns = value.shape
    value = value.reshape(blocks, rows, columns // size, size).transpose(0, 2, 1, 3)
    return value.reshape(blocks, -1, size)


def from_chunks(value, rows):
    blocks, _, size = value.shape
    return value.reshape(blocks, -1, rows, size).transpose(0, 2, 1, 3).reshape(blocks * rows, -1)


def to_owner(block):
    frames, rows = lax.axis_size("frame"), lax.axis_size(ROW)
    part = rows // frames
    pairs = []
    for f in range(frames):
        for c in range(frames):
            for h in range(part):
                pairs.append((f * rows + c * part + h, c * rows + f * part + h))
    return lax.ppermute(block, ALL, pairs)


def owners(pair):
    j, k = divmod(pair, 3)
    if k == 1:
        return [(2 * j, 1, (0, 1)), (2 * j + 1, 1, (2, 3))]
    return [(2 * j + k // 2, 0, (0, 1, 2, 3))]


def q_rows(slot, chunk):
    if slot == 0:
        return 64 * (chunk % 2), chunk // 2
    return 128, chunk % 2


def lanes(shape):
    return lax.broadcasted_iota(jnp.int32, shape, len(shape) - 1)


def half(value, source, target):
    return value if source == target else pltpu.roll(value, 64, 1)


def partner(value):
    lane = lanes(value.shape) % 64
    up8, dn8 = pltpu.roll(value, 120, 1), pltpu.roll(value, 8, 1)
    up12, dn12 = pltpu.roll(value, 116, 1), pltpu.roll(value, 12, 1)
    lower = ((lane >= 16) & (lane < 28)) | ((lane >= 40) & (lane < 52))
    return jnp.where(lane < 8, up8, jnp.where(lane < 16, dn8, jnp.where(lower, up12, dn12)))


def store_queries(out_ref, base, tile, clip, pair_of_heads):
    lane = lanes((64, 128))
    for e in range(2):
        pair = 6 * clip + 2 * pair_of_heads + e
        chunk = [tile[128 * k + 64 * clip : 128 * k + 64 * clip + 64] for k in range(4)]
        for dev, slot, chunks in owners(pair):
            for lo in chunks[: len(chunks) // 2]:
                row, _ = q_rows(slot, lo)
                hi = lo + len(chunks) // 2
                value = jnp.where(lane < 64, half(chunk[lo], e, 0), half(chunk[hi], e, 1))
                out_ref[dev, base + row : base + row + 64, :] = value.astype(out_ref.dtype)


def load_queries(in_ref, base, clip, pair_of_heads):
    lane = lanes((64, 128))
    parts = []
    for e in range(2):
        pair = 6 * clip + 2 * pair_of_heads + e
        found = [None] * 4
        for dev, slot, chunks in owners(pair):
            for c in chunks:
                row, source = q_rows(slot, c)
                value = in_ref[dev, base + row : base + row + 64, :].astype(F32)
                found[c] = half(value, source, e)
        parts.append(found)
    return [jnp.where(lane < 64, a, b) for a, b in zip(*parts)]


def send_kernel(qkv_ref, rs_ref, gain_ref, cos_ref, sin_ref, send_ref, qc_ref):
    lane = lanes((64, 128))
    cosine, sine = cos_ref[...], sin_ref[...]
    rq, rk = rs_ref[:, 0:1], rs_ref[:, 1:2]
    width = 384
    for hp in range(3):
        cut = slice(128 * hp, 128 * hp + 128)
        qn = qkv_ref[:, cut] * rq * gain_ref[0:1, cut]
        kn = qkv_ref[:, width + 128 * hp : width + 128 * hp + 128] * rk * gain_ref[1:2, cut]
        vv = qkv_ref[:, 2 * width + 128 * hp : 2 * width + 128 * hp + 128]
        qc_ref[:, cut] = qn.astype(BF16)
        qr = qn * cosine + partner(qn) * sine
        kr = kn * cosine + partner(kn) * sine
        for clip in range(2):
            store_queries(send_ref, 512, qr, clip, hp)
            for e in range(2):
                for k in range(4):
                    row = 128 * k + 64 * clip
                    kc, vc = kr[row : row + 64], vv[row : row + 64]
                    value = jnp.where(lane < 64, half(kc, e, 0), half(vc, e, 1)).astype(BF16)
                    for dev, slot, _ in owners(6 * clip + 2 * hp + e):
                        at = 256 * slot + 64 * k
                        send_ref[dev, at : at + 64, :] = value


def mix_kernel(o_ref, oc_ref, gate_ref, attn_ref):
    for hp in range(3):
        cut = slice(128 * hp, 128 * hp + 128)
        gate = gate_ref[0:1, cut]
        for clip in range(2):
            for k, chunk in enumerate(load_queries(o_ref, 0, clip, hp)):
                rows = slice(128 * k + 64 * clip, 128 * k + 64 * clip + 64)
                attn_ref[rows, cut] = (chunk + gate * oc_ref[rows, cut]).astype(BF16)


def split_kernel(d_ref, gate_ref, do_ref, doc_ref):
    for hp in range(3):
        cut = slice(128 * hp, 128 * hp + 128)
        tile = d_ref[:, cut]
        doc_ref[:, cut] = (tile * gate_ref[0:1, cut]).astype(BF16)
        for clip in range(2):
            store_queries(do_ref, 0, tile, clip, hp)


def back_kernel(d_ref, dqc_ref, cos_ref, sin_ref, dqn_ref, dkn_ref, dv_ref):
    lane = lanes((64, 128))
    for hp in range(3):
        cut = slice(128 * hp, 128 * hp + 128)
        for clip in range(2):
            queries = load_queries(d_ref, 512, clip, hp)
            for k in range(4):
                rows = slice(128 * k + 64 * clip, 128 * k + 64 * clip + 64)
                cosine, sine = cos_ref[rows, :], sin_ref[rows, :]
                heads = []
                for e in range(2):
                    total = None
                    for dev, slot, _ in owners(6 * clip + 2 * hp + e):
                        at = 256 * slot + 64 * k
                        term = d_ref[dev, at : at + 64, :].astype(F32)
                        total = term if total is None else total + term
                    heads.append(total)
                dk = jnp.where(lane < 64, heads[0], half(heads[1], 0, 1))
                dv = jnp.where(lane < 64, half(heads[0], 1, 0), heads[1])
                dq = queries[k]
                dqn_ref[rows, cut] = dq * cosine + partner(dq * sine) + dqc_ref[rows, cut]
                dkn_ref[rows, cut] = dk * cosine + partner(dk * sine)
                dv_ref[rows, cut] = dv.astype(BF16)


def dot_nt(a, b):
    return lax.dot_general(a, b, (((1,), (1,)), ((), ())), preferred_element_type=F32)


def dot_nn(a, b):
    return lax.dot_general(a, b, (((1,), (0,)), ((), ())), preferred_element_type=F32)


def turned(value):
    return value.astype(F32).T.astype(BF16)


def ff_kernel(hidden_ref, dz_ref, f_in_ref, dgu_ref, out_ref):
    n_rows = out_ref.shape[0]
    part = n_rows // 4
    left = turned(hidden_ref[...])
    tile = left.shape[0] // part
    for c in range(4):
        for j in range(3):
            cut = 384 * c + 128 * j
            block = dot_nn(left, dz_ref[:, cut : cut + 128]).astype(BF16)
            for h in range(part):
                out_ref[c * part + h, tile * j : tile * j + tile, :] = block[tile * h : tile * h + tile]
    base = 3 * tile
    left = turned(f_in_ref[...])
    tile = left.shape[0] // n_rows
    for j in range(0, dgu_ref.shape[1] // 128, 2):
        block = dot_nn(left, dgu_ref[:, 128 * j : 128 * j + 256]).astype(BF16)
        for r in range(n_rows):
            for e in range(2):
                at = base + tile * (j + e)
                out_ref[r, at : at + tile, :] = block[tile * r : tile * r + tile, 128 * e : 128 * e + 128]


def out_kernel(attn_ref, dy_ref, dk_ref, dv_ref, dot_ref, out_ref):
    n_rows = out_ref.shape[0]
    part = n_rows // 4
    wide = dk_ref.shape[0] // n_rows
    tall = 2 * wide + 16
    chunks = dk_ref.shape[1] // 128
    for r in range(n_rows):
        for j in range(chunks):
            cut = slice(128 * j, 128 * j + 128)
            block = jnp.concatenate(
                [
                    dk_ref[wide * r : wide * r + wide, cut],
                    dv_ref[wide * r : wide * r + wide, cut],
                    jnp.broadcast_to(dot_ref[:, cut], (16, 128)),
                ]
            )
            out_ref[r, tall * j : tall * j + tall, :] = block.astype(BF16)
    base = tall * chunks
    left = turned(attn_ref[...])
    tile = left.shape[0] // part
    for c in range(4):
        for j in range(3):
            cut = 384 * c + 128 * j
            block = dot_nn(left, dy_ref[:, cut : cut + 128]).astype(BF16)
            for h in range(part):
                at = base + tile * j
                out_ref[c * part + h, at : at + tile, :] = block[tile * h : tile * h + tile]


def dot_tt(a, b):
    return lax.dot_general(a, b, (((0,), (1,)), ((), ())), preferred_element_type=F32)


def query_block(ref, slot, i, base):
    if slot == 0:
        return ref[pl.ds(i, 1), base : base + 128, :].reshape(128, 128).astype(F32)
    return ref[pl.ds(2 * i, 2), base + 128 : base + 192, :].reshape(128, 128).astype(F32)


def put_block(ref, slot, i, base, value):
    if slot == 0:
        ref[pl.ds(i, 1), base : base + 128, :] = value.reshape(1, 128, 128).astype(ref.dtype)
    else:
        ref[pl.ds(2 * i, 2), base + 128 : base + 192, :] = value.reshape(2, 64, 128).astype(ref.dtype)


def self_kernel(kv_ref, q_ref, o_ref, ot_ref, lse_ref):
    lane = lanes((128, 128))
    for slot in range(2):
        kv = kv_ref[:, 256 * slot : 256 * slot + 256, :].reshape(-1, 128)
        kvt = kv.astype(F32).T.astype(BF16)

        def step(i, carry):
            q = query_block(q_ref, slot, i, 512) * (HDIM ** (-0.5))
            qa = jnp.where(lane < 64, q, 0.0)
            qb = jnp.where(lane < 64, pltpu.roll(q, 64, 1), 0.0)
            q2 = jnp.concatenate([qa, qb], axis=0).astype(BF16)
            s = dot_nt(kv, q2)
            top = jnp.max(s, axis=0, keepdims=True)
            p = jnp.exp(s - top)
            total = jnp.sum(p, axis=0, keepdims=True)
            ot = dot_nn(kvt, p.astype(BF16)) / total
            o = ot.T
            packed = jnp.where(lane < 64, pltpu.roll(o[:128], 64, 1), o[128:])
            put_block(o_ref, slot, i, 0, packed)
            ot_ref[pl.ds(8 * slot + i, 1)] = ot[64:].reshape(1, 64, 256)
            lse_ref[pl.ds(8 * slot + i, 1)] = (top + jnp.log(total)).reshape(1, 1, 256)
            return carry

        lax.fori_loop(0, 8 if slot == 0 else 4, step, 0)


def self_back_kernel(merged, kv_ref, q_ref, do_ref, ot_ref, lse_ref, *rest):
    if merged:
        dkv_ref, acc_ref = rest
        dq_ref, base = dkv_ref, 512
    else:
        dkv_ref, dq_ref, acc_ref = rest
        base = 0
    lane = lanes((128, 128))
    for slot in range(2):
        kv = kv_ref[:, 256 * slot : 256 * slot + 256, :].reshape(-1, 128)
        kvt = kv.astype(F32).T.astype(BF16)
        acc_ref[...] = jnp.zeros_like(acc_ref)

        def step(i, carry):
            q = query_block(q_ref, slot, i, 512) * (HDIM ** (-0.5))
            d = query_block(do_ref, slot, i, 0)
            qa = jnp.where(lane < 64, q, 0.0)
            qb = jnp.where(lane < 64, pltpu.roll(q, 64, 1), 0.0)
            q2 = jnp.concatenate([qa, qb], axis=0).astype(BF16)
            da = jnp.where(lane < 64, 0.0, pltpu.roll(d, 64, 1))
            db = jnp.where(lane < 64, 0.0, d)
            d2 = jnp.concatenate([da, db], axis=0)
            delta = jnp.sum(d2.T[64:] * ot_ref[pl.ds(8 * slot + i, 1)].reshape(64, 256), axis=0, keepdims=True)
            d2 = d2.astype(BF16)
            s = dot_nt(kv, q2)
            p = jnp.exp(s - lse_ref[pl.ds(8 * slot + i, 1)].reshape(1, 256))
            dp = dot_nt(kv, d2)
            ds = (p * (dp - delta)).astype(BF16)
            acc_ref[...] += dot_nn(ds, q2) + dot_nn(p.astype(BF16), d2)
            dq = dot_nn(kvt, ds).T * (HDIM ** (-0.5))
            packed = jnp.where(lane < 64, dq[:128], pltpu.roll(dq[128:], 64, 1))
            put_block(dq_ref, slot, i, base, packed)
            return carry

        lax.fori_loop(0, 8 if slot == 0 else 4, step, 0)
        dkv_ref[:, 256 * slot : 256 * slot + 256, :] = (
            acc_ref[...].reshape(-1, 256, 128).astype(dkv_ref.dtype)
        )


def cross_probs(kc, q, bias, lane, e):
    qm = jnp.where((lane < 64) == (e == 0), q, jnp.zeros_like(q))
    s = jnp.where(bias > 0.0, dot_tt(kc, qm) * (HDIM ** (-0.5)), NEG)
    p = jnp.exp(s - jnp.max(s, axis=0, keepdims=True))
    return p / jnp.sum(p, axis=0, keepdims=True), qm


def cross_kernel(q_ref, kc_ref, vc_ref, bias_ref, o_ref):
    q = q_ref[...].reshape(256, 128)
    lane = lanes((256, 128))
    bias = bias_ref[...]
    outs = []
    for e in range(2):
        p, _ = cross_probs(kc_ref[...], q, bias, lane, e)
        outs.append(dot_tt(p.astype(BF16), vc_ref[...]))
    o_ref[...] = jnp.where(lane < 64, outs[0], outs[1]).reshape(4, 1, 64, 128)


def cross_back_kernel(q_ref, kc_ref, vc_ref, bias_ref, do_ref, dq_ref, dk_ref, dv_ref):
    q = q_ref[...].reshape(256, 128)
    d = do_ref[...].reshape(256, 128)
    lane = lanes((256, 128))
    bias = bias_ref[...]
    kc, vc = kc_ref[...], vc_ref[...]
    dqs, dk, dv = [], 0.0, 0.0
    for e in range(2):
        p, qm = cross_probs(kc, q, bias, lane, e)
        dm = jnp.where((lane < 64) == (e == 0), d, jnp.zeros_like(d))
        dp = dot_tt(vc, dm)
        dt = (p * (dp - jnp.sum(p * dp, axis=0, keepdims=True))).astype(BF16)
        dqs.append(dot_tt(dt, kc))
        dk = dk + dot_tt(qm, dt)
        dv = dv + dot_tt(dm, p.astype(BF16))
    dq = jnp.where(lane < 64, dqs[0], dqs[1]) * (HDIM ** (-0.5))
    dq_ref[...] = dq.reshape(4, 1, 64, 128)
    dk_ref[...] = dk * (HDIM ** (-0.5))
    dv_ref[...] = dv


def call(kernel, outs, *args, scratch=(), flops=0):
    size = sum(math.prod(a.shape) * a.dtype.itemsize for a in (*args, *outs))
    spec = pl.BlockSpec(memory_space=pltpu.VMEM)
    return pl.pallas_call(
        kernel,
        out_shape=outs,
        in_specs=[spec] * len(args),
        out_specs=[spec] * len(outs),
        scratch_shapes=list(scratch),
        compiler_params=pltpu.CompilerParams(vmem_limit_bytes=56 << 20),
        cost_estimate=pl.CostEstimate(flops=flops, bytes_accessed=size, transcendentals=flops // 256),
    )(*args)


def cross_call(kernel, outs, specs, *args):
    token = pl.BlockSpec((4, 1, 64, 128), lambda c, h: (0, c, 0, h))
    bias = pl.BlockSpec((256, 1), lambda c, h: (c, 0))
    back = pl.BlockSpec((128, 256), lambda c, h: (h, c))
    kinds = {"t": token, "b": bias, "o": back}
    return pl.pallas_call(
        kernel,
        grid=(2, 3),
        out_shape=outs,
        in_specs=[kinds[c] for c in specs[0]],
        out_specs=[kinds[c] for c in specs[1]],
        compiler_params=pltpu.CompilerParams(vmem_limit_bytes=40 << 20),
        cost_estimate=pl.CostEstimate(
            flops=12 * len(args) * 256 * 256 * 128, bytes_accessed=4 << 20, transcendentals=12 << 16
        ),
    )(*args)


def shaped(shape, dtype=F32):
    return jax.ShapeDtypeStruct(shape, dtype)


def rms_norm(tensor, gain):
    return tensor * lax.rsqrt(jnp.mean(tensor * tensor, axis=-1, keepdims=True) + EPS) * gain


def rotary_lanes():
    parts = ((0, 16), (1, 24), (2, 24))
    freqs = [[], [], []]
    signs = []
    for which, size in parts:
        for upper in range(2):
            for i in range(size // 2):
                for p in range(3):
                    freqs[p].append(math.exp(-math.log(THETA) * 2.0 * i / size) if p == which else 0.0)
                signs.append(1.0 if upper else -1.0)
    return [jnp.array(f, F32) for f in freqs], jnp.array(signs, F32)


def mm(a, b):
    return jnp.dot(a, b, preferred_element_type=F32)


def body(
    tokens,
    w_query,
    w_key,
    w_value,
    w_out,
    w_gate,
    w_up,
    w_down,
    w_cap_key,
    w_cap_value,
    w_mod,
    norm_gains,
    mix_coefs,
    caption,
    cap_len,
    cap_mask,
    timesteps,
    frame_pos,
    row_pos,
    col_pos,
    grad_out,
):
    clips, frames, rows_here, cols, width = tokens.shape
    local = frames * rows_here * cols
    group = lax.axis_size("frame")
    n_rows = lax.axis_size(ROW)
    n_far = lax.axis_size("far")
    n_all = group * n_rows
    me = lax.axis_index("frame")
    my_row = lax.axis_index(ROW)
    heads_w = width // group
    ff_w = w_gate.shape[1] // group
    count = group * clips * local
    caps = caption.shape[1]
    share = width // n_all

    rows = w_query.shape[0]
    cap2 = caption.reshape(clips * caps, width)

    def by_columns(parts):
        cut = jnp.concatenate([w.reshape(rows, group, -1) for w in parts], axis=2)
        cut = lax.all_to_all(cut.transpose(1, 0, 2), "frame", 0, 0)
        full = row_gather(cut.reshape(group * rows, -1))
        full = full.reshape(n_rows, group, rows, -1).transpose(1, 0, 2, 3)
        return full.reshape(n_rows * group * rows, -1)

    def cap_columns(weight):
        return lax.dot_general(weight, cap2, (((0,), (1,)), ((), ())), preferred_element_type=F32).astype(BF16)

    w_dn = line_gather(w_down)
    w_qkv = by_columns([w_query, w_key, w_value])
    side = row_gather(jnp.concatenate([cap_columns(w_cap_key), cap_columns(w_cap_value), w_out], axis=1))
    tokens_c = clips * caps
    k_pre_t, v_cap_t, w_o = side[:, :tokens_c], side[:, tokens_c : 2 * tokens_c], side[:, 2 * tokens_c :]
    w_gu = by_columns([w_gate, w_up])

    half_width = width // 2
    frequencies = jnp.exp(-math.log(THETA) * jnp.arange(half_width, dtype=F32) / half_width)
    phases = timesteps.astype(F32)[:, None] * frequencies[None, :]
    step_embed = jax.nn.silu(jnp.concatenate([jnp.cos(phases), jnp.sin(phases)], axis=1)).astype(BF16)
    mod_local = mm(step_embed, w_mod).astype(BF16).astype(F32)
    mod_cols = mod_local.shape[1]
    note = jnp.concatenate([mod_local.reshape(-1), frame_pos.astype(F32).reshape(-1)])
    used = note.shape[0]
    note = jnp.pad(note, (0, -used % 512)).reshape(1, -1, 128)
    note = lax.all_to_all(jnp.broadcast_to(note, (n_all,) + note.shape[1:]), ALL, 0, 0)
    note = note.reshape(n_all, -1)
    mod_full = note[:, : clips * mod_cols].reshape(n_all, clips, mod_cols)
    mod_full = mod_full.transpose(1, 0, 2).reshape(clips, 4, width)
    scale_a, gate_a, scale_f, gate_f = (mod_full[:, i] for i in range(4))
    positions = note[:, clips * mod_cols : used].reshape(group, n_rows, clips, frames)[:, 0]
    order = jnp.arange(group)
    pick = (order[None, :] == (me ^ order)[:, None]).astype(F32)
    positions = jnp.sum(pick[:, :, None, None] * positions[None], axis=1)

    above_g, below_g = row_neighbours(grad_out)
    gains = norm_gains
    own_gains = lax.dynamic_slice(gains, (4, me * heads_w), (3, heads_w))
    own_gate = jnp.tanh(lax.dynamic_slice(mix_coefs, (0, me * heads_w), (1, heads_w)))

    full = (group, clips, frames, cols)
    pos_a = jnp.broadcast_to((positions + cap_len.astype(F32)[None, :, None])[..., None], full)
    pos_b = jnp.broadcast_to(row_pos.astype(F32)[0], full)
    pos_e = jnp.broadcast_to(col_pos.astype(F32), full)
    (fa, fb, fe), sign = rotary_lanes()
    angle = (
        pos_a.reshape(count, 1) * fa + pos_b.reshape(count, 1) * fb + pos_e.reshape(count, 1) * fe
    )
    cosine = jnp.tile(jnp.cos(angle), (1, 2))
    sine = jnp.tile(jnp.sin(angle) * sign, (1, 2))

    x_own = tokens.reshape(clips, local, width)
    x_flat = x_own.astype(F32)
    x_group, _ = frame_gather(x_own)

    def pre_piece(x_in, gain, scale_in):
        return rms_norm(x_in, gain) * (1.0 + scale_in[:, None, :])

    h_in = pre_piece(x_group.astype(F32), gains[0], scale_a).astype(BF16).reshape(count, width)
    h_in = lax.optimization_barrier(h_in)
    _, pre_back = jax.vjp(pre_piece, x_flat, gains[0], scale_a)
    qkv = mm(h_in, w_qkv)
    q_zero, k_zero = qkv[:, :heads_w], qkv[:, heads_w : 2 * heads_w]
    squares = jnp.stack([jnp.sum(q_zero * q_zero, axis=1), jnp.sum(k_zero * k_zero, axis=1)])
    rsq = lax.rsqrt(token_sum(squares) / width + EPS).T
    send, q_cap = call(
        send_kernel,
        [shaped((RING, 704, 128), BF16), shaped((count, heads_w), BF16)],
        qkv,
        rsq,
        own_gains,
        cosine,
        sine,
    )
    got = lax.all_to_all(send, "row", 0, 0)
    kv_all = got
    if n_far > 1:
        kv_all = lax.all_gather(got, "far", axis=0, tiled=True)
    keys = kv_all.shape[0] * 256
    work = 12 * keys * 256 * 128 * 2
    o_pack, o_t, lse = call(
        self_kernel,
        [shaped((RING, 192, 128), BF16), shaped((12, 64, 256)), shaped((12, 1, 256))],
        kv_all,
        got,
        flops=2 * work,
    )
    o_back = lax.all_to_all(o_pack, "row", 0, 0)

    usable = (jnp.arange(caps)[None, :] < cap_len[:, None]) & (cap_mask > 0)
    bias = usable.astype(F32).reshape(clips * caps, 1)
    k_pre_t = k_pre_t.astype(F32)
    gain_cap = own_gains[2][:, None]
    r_cap = lax.rsqrt(frame_sum(jnp.sum(k_pre_t * k_pre_t, axis=0, keepdims=True)) / width + EPS)
    k_cap_t = (k_pre_t * r_cap * gain_cap).astype(BF16)
    q_cap4 = q_cap.reshape(group, clips, local, heads_w)
    (out_cross,) = cross_call(
        cross_kernel, [shaped(q_cap4.shape)], ("toob", "t"), q_cap4, k_cap_t, v_cap_t, bias
    )
    o_back, out_cross = beside(o_back, out_cross)
    out_cross = out_cross.reshape(count, heads_w)
    (attn_mix,) = call(mix_kernel, [shaped((count, heads_w), BF16)], o_back, out_cross, own_gate)

    y_one, _ = frame_scatter(mm(attn_mix, w_o).reshape(group, clips, local, width))

    def mid_piece(x_in, y_in, gain_two, gate_in, gain_three, scale_in):
        h_mid = x_in + jnp.tanh(gate_in)[:, None, :] * rms_norm(y_in, gain_two)
        return (h_mid, rms_norm(h_mid, gain_three) * (1.0 + scale_in[:, None, :]))

    (h_mid, f_in32), mid_back = jax.vjp(mid_piece, x_flat, y_one, gains[1], gate_a, gains[2], scale_f)
    f_in, _ = frame_gather(f_in32.astype(BF16))
    f_in = f_in.reshape(count, width)
    gate_up = mm(f_in, w_gu)

    def act_piece(gate_in, up_in):
        return jax.nn.silu(gate_in) * up_in

    hidden32, act_back = jax.vjp(act_piece, gate_up[:, :ff_w], gate_up[:, ff_w:])
    hidden = hidden32.astype(BF16)
    z_out, _ = frame_scatter(mm(hidden, w_dn).reshape(group, clips, local, width))

    def end_piece(h_in_mid, z_in, gain_four, gate_in):
        return h_in_mid + jnp.tanh(gate_in)[:, None, :] * rms_norm(z_in, gain_four)

    y_all, end_back = jax.vjp(end_piece, h_mid, z_out, gains[3], gate_f)
    y_grid = y_all.reshape(tokens.shape)
    above, below = (v.astype(F32) for v in row_neighbours(y_grid.astype(BF16)))
    output = (y_grid + mix_coefs[1] * above + mix_coefs[2] * below).astype(BF16)

    g_center = grad_out.astype(F32)
    d_y = g_center + mix_coefs[1] * below_g.astype(F32) + mix_coefs[2] * above_g.astype(F32)
    d_above = jnp.sum(g_center * above, axis=(0, 1, 2, 3))
    d_below = jnp.sum(g_center * below, axis=(0, 1, 2, 3))
    d_h_end, d_z, d_g_four, d_gate_f = end_back(d_y.reshape(clips, local, width))
    d_z_all, _ = frame_gather(d_z.astype(BF16))
    d_z_all = d_z_all.reshape(count, width)
    d_hidden = lax.dot_general(d_z_all, w_dn, (((1,), (1,)), ((), ())), preferred_element_type=F32)
    d_gu = jnp.concatenate([d.astype(BF16) for d in act_back(d_hidden)], axis=1)
    d_f_in = lax.dot_general(d_gu, w_gu, (((1,), (1,)), ((), ())), preferred_element_type=F32)
    def term(left, right):
        return lax.dot_general(left, right, (((0,), (0,)), ((), ())), preferred_element_type=F32).astype(BF16)

    ff_rows = (w_down.shape[0] * group * (heads_w // 128), width // n_rows * (2 * ff_w // 128))
    (ff_terms,) = call(
        ff_kernel,
        [shaped((n_rows, sum(ff_rows), 128), BF16)],
        hidden,
        d_z_all,
        f_in,
        d_gu,
        flops=6 * count * width * ff_w,
    )
    d_f_in, ff_terms = frame_scatter(d_f_in.reshape(group, clips, local, width), ff_terms)
    ff_sum = row_scatter(ff_terms.reshape(-1, 128))
    d_x_mid, d_y_one, d_g_two, d_gate_a, d_g_three, d_scale_f = mid_back((d_h_end, d_f_in))
    d_y_group, _ = frame_gather(d_y_one.astype(BF16))
    d_y_group = d_y_group.reshape(count, width)
    d_attn = lax.dot_general(d_y_group, w_o, (((1,), (1,)), ((), ())), preferred_element_type=F32)

    d_pack, d_cross = call(
        split_kernel, [shaped((RING, 192, 128), BF16), shaped((count, heads_w), BF16)], d_attn, own_gate
    )
    d_got = lax.all_to_all(d_pack, "row", 0, 0)
    d_mix_gate = jnp.sum(d_attn * out_cross, axis=0) * (1.0 - own_gate[0] * own_gate[0])
    d_q_cross, d_k_cap, d_v_cap = cross_call(
        cross_back_kernel,
        [shaped(q_cap4.shape), shaped((heads_w, clips * caps)), shaped((heads_w, clips * caps))],
        ("toobt", "too"),
        q_cap4,
        k_cap_t,
        v_cap_t,
        bias,
        d_cross.reshape(q_cap4.shape),
    )
    d_got, (d_q_cross, d_k_cap, d_v_cap) = beside(d_got, (d_q_cross, d_k_cap, d_v_cap))
    back_scratch = [pltpu.VMEM((keys, 128), F32)]
    if n_far == 1:
        (d_send,) = call(
            functools.partial(self_back_kernel, True),
            [shaped((RING, 704, 128), BF16)],
            kv_all,
            got,
            d_got,
            o_t,
            lse,
            scratch=back_scratch,
            flops=5 * work,
        )
    else:
        d_kv, d_q = call(
            functools.partial(self_back_kernel, False),
            [shaped((kv_all.shape[0], 512, 128), BF16), shaped((RING, 192, 128), BF16)],
            kv_all,
            got,
            d_got,
            o_t,
            lse,
            scratch=back_scratch,
            flops=5 * work,
        )
        d_kv = lax.psum_scatter(d_kv, "far", scatter_dimension=0, tiled=True)
        d_send = jnp.concatenate([d_kv, d_q], axis=1)
    cap_dot = frame_sum(jnp.sum(d_k_cap * gain_cap * k_pre_t, axis=0, keepdims=True))
    wide = heads_w // n_rows
    tile = width // n_rows
    cut = (2 * wide + 16) * (clips * caps // 128)
    (out_terms,) = call(
        out_kernel,
        [shaped((n_rows, cut + tile * (heads_w // 128), 128), BF16)],
        attn_mix,
        d_y_group,
        d_k_cap,
        d_v_cap,
        cap_dot,
        flops=2 * count * width * heads_w,
    )
    d_recv, (out_terms, output, d_above, d_below) = beside(
        lax.all_to_all(d_send, "row", 0, 0), (out_terms, output, d_above, d_below)
    )
    out_sum = line_scatter(out_terms)
    d_qn, d_kn, d_v = call(
        back_kernel,
        [shaped((count, heads_w)), shaped((count, heads_w)), shaped((count, heads_w), BF16)],
        d_recv,
        d_q_cross.reshape(count, heads_w),
        cosine,
        sine,
    )
    rq, rk = rsq[:, 0:1], rsq[:, 1:2]
    d_g_query = jnp.sum(d_qn * q_zero * rq, axis=0)
    d_g_key = jnp.sum(d_kn * k_zero * rk, axis=0)
    a_q, a_k = d_qn * own_gains[0], d_kn * own_gains[1]
    dots = token_sum(jnp.stack([jnp.sum(a_q * q_zero, axis=1), jnp.sum(a_k * k_zero, axis=1)])).T / width
    d_q_low = (rq * a_q - q_zero * (rq * rq * rq * dots[:, 0:1])).astype(BF16)
    d_k_low = (rk * a_k - k_zero * (rk * rk * rk * dots[:, 1:2])).astype(BF16)
    d_qkv = jnp.concatenate([d_q_low, d_k_low, d_v], axis=1)
    d_h_in = lax.dot_general(d_qkv, w_qkv, (((1,), (1,)), ((), ())), preferred_element_type=F32)
    qkv_sum = line_scatter(term(h_in, d_qkv).reshape(n_rows, -1, 3 * heads_w))
    d_h_in, _ = frame_scatter(d_h_in.reshape(group, clips, local, width))
    d_x_pre, d_g_zero, d_scale_a = pre_back(d_h_in)
    grad_tokens = (d_x_pre + d_x_mid).reshape(tokens.shape)

    def spread(block):
        return lax.dynamic_update_slice(jnp.zeros((width,), F32), block, (me * heads_w,))

    d_mod = jnp.concatenate([d_scale_a, d_gate_a, d_scale_f, d_gate_f], axis=1)
    d_mod = d_mod.reshape(clips, n_all, mod_cols).transpose(1, 0, 2).reshape(n_all, -1)
    rest = jnp.stack(
        [
            d_g_zero,
            d_g_two,
            d_g_three,
            d_g_four,
            spread(d_g_query),
            spread(d_g_key),
            spread(d_mix_gate),
            d_above,
            d_below,
        ]
    )
    rest = rest.reshape(9, n_all, share).transpose(1, 0, 2).reshape(n_all, -1)
    small = jnp.concatenate([d_mod, rest], axis=1)
    small = jnp.pad(small, ((0, 0), (0, -small.shape[1] % 128))).reshape(n_all, -1, 128)
    small = jnp.sum(lax.all_to_all(small, ALL, 0, 0), axis=0).reshape(-1)
    d_mod = small[: clips * mod_cols].reshape(clips, mod_cols)
    rest = small[clips * mod_cols : clips * mod_cols + 9 * share].reshape(9, share)
    d_w_mod = lax.dot_general(
        step_embed, d_mod.astype(BF16), (((0,), (0,)), ((), ())), preferred_element_type=F32
    )
    ff_sum, d_w_mod = beside(ff_sum, d_w_mod)
    mine = w_down.shape[0] * group
    sum_down = to_owner(from_chunks(ff_sum[None, : ff_rows[0]], mine)).astype(F32)
    sum_gate, sum_up = jnp.split(ff_sum[ff_rows[0] :], 2)
    cap_sum = from_chunks(out_sum[None, :cut], 2 * wide + 16)
    sum_out = to_owner(from_chunks(out_sum[None, cut:].astype(BF16), tile)).astype(F32)

    def result(block):
        return from_chunks(block[None], tile).astype(F32)

    d_k_own, d_v_own, cap_dot = cap_sum[:wide], cap_sum[wide : 2 * wide], cap_sum[2 * wide : 2 * wide + 1]
    k_own = lax.dynamic_slice(k_pre_t, (my_row * wide, 0), (wide, clips * caps))
    g_own = lax.dynamic_slice(gain_cap, (my_row * wide, 0), (wide, 1))
    d_g_cap = jnp.sum(d_k_own * k_own * r_cap, axis=1)
    d_k_zero_cap = (r_cap * g_own * d_k_own - k_own * (r_cap * r_cap * r_cap * cap_dot / width)).astype(BF16)

    def cap_weight(d):
        return lax.dot_general(cap2, d, (((0,), (1,)), ((), ())), preferred_element_type=F32)

    d_w_cap_key = cap_weight(d_k_zero_cap)
    d_w_cap_value = cap_weight(d_v_own.astype(BF16))
    d_gains = jnp.concatenate([rest[:6], d_g_cap[None]], axis=0)
    d_mixes = rest[6:]

    return (
        output,
        grad_tokens,
        qkv_sum[:, :heads_w],
        qkv_sum[:, heads_w : 2 * heads_w],
        qkv_sum[:, 2 * heads_w :],
        sum_out,
        result(sum_gate),
        result(sum_up),
        sum_down,
        d_w_cap_key,
        d_w_cap_value,
        d_w_mod,
        d_gains,
        d_mixes,
    )


def solution(mesh):
    frame, row = mesh.shape["frame"], mesh.shape["row"]
    fine = Mesh(mesh.devices.reshape(frame, row // RING, RING), ("frame", "far", "row"))
    grid = P(None, "frame", ROW, None, None)
    rows, columns = P(ALL, None), P(None, ALL)
    tile = P(ROW, "frame")
    return jax.shard_map(
        body,
        mesh=fine,
        in_specs=(
            (grid,)
            + (rows,) * 7
            + (columns,) * 3
            + (P(),) * 6
            + (P(None, "frame"), P(ROW), P(), grid)
        ),
        out_specs=(grid, grid) + (tile,) * 7 + (columns,) * 5,
        check_vma=False,
    )
```

```python
import functools
import itertools
import math

import jax
import jax.numpy as jnp
from jax import lax
from jax.experimental import pallas as pl
from jax.experimental.pallas import tpu as pltpu
from jax.sharding import Mesh
from jax.sharding import PartitionSpec as P

HDIM = 64
EPS = 1e-05
THETA = 10000.0
NEG = -1000000000.0
F32 = jnp.float32
BF16 = jnp.bfloat16
RING = 8
TEAM = ("y", "x")
PLANE = ("z", "core")
GROUP = ("far", "z", "core")
FRAME = ("y", "core")
ROW = ("far", "z", "x")
ALL = ("y", "core", "far", "z", "x")


def swap(value, bits):
    return lax.ppermute(value, TEAM, [(i, i ^ bits) for i in range(4)])


def team_sum(value):
    value = value + swap(value, 1)
    return value + swap(value, 2)


def token_sum(value):
    blocks = value.reshape(value.shape[0], 4, -1)
    got = swap(blocks, 1).reshape(value.shape[0], 2, 2, -1)
    blocks = blocks + got[:, :, ::-1].reshape(blocks.shape)
    got = swap(blocks, 2)
    blocks = blocks + jnp.concatenate([got[:, 2:], got[:, :2]], axis=1)
    return blocks.reshape(value.shape)


def beside(moved, work):
    return (moved, None) if work is None else lax.optimization_barrier((moved, work))


def team_gather(value, work=None):
    others, work = beside([swap(value, k) for k in (3, 2, 1)], work)
    return jnp.stack([value, others[2], others[1], others[0]]), work


def team_scatter(terms, work=None):
    low = terms.astype(BF16)
    others, work = beside([swap(low[k], k) for k in (3, 2, 1)], work)
    return terms[0] + sum(other.astype(F32) for other in others), work


def relocate(block, target):
    sizes = [lax.axis_size(axis) for axis in ALL]
    pairs = []
    for index, where in enumerate(itertools.product(*(range(size) for size in sizes))):
        to = 0
        for size, at in zip(sizes, target(*where)):
            to = to * size + at
        pairs.append((index, to))
    return lax.ppermute(block, ALL, pairs)


def exchange(block):
    return relocate(block, lambda y, core, far, z, x: (y, x, far, z, core))


def to_owner(block):
    if lax.axis_size("far") == 1:
        return relocate(block, lambda y, core, far, z, x: (z // 2, z % 2, 0, 2 * y + x, core))
    return relocate(block, lambda y, core, far, z, x: (far // 2, far % 2, 2 * y + x, z, core))


def group_gather(block):
    return lax.all_gather(block, GROUP, axis=0, tiled=True)


def group_scatter(terms):
    terms = terms.reshape(-1, terms.shape[-1])
    return lax.psum_scatter(terms, GROUP, scatter_dimension=0, tiled=True)


def row_neighbours(block):
    count = lax.axis_size(ROW)
    forward = [(i, i + 1) for i in range(count - 1)]
    above = lax.ppermute(block, ROW, forward)
    below = lax.ppermute(block, ROW, [(b, a) for a, b in forward])
    return above, below


def to_chunks(value, size):
    blocks, rows, columns = value.shape
    value = value.reshape(blocks, rows, columns // size, size).transpose(0, 2, 1, 3)
    return value.reshape(blocks, -1, size)


def from_chunks(value, rows):
    blocks, _, size = value.shape
    return value.reshape(blocks, -1, rows, size).transpose(0, 2, 1, 3).reshape(blocks * rows, -1)


def owners(pair):
    j, k = divmod(pair, 3)
    if k == 1:
        return [(2 * j, 1, (0, 1)), (2 * j + 1, 1, (2, 3))]
    return [(2 * j + k // 2, 0, (0, 1, 2, 3))]


def q_rows(slot, chunk):
    if slot == 0:
        return 64 * (chunk % 2), chunk // 2
    return 128, chunk % 2


def lanes(shape):
    return lax.broadcasted_iota(jnp.int32, shape, len(shape) - 1)


def half(value, source, target):
    return value if source == target else pltpu.roll(value, 64, 1)


def partner(value):
    lane = lanes(value.shape) % 64
    up8, dn8 = pltpu.roll(value, 120, 1), pltpu.roll(value, 8, 1)
    up12, dn12 = pltpu.roll(value, 116, 1), pltpu.roll(value, 12, 1)
    lower = ((lane >= 16) & (lane < 28)) | ((lane >= 40) & (lane < 52))
    return jnp.where(lane < 8, up8, jnp.where(lane < 16, dn8, jnp.where(lower, up12, dn12)))


def store_queries(out_ref, base, tile, clip, pair_of_heads):
    lane = lanes((64, 128))
    for e in range(2):
        pair = 6 * clip + 2 * pair_of_heads + e
        chunk = [tile[128 * k + 64 * clip : 128 * k + 64 * clip + 64] for k in range(4)]
        for dev, slot, chunks in owners(pair):
            for lo in chunks[: len(chunks) // 2]:
                row, _ = q_rows(slot, lo)
                hi = lo + len(chunks) // 2
                value = jnp.where(lane < 64, half(chunk[lo], e, 0), half(chunk[hi], e, 1))
                out_ref[dev, base + row : base + row + 64, :] = value.astype(out_ref.dtype)


def load_queries(in_ref, base, clip, pair_of_heads):
    lane = lanes((64, 128))
    parts = []
    for e in range(2):
        pair = 6 * clip + 2 * pair_of_heads + e
        found = [None] * 4
        for dev, slot, chunks in owners(pair):
            for c in chunks:
                row, source = q_rows(slot, c)
                value = in_ref[dev, base + row : base + row + 64, :].astype(F32)
                found[c] = half(value, source, e)
        parts.append(found)
    return [jnp.where(lane < 64, a, b) for a, b in zip(*parts)]


def send_kernel(qkv_ref, rs_ref, gain_ref, cos_ref, sin_ref, send_ref, qc_ref):
    lane = lanes((64, 128))
    cosine, sine = cos_ref[...], sin_ref[...]
    rq, rk = rs_ref[:, 0:1], rs_ref[:, 1:2]
    width = 384
    for hp in range(3):
        cut = slice(128 * hp, 128 * hp + 128)
        qn = qkv_ref[:, cut] * rq * gain_ref[0:1, cut]
        kn = qkv_ref[:, width + 128 * hp : width + 128 * hp + 128] * rk * gain_ref[1:2, cut]
        vv = qkv_ref[:, 2 * width + 128 * hp : 2 * width + 128 * hp + 128]
        qc_ref[:, cut] = qn.astype(BF16)
        qr = qn * cosine + partner(qn) * sine
        kr = kn * cosine + partner(kn) * sine
        for clip in range(2):
            store_queries(send_ref, 512, qr, clip, hp)
            for e in range(2):
                for k in range(4):
                    row = 128 * k + 64 * clip
                    kc, vc = kr[row : row + 64], vv[row : row + 64]
                    value = jnp.where(lane < 64, half(kc, e, 0), half(vc, e, 1)).astype(BF16)
                    for dev, slot, _ in owners(6 * clip + 2 * hp + e):
                        at = 256 * slot + 64 * k
                        send_ref[dev, at : at + 64, :] = value


def mix_kernel(o_ref, oc_ref, gate_ref, attn_ref):
    for hp in range(3):
        cut = slice(128 * hp, 128 * hp + 128)
        gate = gate_ref[0:1, cut]
        for clip in range(2):
            for k, chunk in enumerate(load_queries(o_ref, 0, clip, hp)):
                rows = slice(128 * k + 64 * clip, 128 * k + 64 * clip + 64)
                attn_ref[rows, cut] = (chunk + gate * oc_ref[rows, cut]).astype(BF16)


def split_kernel(d_ref, gate_ref, do_ref, doc_ref):
    for hp in range(3):
        cut = slice(128 * hp, 128 * hp + 128)
        tile = d_ref[:, cut]
        doc_ref[:, cut] = (tile * gate_ref[0:1, cut]).astype(BF16)
        for clip in range(2):
            store_queries(do_ref, 0, tile, clip, hp)


def back_kernel(d_ref, dqc_ref, cos_ref, sin_ref, dqn_ref, dkn_ref, dv_ref):
    lane = lanes((64, 128))
    for hp in range(3):
        cut = slice(128 * hp, 128 * hp + 128)
        for clip in range(2):
            queries = load_queries(d_ref, 512, clip, hp)
            for k in range(4):
                rows = slice(128 * k + 64 * clip, 128 * k + 64 * clip + 64)
                cosine, sine = cos_ref[rows, :], sin_ref[rows, :]
                heads = []
                for e in range(2):
                    total = None
                    for dev, slot, _ in owners(6 * clip + 2 * hp + e):
                        at = 256 * slot + 64 * k
                        term = d_ref[dev, at : at + 64, :].astype(F32)
                        total = term if total is None else total + term
                    heads.append(total)
                dk = jnp.where(lane < 64, heads[0], half(heads[1], 0, 1))
                dv = jnp.where(lane < 64, half(heads[0], 1, 0), heads[1])
                dq = queries[k]
                dqn_ref[rows, cut] = dq * cosine + partner(dq * sine) + dqc_ref[rows, cut]
                dkn_ref[rows, cut] = dk * cosine + partner(dk * sine)
                dv_ref[rows, cut] = dv.astype(BF16)


def dot_nt(a, b):
    return lax.dot_general(a, b, (((1,), (1,)), ((), ())), preferred_element_type=F32)


def dot_nn(a, b):
    return lax.dot_general(a, b, (((1,), (0,)), ((), ())), preferred_element_type=F32)


def turned(value):
    return value.astype(F32).T.astype(BF16)


def ff_kernel(hidden_ref, dz_ref, f_in_ref, dgu_ref, out_ref):
    n_rows = out_ref.shape[0]
    part = n_rows // 4
    left = turned(hidden_ref[...])
    tile = left.shape[0] // part

    def down(c, carry):
        block = dot_nn(left, dz_ref[:, pl.ds(pl.multiple_of(384 * c, 128), 384)]).astype(BF16)
        for j in range(3):
            for h in range(part):
                out_ref[c * part + h, tile * j : tile * j + tile, :] = block[
                    tile * h : tile * h + tile, 128 * j : 128 * j + 128
                ]
        return carry

    lax.fori_loop(0, 4, down, 0)
    base = 3 * tile
    left_f = turned(f_in_ref[...])
    tile_f = left_f.shape[0] // n_rows

    def gate_up(j, carry):
        block = dot_nn(left_f, dgu_ref[:, pl.ds(pl.multiple_of(256 * j, 128), 256)]).astype(BF16)
        for e in range(2):
            at = pl.multiple_of(base + tile_f * (2 * j + e), 16)
            for r in range(n_rows):
                out_ref[r, pl.ds(at, tile_f), :] = block[
                    tile_f * r : tile_f * r + tile_f, 128 * e : 128 * e + 128
                ]
        return carry

    lax.fori_loop(0, dgu_ref.shape[1] // 256, gate_up, 0)


def out_kernel(attn_ref, dy_ref, dk_ref, dv_ref, dot_ref, out_ref):
    n_rows = out_ref.shape[0]
    wide = dk_ref.shape[0] // n_rows
    tall = 2 * wide + 16
    chunks = dk_ref.shape[1] // 128
    for r in range(n_rows):
        for j in range(chunks):
            cut = slice(128 * j, 128 * j + 128)
            block = jnp.concatenate(
                [
                    dk_ref[wide * r : wide * r + wide, cut],
                    dv_ref[wide * r : wide * r + wide, cut],
                    jnp.broadcast_to(dot_ref[:, cut], (16, 128)),
                ]
            )
            out_ref[r, tall * j : tall * j + tall, :] = block.astype(BF16)
    base = tall * chunks
    left = turned(attn_ref[...])
    tile = left.shape[0] // (n_rows // 4)
    for f in range(4):
        block = dot_nn(left, dy_ref[:, 384 * f : 384 * f + 384]).astype(BF16)
        for part in range(n_rows // 4):
            member = f * (n_rows // 4) + part
            for j in range(3):
                out_ref[member, base + tile * j : base + tile * j + tile, :] = block[
                    tile * part : tile * part + tile, 128 * j : 128 * j + 128
                ]


def dot_tt(a, b):
    return lax.dot_general(a, b, (((0,), (1,)), ((), ())), preferred_element_type=F32)


def block_of(ref, i, base):
    at = pl.multiple_of(base + 64 * (i // 4), 64)
    return ref[pl.ds(2 * (i % 4), 2), pl.ds(at, 64), :].reshape(128, 128).astype(F32)


def put_block(ref, i, base, value):
    at = pl.multiple_of(base + 64 * (i // 4), 64)
    ref[pl.ds(2 * (i % 4), 2), pl.ds(at, 64), :] = value.reshape(2, 64, 128).astype(ref.dtype)


def slot_keys(kv_ref, slot):
    return kv_ref[:, pl.ds(pl.multiple_of(256 * slot, 256), 256), :].reshape(-1, 128)


def self_kernel(kv_ref, q_ref, o_ref, ot_ref, lse_ref, kvt_ref):
    lane = lanes((128, 128))
    for slot in range(2):
        kvt_ref[slot] = turned(slot_keys(kv_ref, slot))

    def step(i, carry):
        slot = i // 8
        q = block_of(q_ref, i, 512) * (HDIM ** (-0.5))
        qa = jnp.where(lane < 64, q, 0.0)
        qb = jnp.where(lane < 64, pltpu.roll(q, 64, 1), 0.0)
        q2 = jnp.concatenate([qa, qb], axis=0).astype(BF16)
        s = dot_nt(slot_keys(kv_ref, slot), q2)
        top = jnp.max(s, axis=0, keepdims=True)
        p = jnp.exp(s - top)
        total = jnp.sum(p, axis=0, keepdims=True)
        ot = dot_nn(kvt_ref[slot], p.astype(BF16)) / total
        o = ot.T
        put_block(o_ref, i, 0, jnp.where(lane < 64, pltpu.roll(o[:128], 64, 1), o[128:]))
        ot_ref[pl.ds(i, 1)] = ot[64:].reshape(1, 64, 256)
        lse_ref[pl.ds(i, 1)] = (top + jnp.log(total)).reshape(1, 1, 256)
        return carry

    lax.fori_loop(0, 12, step, 0)


def self_back_kernel(merged, kv_ref, q_ref, do_ref, ot_ref, lse_ref, *rest):
    if merged:
        dkv_ref, acc_ref, kvt_ref = rest
        dq_ref, base = dkv_ref, 512
    else:
        dkv_ref, dq_ref, acc_ref, kvt_ref = rest
        base = 0
    lane = lanes((128, 128))
    for slot in range(2):
        kvt_ref[slot] = turned(slot_keys(kv_ref, slot))
    acc_ref[...] = jnp.zeros_like(acc_ref)

    def step(i, carry):
        slot = i // 8
        q = block_of(q_ref, i, 512) * (HDIM ** (-0.5))
        d = block_of(do_ref, i, 0)
        qa = jnp.where(lane < 64, q, 0.0)
        qb = jnp.where(lane < 64, pltpu.roll(q, 64, 1), 0.0)
        q2 = jnp.concatenate([qa, qb], axis=0).astype(BF16)
        da = jnp.where(lane < 64, 0.0, pltpu.roll(d, 64, 1))
        db = jnp.where(lane < 64, 0.0, d)
        d2 = jnp.concatenate([da, db], axis=0)
        delta = jnp.sum(d2.T[64:] * ot_ref[pl.ds(i, 1)].reshape(64, 256), axis=0, keepdims=True)
        d2 = d2.astype(BF16)
        kv = slot_keys(kv_ref, slot)
        p = jnp.exp(dot_nt(kv, q2) - lse_ref[pl.ds(i, 1)].reshape(1, 256))
        ds = (p * (dot_nt(kv, d2) - delta)).astype(BF16)
        acc_ref[slot] += dot_nn(ds, q2) + dot_nn(p.astype(BF16), d2)
        dq = dot_nn(kvt_ref[slot], ds).T * (HDIM ** (-0.5))
        put_block(dq_ref, i, base, jnp.where(lane < 64, dq[:128], pltpu.roll(dq[128:], 64, 1)))
        return carry

    lax.fori_loop(0, 12, step, 0)
    for slot in range(2):
        dkv_ref[:, 256 * slot : 256 * slot + 256, :] = (
            acc_ref[slot].reshape(-1, 256, 128).astype(dkv_ref.dtype)
        )


def cross_probs(kc, q, bias, lane, e):
    qm = jnp.where((lane < 64) == (e == 0), q, jnp.zeros_like(q))
    s = jnp.where(bias > 0.0, dot_tt(kc, qm) * (HDIM ** (-0.5)), NEG)
    p = jnp.exp(s - jnp.max(s, axis=0, keepdims=True))
    return p / jnp.sum(p, axis=0, keepdims=True), qm


def cross_kernel(q_ref, kc_ref, vc_ref, bias_ref, o_ref):
    q = q_ref[...].reshape(256, 128)
    lane = lanes((256, 128))
    bias = bias_ref[...]
    outs = []
    for e in range(2):
        p, _ = cross_probs(kc_ref[...], q, bias, lane, e)
        outs.append(dot_tt(p.astype(BF16), vc_ref[...]))
    o_ref[...] = jnp.where(lane < 64, outs[0], outs[1]).reshape(4, 1, 64, 128)


def cross_back_kernel(q_ref, kc_ref, vc_ref, bias_ref, do_ref, dq_ref, dk_ref, dv_ref):
    q = q_ref[...].reshape(256, 128)
    d = do_ref[...].reshape(256, 128)
    lane = lanes((256, 128))
    bias = bias_ref[...]
    kc, vc = kc_ref[...], vc_ref[...]
    dqs, dk, dv = [], 0.0, 0.0
    for e in range(2):
        p, qm = cross_probs(kc, q, bias, lane, e)
        dm = jnp.where((lane < 64) == (e == 0), d, jnp.zeros_like(d))
        dp = dot_tt(vc, dm)
        dt = (p * (dp - jnp.sum(p * dp, axis=0, keepdims=True))).astype(BF16)
        dqs.append(dot_tt(dt, kc))
        dk = dk + dot_tt(qm, dt)
        dv = dv + dot_tt(dm, p.astype(BF16))
    dq = jnp.where(lane < 64, dqs[0], dqs[1]) * (HDIM ** (-0.5))
    dq_ref[...] = dq.reshape(4, 1, 64, 128)
    dk_ref[...] = dk * (HDIM ** (-0.5))
    dv_ref[...] = dv


def call(kernel, outs, *args, scratch=(), flops=0):
    size = sum(math.prod(a.shape) * a.dtype.itemsize for a in (*args, *outs))
    spec = pl.BlockSpec(memory_space=pltpu.VMEM)
    return pl.pallas_call(
        kernel,
        out_shape=outs,
        in_specs=[spec] * len(args),
        out_specs=[spec] * len(outs),
        scratch_shapes=list(scratch),
        compiler_params=pltpu.CompilerParams(vmem_limit_bytes=56 << 20),
        cost_estimate=pl.CostEstimate(flops=flops, bytes_accessed=size, transcendentals=flops // 256),
    )(*args)


def cross_call(kernel, outs, specs, *args):
    token = pl.BlockSpec((4, 1, 64, 128), lambda c, h: (0, c, 0, h))
    bias = pl.BlockSpec((256, 1), lambda c, h: (c, 0))
    back = pl.BlockSpec((128, 256), lambda c, h: (h, c))
    kinds = {"t": token, "b": bias, "o": back}
    return pl.pallas_call(
        kernel,
        grid=(2, 3),
        out_shape=outs,
        in_specs=[kinds[c] for c in specs[0]],
        out_specs=[kinds[c] for c in specs[1]],
        compiler_params=pltpu.CompilerParams(vmem_limit_bytes=40 << 20),
        cost_estimate=pl.CostEstimate(
            flops=12 * len(args) * 256 * 256 * 128, bytes_accessed=4 << 20, transcendentals=12 << 16
        ),
    )(*args)


def shaped(shape, dtype=F32):
    return jax.ShapeDtypeStruct(shape, dtype)


def rms_norm(tensor, gain):
    return tensor * lax.rsqrt(jnp.mean(tensor * tensor, axis=-1, keepdims=True) + EPS) * gain


def rotary_lanes():
    parts = ((0, 16), (1, 24), (2, 24))
    freqs = [[], [], []]
    signs = []
    for which, size in parts:
        for upper in range(2):
            for i in range(size // 2):
                for p in range(3):
                    freqs[p].append(math.exp(-math.log(THETA) * 2.0 * i / size) if p == which else 0.0)
                signs.append(1.0 if upper else -1.0)
    return [jnp.array(f, F32) for f in freqs], jnp.array(signs, F32)


def mm(a, b):
    return jnp.dot(a, b, preferred_element_type=F32)


def body(
    tokens,
    w_query,
    w_key,
    w_value,
    w_out,
    w_gate,
    w_up,
    w_down,
    w_cap_key,
    w_cap_value,
    w_mod,
    norm_gains,
    mix_coefs,
    caption,
    cap_len,
    cap_mask,
    timesteps,
    frame_pos,
    row_pos,
    col_pos,
    grad_out,
):
    clips, frames, rows_here, cols, width = tokens.shape
    local = frames * rows_here * cols
    group = lax.axis_size("y") * lax.axis_size("x")
    n_rows = lax.axis_size(ROW)
    n_far = lax.axis_size("far")
    n_all = group * n_rows
    me = lax.axis_index(TEAM)
    my_member = lax.axis_index(GROUP)
    heads_w = width // group
    ff_w = w_gate.shape[1] // group
    count = group * clips * local
    caps = caption.shape[1]
    share = width // n_all

    rows = w_query.shape[0]
    cap2 = caption.reshape(clips * caps, width)

    def by_columns(parts):
        cut = jnp.concatenate([w.reshape(rows, group, -1) for w in parts], axis=2)
        cut = lax.all_to_all(cut.transpose(1, 0, 2), TEAM, 0, 0)
        return cut.reshape(group * rows, -1)

    def in_order(gathered):
        full = gathered.reshape(n_far, RING // 2, 2, 2, 2, rows, -1).transpose(3, 2, 0, 1, 4, 5, 6)
        return full.reshape(width, -1)

    def cap_columns(weight):
        return lax.dot_general(weight, cap2, (((0,), (1,)), ((), ())), preferred_element_type=F32).astype(BF16)

    cut_qkv = by_columns([w_query, w_key, w_value])
    cut_gu = by_columns([w_gate, w_up])

    half_width = width // 2
    frequencies = jnp.exp(-math.log(THETA) * jnp.arange(half_width, dtype=F32) / half_width)
    phases = timesteps.astype(F32)[:, None] * frequencies[None, :]
    step_embed = jax.nn.silu(jnp.concatenate([jnp.cos(phases), jnp.sin(phases)], axis=1)).astype(BF16)
    mod_local = mm(step_embed, w_mod).astype(BF16).astype(F32)
    mod_cols = mod_local.shape[1]
    note = jnp.concatenate([mod_local.reshape(-1), frame_pos.astype(F32).reshape(-1), row_pos.astype(F32)])
    used = note.shape[0]
    note = jnp.pad(note, (0, -used % 512)).reshape(1, -1, 128)
    note = lax.all_to_all(jnp.broadcast_to(note, (n_all,) + note.shape[1:]), ALL, 0, 0)
    note = note.reshape(n_all, -1)
    x_own = tokens.reshape(clips, local, width)
    x_flat = x_own.astype(F32)
    x_group, _ = team_gather(x_own)
    w_qkv = in_order(group_gather(cut_qkv))
    side = jnp.concatenate([cap_columns(w_cap_key), cap_columns(w_cap_value), w_out], axis=1)
    side = group_gather(exchange(side))
    tokens_c = clips * caps
    w_gu = group_gather(cut_gu)
    w_dn = group_gather(exchange(w_down))
    mod_full = note[:, : clips * mod_cols].reshape(n_all, clips, mod_cols)
    mod_full = mod_full.transpose(1, 0, 2).reshape(clips, 4, width)
    scale_a, gate_a, scale_f, gate_f = (mod_full[:, i] for i in range(4))
    positions = note[:, clips * mod_cols : used].reshape(2, 2, n_far, RING // 2, 2, -1)
    here = [lax.axis_index(axis) for axis in ("core", "far", "z")]
    positions = lax.dynamic_slice(positions, (0, *here, 0, 0), (2, 1, 1, 1, 2, positions.shape[-1]))
    order = jnp.arange(group)
    chosen = (order[None, :] == (me ^ order)[:, None]).astype(F32)
    positions = jnp.sum(chosen[:, :, None] * positions.reshape(1, group, -1), axis=1)

    above_g, below_g = row_neighbours(grad_out)
    gains = norm_gains
    own_gains = lax.dynamic_slice(gains, (4, me * heads_w), (3, heads_w))
    own_gate = jnp.tanh(lax.dynamic_slice(mix_coefs, (0, me * heads_w), (1, heads_w)))

    full = (group, clips, frames, cols)
    frame_at = positions[:, :-1].reshape(group, clips, frames) + cap_len.astype(F32)[None, :, None]
    pos_a = jnp.broadcast_to(frame_at[..., None], full)
    pos_b = jnp.broadcast_to(positions[:, -1:, None, None], full)
    pos_e = jnp.broadcast_to(col_pos.astype(F32), full)
    (fa, fb, fe), sign = rotary_lanes()
    angle = (
        pos_a.reshape(count, 1) * fa + pos_b.reshape(count, 1) * fb + pos_e.reshape(count, 1) * fe
    )
    cosine = jnp.tile(jnp.cos(angle), (1, 2))
    sine = jnp.tile(jnp.sin(angle) * sign, (1, 2))

    def pre_piece(x_in, gain, scale_in):
        return rms_norm(x_in, gain) * (1.0 + scale_in[:, None, :])

    h_in = pre_piece(x_group.astype(F32), gains[0], scale_a).astype(BF16).reshape(count, width)
    h_in = lax.optimization_barrier(h_in)
    _, pre_back = jax.vjp(pre_piece, x_flat, gains[0], scale_a)
    qkv = mm(h_in, w_qkv)
    q_zero, k_zero = qkv[:, :heads_w], qkv[:, heads_w : 2 * heads_w]
    squares = jnp.stack([jnp.sum(q_zero * q_zero, axis=1), jnp.sum(k_zero * k_zero, axis=1)])
    rsq = lax.rsqrt(token_sum(squares) / width + EPS).T
    send, q_cap = call(
        send_kernel,
        [shaped((RING, 704, 128), BF16), shaped((count, heads_w), BF16)],
        qkv,
        rsq,
        own_gains,
        cosine,
        sine,
    )
    send, side = beside(send, side)
    k_pre_t, v_cap_t, w_o = side[:, :tokens_c], side[:, tokens_c : 2 * tokens_c], side[:, 2 * tokens_c :]
    got = lax.all_to_all(send, PLANE, 0, 0)
    kv_all = got
    if n_far > 1:
        kv_all = lax.all_gather(got, "far", axis=0, tiled=True)
    keys = kv_all.shape[0] * 256
    work = 12 * keys * 256 * 128 * 2
    o_pack, o_t, lse = call(
        self_kernel,
        [shaped((RING, 192, 128), BF16), shaped((12, 64, 256)), shaped((12, 1, 256))],
        kv_all,
        got,
        scratch=[pltpu.VMEM((2, 128, keys), BF16)],
        flops=2 * work,
    )
    o_back = lax.all_to_all(o_pack, PLANE, 0, 0)
    o_back, w_gu = beside(o_back, w_gu)
    w_gu = in_order(w_gu)

    usable = (jnp.arange(caps)[None, :] < cap_len[:, None]) & (cap_mask > 0)
    bias = usable.astype(F32).reshape(clips * caps, 1)
    k_pre_t = k_pre_t.astype(F32)
    gain_cap = own_gains[2][:, None]
    r_cap = lax.rsqrt(team_sum(jnp.sum(k_pre_t * k_pre_t, axis=0, keepdims=True)) / width + EPS)
    k_cap_t = (k_pre_t * r_cap * gain_cap).astype(BF16)
    q_cap4 = q_cap.reshape(group, clips, local, heads_w)
    (out_cross,) = cross_call(
        cross_kernel, [shaped(q_cap4.shape)], ("toob", "t"), q_cap4, k_cap_t, v_cap_t, bias
    )
    o_back, out_cross = beside(o_back, out_cross)
    out_cross = out_cross.reshape(count, heads_w)
    (attn_mix,) = call(mix_kernel, [shaped((count, heads_w), BF16)], o_back, out_cross, own_gate)

    y_one, _ = team_scatter(mm(attn_mix, w_o).reshape(group, clips, local, width))

    def mid_piece(x_in, y_in, gain_two, gate_in, gain_three, scale_in):
        h_mid = x_in + jnp.tanh(gate_in)[:, None, :] * rms_norm(y_in, gain_two)
        return (h_mid, rms_norm(h_mid, gain_three) * (1.0 + scale_in[:, None, :]))

    (h_mid, f_in32), mid_back = jax.vjp(mid_piece, x_flat, y_one, gains[1], gate_a, gains[2], scale_f)
    f_in, _ = team_gather(f_in32.astype(BF16))
    f_in = f_in.reshape(count, width)
    gate_up = mm(f_in, w_gu)

    def act_piece(gate_in, up_in):
        return jax.nn.silu(gate_in) * up_in

    hidden32, act_back = jax.vjp(act_piece, gate_up[:, :ff_w], gate_up[:, ff_w:])
    hidden = hidden32.astype(BF16)
    z_out, _ = team_scatter(mm(hidden, w_dn).reshape(group, clips, local, width))

    def end_piece(h_in_mid, z_in, gain_four, gate_in):
        return h_in_mid + jnp.tanh(gate_in)[:, None, :] * rms_norm(z_in, gain_four)

    y_all, end_back = jax.vjp(end_piece, h_mid, z_out, gains[3], gate_f)
    y_grid = y_all.reshape(tokens.shape)
    above, below = row_neighbours(y_grid.astype(BF16))
    g_center = grad_out.astype(F32)
    d_y = g_center + mix_coefs[1] * below_g.astype(F32) + mix_coefs[2] * above_g.astype(F32)
    d_h_end, d_z, d_g_four, d_gate_f = end_back(d_y.reshape(clips, local, width))
    d_z_all, _ = team_gather(d_z.astype(BF16))
    d_z_all = d_z_all.reshape(count, width)
    d_hidden = lax.dot_general(d_z_all, w_dn, (((1,), (1,)), ((), ())), preferred_element_type=F32)
    d_gu = jnp.concatenate([d.astype(BF16) for d in act_back(d_hidden)], axis=1)
    d_f_in = lax.dot_general(d_gu, w_gu, (((1,), (1,)), ((), ())), preferred_element_type=F32)
    def term(left, right):
        return lax.dot_general(left, right, (((0,), (0,)), ((), ())), preferred_element_type=F32).astype(BF16)

    ff_rows = (w_down.shape[0] * group * (heads_w // 128), width // n_rows * (2 * ff_w // 128))
    (ff_terms,) = call(
        ff_kernel,
        [shaped((n_rows, sum(ff_rows), 128), BF16)],
        hidden,
        d_z_all,
        f_in,
        d_gu,
        flops=6 * count * width * ff_w,
    )
    d_f_in, ff_terms = team_scatter(d_f_in.reshape(group, clips, local, width), ff_terms)
    ff_sum = group_scatter(ff_terms)
    d_x_mid, d_y_one, d_g_two, d_gate_a, d_g_three, d_scale_f = mid_back((d_h_end, d_f_in))
    d_y_group, (above, below) = team_gather(d_y_one.astype(BF16), (above, below))
    d_y_group = d_y_group.reshape(count, width)
    d_attn = lax.dot_general(d_y_group, w_o, (((1,), (1,)), ((), ())), preferred_element_type=F32)

    d_pack, d_cross = call(
        split_kernel, [shaped((RING, 192, 128), BF16), shaped((count, heads_w), BF16)], d_attn, own_gate
    )
    d_got = lax.all_to_all(d_pack, PLANE, 0, 0)
    above, below = above.astype(F32), below.astype(F32)
    output = (y_grid + mix_coefs[1] * above + mix_coefs[2] * below).astype(BF16)
    d_above = jnp.sum(g_center * above, axis=(0, 1, 2, 3))
    d_below = jnp.sum(g_center * below, axis=(0, 1, 2, 3))
    d_mix_gate = jnp.sum(d_attn * out_cross, axis=0) * (1.0 - own_gate[0] * own_gate[0])
    d_q_cross, d_k_cap, d_v_cap = cross_call(
        cross_back_kernel,
        [shaped(q_cap4.shape), shaped((heads_w, clips * caps)), shaped((heads_w, clips * caps))],
        ("toobt", "too"),
        q_cap4,
        k_cap_t,
        v_cap_t,
        bias,
        d_cross.reshape(q_cap4.shape),
    )
    cap_dot = team_sum(jnp.sum(d_k_cap * gain_cap * k_pre_t, axis=0, keepdims=True))
    wide = heads_w // n_rows
    tile = width // n_rows
    cut = (2 * wide + 16) * (clips * caps // 128)
    (out_terms,) = call(
        out_kernel,
        [shaped((n_rows, cut + tile * (heads_w // 128), 128), BF16)],
        attn_mix,
        d_y_group,
        d_k_cap,
        d_v_cap,
        cap_dot,
        flops=2 * count * width * heads_w,
    )
    d_got, (d_q_cross, out_terms) = beside(d_got, (d_q_cross, out_terms))
    back_scratch = [pltpu.VMEM((2, keys, 128), F32), pltpu.VMEM((2, 128, keys), BF16)]
    if n_far == 1:
        (d_send,) = call(
            functools.partial(self_back_kernel, True),
            [shaped((RING, 704, 128), BF16)],
            kv_all,
            got,
            d_got,
            o_t,
            lse,
            scratch=back_scratch,
            flops=5 * work,
        )
    else:
        d_kv, d_q = call(
            functools.partial(self_back_kernel, False),
            [shaped((kv_all.shape[0], 512, 128), BF16), shaped((RING, 192, 128), BF16)],
            kv_all,
            got,
            d_got,
            o_t,
            lse,
            scratch=back_scratch,
            flops=5 * work,
        )
        d_kv = lax.psum_scatter(d_kv, "far", scatter_dimension=0, tiled=True)
        d_send = jnp.concatenate([d_kv, d_q], axis=1)
    d_recv, (output, d_above, d_below, ff_sum) = beside(
        lax.all_to_all(d_send, PLANE, 0, 0), (output, d_above, d_below, ff_sum)
    )
    out_terms, ff_sum = beside(out_terms, ff_sum)
    out_sum = group_scatter(out_terms)
    d_qn, d_kn, d_v = call(
        back_kernel,
        [shaped((count, heads_w)), shaped((count, heads_w)), shaped((count, heads_w), BF16)],
        d_recv,
        d_q_cross.reshape(count, heads_w),
        cosine,
        sine,
    )
    rq, rk = rsq[:, 0:1], rsq[:, 1:2]
    d_g_query = jnp.sum(d_qn * q_zero * rq, axis=0)
    d_g_key = jnp.sum(d_kn * k_zero * rk, axis=0)
    a_q, a_k = d_qn * own_gains[0], d_kn * own_gains[1]
    dots = token_sum(jnp.stack([jnp.sum(a_q * q_zero, axis=1), jnp.sum(a_k * k_zero, axis=1)])).T / width
    d_q_low = (rq * a_q - q_zero * (rq * rq * rq * dots[:, 0:1])).astype(BF16)
    d_k_low = (rk * a_k - k_zero * (rk * rk * rk * dots[:, 1:2])).astype(BF16)
    d_qkv = jnp.concatenate([d_q_low, d_k_low, d_v], axis=1)
    d_qkv, term_qkv = beside(d_qkv, term(h_in, d_qkv))
    term_qkv, out_sum = beside(term_qkv, out_sum)
    qkv_sum = group_scatter(term_qkv)
    d_h_in = lax.dot_general(d_qkv, w_qkv, (((1,), (1,)), ((), ())), preferred_element_type=F32)
    d_h_in, _ = team_scatter(d_h_in.reshape(group, clips, local, width))
    d_x_pre, d_g_zero, d_scale_a = pre_back(d_h_in)
    grad_tokens = (d_x_pre + d_x_mid).reshape(tokens.shape)

    def spread(block):
        return lax.dynamic_update_slice(jnp.zeros((width,), F32), block, (me * heads_w,))

    d_mod = jnp.concatenate([d_scale_a, d_gate_a, d_scale_f, d_gate_f], axis=1)
    d_mod = d_mod.reshape(clips, n_all, mod_cols).transpose(1, 0, 2).reshape(n_all, -1)
    rest = jnp.stack(
        [
            d_g_zero,
            d_g_two,
            d_g_three,
            d_g_four,
            spread(d_g_query),
            spread(d_g_key),
            spread(d_mix_gate),
            d_above,
            d_below,
        ]
    )
    rest = rest.reshape(9, n_all, share).transpose(1, 0, 2).reshape(n_all, -1)
    small = jnp.concatenate([d_mod, rest], axis=1)
    small = jnp.pad(small, ((0, 0), (0, -small.shape[1] % 128))).reshape(n_all, -1, 128)
    small = jnp.sum(lax.all_to_all(small, ALL, 0, 0), axis=0).reshape(-1)
    d_mod = small[: clips * mod_cols].reshape(clips, mod_cols)
    rest = small[clips * mod_cols : clips * mod_cols + 9 * share].reshape(9, share)
    d_w_mod = lax.dot_general(
        step_embed, d_mod.astype(BF16), (((0,), (0,)), ((), ())), preferred_element_type=F32
    )
    three = heads_w // 128
    mine = w_down.shape[0] * group
    sum_down = to_owner(from_chunks(ff_sum[None, : ff_rows[0]], mine)).astype(F32)
    sum_gate, sum_up = jnp.split(exchange(ff_sum[ff_rows[0] :]), 2)
    cap_sum = from_chunks(out_sum[None, :cut].astype(F32), 2 * wide + 16)
    sum_out = to_owner(from_chunks(out_sum[None, cut:], tile)).astype(F32)
    qkv_sum = exchange(qkv_sum).astype(F32)

    def result(block):
        return from_chunks(block[None], tile).astype(F32)

    d_k_own, d_v_own, cap_dot = cap_sum[:wide], cap_sum[wide : 2 * wide], cap_sum[2 * wide : 2 * wide + 1]
    k_own = lax.dynamic_slice(k_pre_t, (my_member * wide, 0), (wide, clips * caps))
    g_own = lax.dynamic_slice(gain_cap, (my_member * wide, 0), (wide, 1))
    d_g_cap = exchange(jnp.sum(d_k_own * k_own * r_cap, axis=1)[None])
    d_k_zero_cap = r_cap * g_own * d_k_own - k_own * (r_cap * r_cap * r_cap * cap_dot / width)
    d_caps = exchange(jnp.concatenate([d_k_zero_cap, d_v_own]).astype(BF16))

    def cap_weight(d):
        return lax.dot_general(cap2, d, (((0,), (1,)), ((), ())), preferred_element_type=F32)

    d_w_cap_key = cap_weight(d_caps[:wide])
    d_w_cap_value = cap_weight(d_caps[wide:])
    d_gains = jnp.concatenate([rest[:6], d_g_cap], axis=0)
    d_mixes = rest[6:]

    return (
        output,
        grad_tokens,
        qkv_sum[:, :heads_w],
        qkv_sum[:, heads_w : 2 * heads_w],
        qkv_sum[:, 2 * heads_w :],
        sum_out,
        result(sum_gate),
        result(sum_up),
        sum_down,
        d_w_cap_key,
        d_w_cap_value,
        d_w_mod,
        d_gains,
        d_mixes,
    )


def solution(mesh):
    frame, row = mesh.shape["frame"], mesh.shape["row"]
    fine = Mesh(mesh.devices.reshape(frame // 2, 2, row // RING, RING // 2, 2), ALL)
    grid = P(None, FRAME, ROW, None, None)
    rows, columns = P(ALL, None), P(None, ALL)
    tile = P(ROW, FRAME)
    return jax.shard_map(
        body,
        mesh=fine,
        in_specs=(
            (grid,)
            + (rows,) * 7
            + (columns,) * 3
            + (P(),) * 6
            + (P(None, FRAME), P(ROW), P(), grid)
        ),
        out_specs=(grid, grid) + (tile,) * 7 + (columns,) * 5,
        check_vma=False,
    )
```

```python
import functools
import itertools
import math

import jax
import jax.numpy as jnp
from jax import lax
from jax.experimental import pallas as pl
from jax.experimental.pallas import tpu as pltpu
from jax.sharding import Mesh
from jax.sharding import PartitionSpec as P

HDIM = 64
EPS = 1e-05
THETA = 10000.0
NEG = -1000000000.0
F32 = jnp.float32
BF16 = jnp.bfloat16
RING = 8
TEAM = ("y", "x")
PLANE = ("z", "core")
GROUP = ("far", "z", "core")
FRAME = ("y", "core")
ROW = ("far", "z", "x")
ALL = ("y", "core", "far", "z", "x")


def swap(value, bits):
    return lax.ppermute(value, TEAM, [(i, i ^ bits) for i in range(4)])


def team_sum(value):
    one, two, three = (swap(value, k) for k in (1, 2, 3))
    return (value + one) + (two + three)


def token_sum(value):
    blocks = value.reshape(value.shape[0], 4, -1)
    one, two, three = (swap(blocks, k) for k in (1, 2, 3))
    pairs = one.reshape(value.shape[0], 2, 2, -1)[:, :, ::-1].reshape(blocks.shape)
    halves = jnp.concatenate([two[:, 2:], two[:, :2]], axis=1)
    return ((blocks + pairs) + (halves + three[:, ::-1])).reshape(value.shape)


def beside(moved, work):
    return (moved, None) if work is None else lax.optimization_barrier((moved, work))


def team_gather(value, work=None):
    others, work = beside([swap(value, k) for k in (3, 2, 1)], work)
    return jnp.stack([value, others[2], others[1], others[0]]), work


def team_scatter(terms, work=None):
    low = terms.astype(BF16)
    others, work = beside([swap(low[k], k) for k in (3, 2, 1)], work)
    return terms[0] + sum(other.astype(F32) for other in others), work


def relocate(block, target):
    sizes = [lax.axis_size(axis) for axis in ALL]
    pairs = []
    for index, where in enumerate(itertools.product(*(range(size) for size in sizes))):
        to = 0
        for size, at in zip(sizes, target(*where)):
            to = to * size + at
        pairs.append((index, to))
    return lax.ppermute(block, ALL, pairs)


def exchange(block):
    return relocate(block, lambda y, core, far, z, x: (y, x, far, z, core))


def to_owner(block):
    if lax.axis_size("far") == 1:
        return relocate(block, lambda y, core, far, z, x: (z // 2, z % 2, 0, 2 * y + x, core))
    return relocate(block, lambda y, core, far, z, x: (far // 2, far % 2, 2 * y + x, z, core))


def group_gather(block):
    return lax.all_gather(block, GROUP, axis=0, tiled=True)


def group_scatter(terms):
    terms = terms.reshape(-1, terms.shape[-1])
    return lax.psum_scatter(terms, GROUP, scatter_dimension=0, tiled=True)


def row_neighbours(block):
    count = lax.axis_size(ROW)
    forward = [(i, i + 1) for i in range(count - 1)]
    above = lax.ppermute(block, ROW, forward)
    below = lax.ppermute(block, ROW, [(b, a) for a, b in forward])
    return above, below


def to_chunks(value, size):
    blocks, rows, columns = value.shape
    value = value.reshape(blocks, rows, columns // size, size).transpose(0, 2, 1, 3)
    return value.reshape(blocks, -1, size)


def from_chunks(value, rows):
    blocks, _, size = value.shape
    return value.reshape(blocks, -1, rows, size).transpose(0, 2, 1, 3).reshape(blocks * rows, -1)


def owners(pair):
    j, k = divmod(pair, 3)
    if k == 1:
        return [(2 * j, 1, (0, 1)), (2 * j + 1, 1, (2, 3))]
    return [(2 * j + k // 2, 0, (0, 1, 2, 3))]


def q_rows(slot, chunk):
    if slot == 0:
        return 64 * (chunk % 2), chunk // 2
    return 128, chunk % 2


def lanes(shape):
    return lax.broadcasted_iota(jnp.int32, shape, len(shape) - 1)


def half(value, source, target):
    return value if source == target else pltpu.roll(value, 64, 1)


def partner(value):
    lane = lanes(value.shape) % 64
    up8, dn8 = pltpu.roll(value, 120, 1), pltpu.roll(value, 8, 1)
    up12, dn12 = pltpu.roll(value, 116, 1), pltpu.roll(value, 12, 1)
    lower = ((lane >= 16) & (lane < 28)) | ((lane >= 40) & (lane < 52))
    return jnp.where(lane < 8, up8, jnp.where(lane < 16, dn8, jnp.where(lower, up12, dn12)))


def store_queries(out_ref, base, tile, clip, pair_of_heads):
    lane = lanes((64, 128))
    for e in range(2):
        pair = 6 * clip + 2 * pair_of_heads + e
        chunk = [tile[128 * k + 64 * clip : 128 * k + 64 * clip + 64] for k in range(4)]
        for dev, slot, chunks in owners(pair):
            for lo in chunks[: len(chunks) // 2]:
                row, _ = q_rows(slot, lo)
                hi = lo + len(chunks) // 2
                value = jnp.where(lane < 64, half(chunk[lo], e, 0), half(chunk[hi], e, 1))
                out_ref[dev, base + row : base + row + 64, :] = value.astype(out_ref.dtype)


def load_queries(in_ref, base, clip, pair_of_heads):
    lane = lanes((64, 128))
    parts = []
    for e in range(2):
        pair = 6 * clip + 2 * pair_of_heads + e
        found = [None] * 4
        for dev, slot, chunks in owners(pair):
            for c in chunks:
                row, source = q_rows(slot, c)
                value = in_ref[dev, base + row : base + row + 64, :].astype(F32)
                found[c] = half(value, source, e)
        parts.append(found)
    return [jnp.where(lane < 64, a, b) for a, b in zip(*parts)]


def send_kernel(qkv_ref, rs_ref, gain_ref, cos_ref, sin_ref, send_ref, qc_ref):
    lane = lanes((64, 128))
    cosine, sine = cos_ref[...], sin_ref[...]
    rq, rk = rs_ref[:, 0:1], rs_ref[:, 1:2]
    width = 384
    for hp in range(3):
        cut = slice(128 * hp, 128 * hp + 128)
        qn = qkv_ref[:, cut] * rq * gain_ref[0:1, cut]
        kn = qkv_ref[:, width + 128 * hp : width + 128 * hp + 128] * rk * gain_ref[1:2, cut]
        vv = qkv_ref[:, 2 * width + 128 * hp : 2 * width + 128 * hp + 128]
        qc_ref[:, cut] = qn.astype(BF16)
        qr = qn * cosine + partner(qn) * sine
        kr = kn * cosine + partner(kn) * sine
        for clip in range(2):
            store_queries(send_ref, 512, qr, clip, hp)
            for e in range(2):
                for k in range(4):
                    row = 128 * k + 64 * clip
                    kc, vc = kr[row : row + 64], vv[row : row + 64]
                    value = jnp.where(lane < 64, half(kc, e, 0), half(vc, e, 1)).astype(BF16)
                    for dev, slot, _ in owners(6 * clip + 2 * hp + e):
                        at = 256 * slot + 64 * k
                        send_ref[dev, at : at + 64, :] = value


def mix_kernel(o_ref, oc_ref, gate_ref, attn_ref):
    for hp in range(3):
        cut = slice(128 * hp, 128 * hp + 128)
        gate = gate_ref[0:1, cut]
        for clip in range(2):
            for k, chunk in enumerate(load_queries(o_ref, 0, clip, hp)):
                rows = slice(128 * k + 64 * clip, 128 * k + 64 * clip + 64)
                attn_ref[rows, cut] = (chunk + gate * oc_ref[rows, cut]).astype(BF16)


def split_kernel(d_ref, gate_ref, do_ref, doc_ref):
    for hp in range(3):
        cut = slice(128 * hp, 128 * hp + 128)
        tile = d_ref[:, cut]
        doc_ref[:, cut] = (tile * gate_ref[0:1, cut]).astype(BF16)
        for clip in range(2):
            store_queries(do_ref, 0, tile, clip, hp)


def back_kernel(d_ref, dqc_ref, cos_ref, sin_ref, dqn_ref, dkn_ref, dv_ref):
    lane = lanes((64, 128))
    for hp in range(3):
        cut = slice(128 * hp, 128 * hp + 128)
        for clip in range(2):
            queries = load_queries(d_ref, 512, clip, hp)
            for k in range(4):
                rows = slice(128 * k + 64 * clip, 128 * k + 64 * clip + 64)
                cosine, sine = cos_ref[rows, :], sin_ref[rows, :]
                heads = []
                for e in range(2):
                    total = None
                    for dev, slot, _ in owners(6 * clip + 2 * hp + e):
                        at = 256 * slot + 64 * k
                        term = d_ref[dev, at : at + 64, :].astype(F32)
                        total = term if total is None else total + term
                    heads.append(total)
                dk = jnp.where(lane < 64, heads[0], half(heads[1], 0, 1))
                dv = jnp.where(lane < 64, half(heads[0], 1, 0), heads[1])
                dq = queries[k]
                dqn_ref[rows, cut] = dq * cosine + partner(dq * sine) + dqc_ref[rows, cut]
                dkn_ref[rows, cut] = dk * cosine + partner(dk * sine)
                dv_ref[rows, cut] = dv.astype(BF16)


def dot_nt(a, b):
    return lax.dot_general(a, b, (((1,), (1,)), ((), ())), preferred_element_type=F32)


def dot_nn(a, b):
    return lax.dot_general(a, b, (((1,), (0,)), ((), ())), preferred_element_type=F32)


def turned(value):
    return value.astype(F32).T.astype(BF16)


def ff_kernel(hidden_ref, dz_ref, f_in_ref, dgu_ref, out_ref):
    n_rows = out_ref.shape[0]
    part = n_rows // 4
    left = turned(hidden_ref[...])
    tile = left.shape[0] // part

    def down(c, carry):
        block = dot_nn(left, dz_ref[:, pl.ds(pl.multiple_of(384 * c, 128), 384)]).astype(BF16)
        for j in range(3):
            for h in range(part):
                out_ref[c * part + h, tile * j : tile * j + tile, :] = block[
                    tile * h : tile * h + tile, 128 * j : 128 * j + 128
                ]
        return carry

    lax.fori_loop(0, 4, down, 0)
    base = 3 * tile
    left_f = turned(f_in_ref[...])
    tile_f = left_f.shape[0] // n_rows

    def gate_up(j, carry):
        block = dot_nn(left_f, dgu_ref[:, pl.ds(pl.multiple_of(256 * j, 128), 256)]).astype(BF16)
        for e in range(2):
            at = pl.multiple_of(base + tile_f * (2 * j + e), 16)
            for r in range(n_rows):
                out_ref[r, pl.ds(at, tile_f), :] = block[
                    tile_f * r : tile_f * r + tile_f, 128 * e : 128 * e + 128
                ]
        return carry

    lax.fori_loop(0, dgu_ref.shape[1] // 256, gate_up, 0)


def out_kernel(attn_ref, dy_ref, dk_ref, dv_ref, dot_ref, out_ref):
    n_rows = out_ref.shape[0]
    wide = dk_ref.shape[0] // n_rows
    tall = 2 * wide + 16
    chunks = dk_ref.shape[1] // 128
    for r in range(n_rows):
        for j in range(chunks):
            cut = slice(128 * j, 128 * j + 128)
            block = jnp.concatenate(
                [
                    dk_ref[wide * r : wide * r + wide, cut],
                    dv_ref[wide * r : wide * r + wide, cut],
                    jnp.broadcast_to(dot_ref[:, cut], (16, 128)),
                ]
            )
            out_ref[r, tall * j : tall * j + tall, :] = block.astype(BF16)
    base = tall * chunks
    left = turned(attn_ref[...])
    tile = left.shape[0] // (n_rows // 4)
    for f in range(4):
        block = dot_nn(left, dy_ref[:, 384 * f : 384 * f + 384]).astype(BF16)
        for part in range(n_rows // 4):
            member = f * (n_rows // 4) + part
            for j in range(3):
                out_ref[member, base + tile * j : base + tile * j + tile, :] = block[
                    tile * part : tile * part + tile, 128 * j : 128 * j + 128
                ]


def dot_tt(a, b):
    return lax.dot_general(a, b, (((0,), (1,)), ((), ())), preferred_element_type=F32)


def block_of(ref, i, base):
    at = pl.multiple_of(base + 64 * (i // 4), 64)
    return ref[pl.ds(2 * (i % 4), 2), pl.ds(at, 64), :].reshape(128, 128).astype(F32)


def put_block(ref, i, base, value):
    at = pl.multiple_of(base + 64 * (i // 4), 64)
    ref[pl.ds(2 * (i % 4), 2), pl.ds(at, 64), :] = value.reshape(2, 64, 128).astype(ref.dtype)


def slot_keys(kv_ref, slot):
    return kv_ref[:, pl.ds(pl.multiple_of(256 * slot, 256), 256), :].reshape(-1, 128)


def self_kernel(kv_ref, q_ref, o_ref, ot_ref, lse_ref, kvt_ref):
    lane = lanes((128, 128))
    for slot in range(2):
        kvt_ref[slot] = turned(slot_keys(kv_ref, slot))

    def step(i, carry):
        slot = i // 8
        q = block_of(q_ref, i, 512) * (HDIM ** (-0.5))
        qa = jnp.where(lane < 64, q, 0.0)
        qb = jnp.where(lane < 64, pltpu.roll(q, 64, 1), 0.0)
        q2 = jnp.concatenate([qa, qb], axis=0).astype(BF16)
        s = dot_nt(slot_keys(kv_ref, slot), q2)
        top = jnp.max(s, axis=0, keepdims=True)
        p = jnp.exp(s - top)
        total = jnp.sum(p, axis=0, keepdims=True)
        ot = dot_nn(kvt_ref[slot], p.astype(BF16)) / total
        o = ot.T
        put_block(o_ref, i, 0, jnp.where(lane < 64, pltpu.roll(o[:128], 64, 1), o[128:]))
        ot_ref[pl.ds(i, 1)] = ot[64:].reshape(1, 64, 256)
        lse_ref[pl.ds(i, 1)] = (top + jnp.log(total)).reshape(1, 1, 256)
        return carry

    lax.fori_loop(0, 12, step, 0)


def self_back_kernel(merged, kv_ref, q_ref, do_ref, ot_ref, lse_ref, *rest):
    if merged:
        dkv_ref, acc_ref, kvt_ref = rest
        dq_ref, base = dkv_ref, 512
    else:
        dkv_ref, dq_ref, acc_ref, kvt_ref = rest
        base = 0
    lane = lanes((128, 128))
    for slot in range(2):
        kvt_ref[slot] = turned(slot_keys(kv_ref, slot))
    acc_ref[...] = jnp.zeros_like(acc_ref)

    def step(i, carry):
        slot = i // 8
        q = block_of(q_ref, i, 512) * (HDIM ** (-0.5))
        d = block_of(do_ref, i, 0)
        qa = jnp.where(lane < 64, q, 0.0)
        qb = jnp.where(lane < 64, pltpu.roll(q, 64, 1), 0.0)
        q2 = jnp.concatenate([qa, qb], axis=0).astype(BF16)
        da = jnp.where(lane < 64, 0.0, pltpu.roll(d, 64, 1))
        db = jnp.where(lane < 64, 0.0, d)
        d2 = jnp.concatenate([da, db], axis=0)
        delta = jnp.sum(d2.T[64:] * ot_ref[pl.ds(i, 1)].reshape(64, 256), axis=0, keepdims=True)
        d2 = d2.astype(BF16)
        kv = slot_keys(kv_ref, slot)
        p = jnp.exp(dot_nt(kv, q2) - lse_ref[pl.ds(i, 1)].reshape(1, 256))
        ds = (p * (dot_nt(kv, d2) - delta)).astype(BF16)
        acc_ref[slot] += dot_nn(ds, q2) + dot_nn(p.astype(BF16), d2)
        dq = dot_nn(kvt_ref[slot], ds).T * (HDIM ** (-0.5))
        put_block(dq_ref, i, base, jnp.where(lane < 64, dq[:128], pltpu.roll(dq[128:], 64, 1)))
        return carry

    lax.fori_loop(0, 12, step, 0)
    for slot in range(2):
        dkv_ref[:, 256 * slot : 256 * slot + 256, :] = (
            acc_ref[slot].reshape(-1, 256, 128).astype(dkv_ref.dtype)
        )


def cross_probs(kc, q, bias, lane, e):
    qm = jnp.where((lane < 64) == (e == 0), q, jnp.zeros_like(q))
    s = jnp.where(bias > 0.0, dot_tt(kc, qm) * (HDIM ** (-0.5)), NEG)
    p = jnp.exp(s - jnp.max(s, axis=0, keepdims=True))
    return p / jnp.sum(p, axis=0, keepdims=True), qm


def cross_kernel(q_ref, kc_ref, vc_ref, bias_ref, o_ref):
    q = q_ref[...].reshape(256, 128)
    lane = lanes((256, 128))
    bias = bias_ref[...]
    outs = []
    for e in range(2):
        p, _ = cross_probs(kc_ref[...], q, bias, lane, e)
        outs.append(dot_tt(p.astype(BF16), vc_ref[...]))
    o_ref[...] = jnp.where(lane < 64, outs[0], outs[1]).reshape(4, 1, 64, 128)


def cross_back_kernel(q_ref, kc_ref, vc_ref, bias_ref, do_ref, dq_ref, dk_ref, dv_ref):
    q = q_ref[...].reshape(256, 128)
    d = do_ref[...].reshape(256, 128)
    lane = lanes((256, 128))
    bias = bias_ref[...]
    kc, vc = kc_ref[...], vc_ref[...]
    dqs, dk, dv = [], 0.0, 0.0
    for e in range(2):
        p, qm = cross_probs(kc, q, bias, lane, e)
        dm = jnp.where((lane < 64) == (e == 0), d, jnp.zeros_like(d))
        dp = dot_tt(vc, dm)
        dt = (p * (dp - jnp.sum(p * dp, axis=0, keepdims=True))).astype(BF16)
        dqs.append(dot_tt(dt, kc))
        dk = dk + dot_tt(qm, dt)
        dv = dv + dot_tt(dm, p.astype(BF16))
    dq = jnp.where(lane < 64, dqs[0], dqs[1]) * (HDIM ** (-0.5))
    dq_ref[...] = dq.reshape(4, 1, 64, 128)
    dk_ref[...] = dk * (HDIM ** (-0.5))
    dv_ref[...] = dv


def call(kernel, outs, *args, scratch=(), flops=0, grant=16):
    size = sum(math.prod(a.shape) * a.dtype.itemsize for a in (*args, *outs))
    spec = pl.BlockSpec(memory_space=pltpu.VMEM)
    return pl.pallas_call(
        kernel,
        out_shape=outs,
        in_specs=[spec] * len(args),
        out_specs=[spec] * len(outs),
        scratch_shapes=list(scratch),
        compiler_params=pltpu.CompilerParams(vmem_limit_bytes=grant << 20),
        cost_estimate=pl.CostEstimate(flops=flops, bytes_accessed=size, transcendentals=flops // 256),
    )(*args)


def cross_call(kernel, outs, specs, *args):
    token = pl.BlockSpec((4, 1, 64, 128), lambda c, h: (0, c, 0, h))
    bias = pl.BlockSpec((256, 1), lambda c, h: (c, 0))
    back = pl.BlockSpec((128, 256), lambda c, h: (h, c))
    kinds = {"t": token, "b": bias, "o": back}
    return pl.pallas_call(
        kernel,
        grid=(2, 3),
        out_shape=outs,
        in_specs=[kinds[c] for c in specs[0]],
        out_specs=[kinds[c] for c in specs[1]],
        compiler_params=pltpu.CompilerParams(vmem_limit_bytes=16 << 20),
        cost_estimate=pl.CostEstimate(
            flops=12 * len(args) * 256 * 256 * 128, bytes_accessed=4 << 20, transcendentals=12 << 16
        ),
    )(*args)


def product_kernel(left_ref, right_ref, out_ref):
    term = dot_nt(left_ref[...], right_ref[...])

    @pl.when(pl.program_id(0) == 0)
    def _():
        out_ref[...] = term

    @pl.when(pl.program_id(0) > 0)
    def _():
        out_ref[...] += term


def product(left, right):
    (rows, deep), (columns, _) = left.shape, right.shape
    return pl.pallas_call(
        product_kernel,
        grid=(deep // 512,),
        out_shape=shaped((rows, columns)),
        in_specs=[pl.BlockSpec((rows, 512), lambda k: (0, k)), pl.BlockSpec((columns, 512), lambda k: (0, k))],
        out_specs=pl.BlockSpec((rows, columns), lambda k: (0, 0)),
        compiler_params=pltpu.CompilerParams(vmem_limit_bytes=20 << 20),
        cost_estimate=pl.CostEstimate(
            flops=2 * rows * columns * deep, bytes_accessed=2 * deep * (rows + columns), transcendentals=0
        ),
    )(left, right)


def shaped(shape, dtype=F32):
    return jax.ShapeDtypeStruct(shape, dtype)


def rms_norm(tensor, gain):
    return tensor * lax.rsqrt(jnp.mean(tensor * tensor, axis=-1, keepdims=True) + EPS) * gain


def rotary_lanes():
    parts = ((0, 16), (1, 24), (2, 24))
    freqs = [[], [], []]
    signs = []
    for which, size in parts:
        for upper in range(2):
            for i in range(size // 2):
                for p in range(3):
                    freqs[p].append(math.exp(-math.log(THETA) * 2.0 * i / size) if p == which else 0.0)
                signs.append(1.0 if upper else -1.0)
    return [jnp.array(f, F32) for f in freqs], jnp.array(signs, F32)


def mm(a, b):
    return jnp.dot(a, b, preferred_element_type=F32)


def body(
    tokens,
    w_query,
    w_key,
    w_value,
    w_out,
    w_gate,
    w_up,
    w_down,
    w_cap_key,
    w_cap_value,
    w_mod,
    norm_gains,
    mix_coefs,
    caption,
    cap_len,
    cap_mask,
    timesteps,
    frame_pos,
    row_pos,
    col_pos,
    grad_out,
):
    clips, frames, rows_here, cols, width = tokens.shape
    local = frames * rows_here * cols
    group = lax.axis_size("y") * lax.axis_size("x")
    n_rows = lax.axis_size(ROW)
    n_far = lax.axis_size("far")
    n_all = group * n_rows
    me = lax.axis_index(TEAM)
    my_member = lax.axis_index(GROUP)
    heads_w = width // group
    ff_w = w_gate.shape[1] // group
    count = group * clips * local
    caps = caption.shape[1]
    share = width // n_all

    rows = w_query.shape[0]
    cap2 = caption.reshape(clips * caps, width)

    def by_columns(parts):
        cut = jnp.concatenate([w.reshape(rows, group, -1) for w in parts], axis=2)
        cut = lax.all_to_all(cut.transpose(1, 0, 2), TEAM, 0, 0)
        return cut.reshape(group * rows, -1)

    def in_order(gathered):
        full = gathered.reshape(n_far, RING // 2, 2, 2, 2, rows, -1).transpose(3, 2, 0, 1, 4, 5, 6)
        return full.reshape(width, -1)

    def cap_columns(weight):
        return lax.dot_general(weight, cap2, (((0,), (1,)), ((), ())), preferred_element_type=F32).astype(BF16)

    cut_qkv = by_columns([w_query, w_key, w_value])

    half_width = width // 2
    frequencies = jnp.exp(-math.log(THETA) * jnp.arange(half_width, dtype=F32) / half_width)
    phases = timesteps.astype(F32)[:, None] * frequencies[None, :]
    step_embed = jax.nn.silu(jnp.concatenate([jnp.cos(phases), jnp.sin(phases)], axis=1)).astype(BF16)
    mod_local = mm(step_embed, w_mod).astype(BF16).astype(F32)
    mod_cols = mod_local.shape[1]
    note = jnp.concatenate([mod_local.reshape(-1), frame_pos.astype(F32).reshape(-1), row_pos.astype(F32)])
    used = note.shape[0]
    note = jnp.pad(note, (0, -used % 512)).reshape(1, -1, 128)
    note = lax.all_to_all(jnp.broadcast_to(note, (n_all,) + note.shape[1:]), ALL, 0, 0)
    note, (w_gate, w_up) = beside(note, (w_gate, w_up))
    cut_gu = by_columns([w_gate, w_up])
    note = note.reshape(n_all, -1)
    x_own = tokens.reshape(clips, local, width)
    x_flat = x_own.astype(F32)
    x_group, _ = team_gather(x_own)
    w_qkv = in_order(group_gather(cut_qkv))
    tokens_c = clips * caps
    blank = jnp.zeros((rows, width - 2 * tokens_c), BF16)
    cap_rows = jnp.concatenate([cap_columns(w_cap_key), cap_columns(w_cap_value), blank], axis=1)
    side = group_gather(exchange(jnp.concatenate([w_out, cap_rows])))
    down_rows = exchange(w_down)
    mod_full = note[:, : clips * mod_cols].reshape(n_all, clips, mod_cols)
    mod_full = mod_full.transpose(1, 0, 2).reshape(clips, 4, width)
    scale_a, gate_a, scale_f, gate_f = (mod_full[:, i] for i in range(4))
    positions = note[:, clips * mod_cols : used].reshape(2, 2, n_far, RING // 2, 2, -1)
    here = [lax.axis_index(axis) for axis in ("core", "far", "z")]
    positions = lax.dynamic_slice(positions, (0, *here, 0, 0), (2, 1, 1, 1, 2, positions.shape[-1]))
    order = jnp.arange(group)
    chosen = (order[None, :] == (me ^ order)[:, None]).astype(F32)
    positions = jnp.sum(chosen[:, :, None] * positions.reshape(1, group, -1), axis=1)

    gains = norm_gains
    own_gains = lax.dynamic_slice(gains, (4, me * heads_w), (3, heads_w))
    own_gate = jnp.tanh(lax.dynamic_slice(mix_coefs, (0, me * heads_w), (1, heads_w)))

    full = (group, clips, frames, cols)
    frame_at = positions[:, :-1].reshape(group, clips, frames) + cap_len.astype(F32)[None, :, None]
    pos_a = jnp.broadcast_to(frame_at[..., None], full)
    pos_b = jnp.broadcast_to(positions[:, -1:, None, None], full)
    pos_e = jnp.broadcast_to(col_pos.astype(F32), full)
    (fa, fb, fe), sign = rotary_lanes()
    angle = (
        pos_a.reshape(count, 1) * fa + pos_b.reshape(count, 1) * fb + pos_e.reshape(count, 1) * fe
    )
    cosine = jnp.tile(jnp.cos(angle), (1, 2))
    sine = jnp.tile(jnp.sin(angle) * sign, (1, 2))

    def pre_piece(x_in, gain, scale_in):
        return rms_norm(x_in, gain) * (1.0 + scale_in[:, None, :])

    h_in = pre_piece(x_group.astype(F32), gains[0], scale_a).astype(BF16).reshape(count, width)
    h_in = lax.optimization_barrier(h_in)
    _, pre_back = jax.vjp(pre_piece, x_flat, gains[0], scale_a)
    qkv = mm(h_in, w_qkv)
    q_zero, k_zero = qkv[:, :heads_w], qkv[:, heads_w : 2 * heads_w]
    squares = jnp.stack([jnp.sum(q_zero * q_zero, axis=1), jnp.sum(k_zero * k_zero, axis=1)])
    rsq = lax.rsqrt(token_sum(squares) / width + EPS).T
    send, q_cap = call(
        send_kernel,
        [shaped((RING, 704, 128), BF16), shaped((count, heads_w), BF16)],
        qkv,
        rsq,
        own_gains,
        cosine,
        sine,
    )
    got, (side, cut_gu, down_rows, (above_g, below_g)) = beside(
        lax.all_to_all(send, PLANE, 0, 0), (side, cut_gu, down_rows, row_neighbours(grad_out))
    )
    w_gu = group_gather(cut_gu)
    kv_all = got
    if n_far > 1:
        kv_all = lax.all_gather(got, "far", axis=0, tiled=True)
    keys = kv_all.shape[0] * 256
    work = 12 * keys * 256 * 128 * 2
    o_pack, o_t, lse = call(
        self_kernel,
        [shaped((RING, 192, 128), BF16), shaped((12, 64, 256)), shaped((12, 1, 256))],
        kv_all,
        got,
        scratch=[pltpu.VMEM((2, 128, keys), BF16)],
        flops=2 * work,
        grant=24 if n_far == 1 else 56,
    )
    o_pack, side = beside(o_pack, side)
    o_back = lax.all_to_all(o_pack, PLANE, 0, 0)
    side = side.reshape(n_rows, -1, width)
    w_o = side[:, :rows].reshape(-1, width)
    k_pre_t = side[:, rows:, :tokens_c].reshape(-1, tokens_c)
    v_cap_t = side[:, rows:, tokens_c : 2 * tokens_c].reshape(-1, tokens_c)

    usable = (jnp.arange(caps)[None, :] < cap_len[:, None]) & (cap_mask > 0)
    bias = usable.astype(F32).reshape(clips * caps, 1)
    k_pre_t = k_pre_t.astype(F32)
    gain_cap = own_gains[2][:, None]
    r_cap = lax.rsqrt(team_sum(jnp.sum(k_pre_t * k_pre_t, axis=0, keepdims=True)) / width + EPS)
    k_cap_t = (k_pre_t * r_cap * gain_cap).astype(BF16)
    q_cap4 = q_cap.reshape(group, clips, local, heads_w)
    (out_cross,) = cross_call(
        cross_kernel, [shaped(q_cap4.shape)], ("toob", "t"), q_cap4, k_cap_t, v_cap_t, bias
    )
    o_back, out_cross = beside(o_back, out_cross)
    out_cross = out_cross.reshape(count, heads_w)
    (attn_mix,) = call(mix_kernel, [shaped((count, heads_w), BF16)], o_back, out_cross, own_gate)

    y_one, (w_gu, down_rows) = team_scatter(
        mm(attn_mix, w_o).reshape(group, clips, local, width), (w_gu, down_rows)
    )
    w_dn = group_gather(down_rows)

    def mid_piece(x_in, y_in, gain_two, gate_in, gain_three, scale_in):
        h_mid = x_in + jnp.tanh(gate_in)[:, None, :] * rms_norm(y_in, gain_two)
        return (h_mid, rms_norm(h_mid, gain_three) * (1.0 + scale_in[:, None, :]))

    (h_mid, f_in32), mid_back = jax.vjp(mid_piece, x_flat, y_one, gains[1], gate_a, gains[2], scale_f)
    f_in, w_gu = team_gather(f_in32.astype(BF16), in_order(w_gu))
    f_in = f_in.reshape(count, width)
    gate_up = mm(f_in, w_gu)

    def act_piece(gate_in, up_in):
        return jax.nn.silu(gate_in) * up_in

    hidden32, act_back = jax.vjp(act_piece, gate_up[:, :ff_w], gate_up[:, ff_w:])
    hidden = hidden32.astype(BF16)
    z_out, _ = team_scatter(mm(hidden, w_dn).reshape(group, clips, local, width))

    def end_piece(h_in_mid, z_in, gain_four, gate_in):
        return h_in_mid + jnp.tanh(gate_in)[:, None, :] * rms_norm(z_in, gain_four)

    y_all, end_back = jax.vjp(end_piece, h_mid, z_out, gains[3], gate_f)
    y_grid = y_all.reshape(tokens.shape)
    above, below = row_neighbours(y_grid.astype(BF16))
    g_center = grad_out.astype(F32)
    d_y = g_center + mix_coefs[1] * below_g.astype(F32) + mix_coefs[2] * above_g.astype(F32)
    d_h_end, d_z, d_g_four, d_gate_f = end_back(d_y.reshape(clips, local, width))
    d_z_all, _ = team_gather(d_z.astype(BF16))
    d_z_all = d_z_all.reshape(count, width)
    d_hidden = lax.dot_general(d_z_all, w_dn, (((1,), (1,)), ((), ())), preferred_element_type=F32)
    d_gu = jnp.concatenate([d.astype(BF16) for d in act_back(d_hidden)], axis=1)
    d_f_in = product(d_gu, w_gu)
    def term(left, right):
        return lax.dot_general(left, right, (((0,), (0,)), ((), ())), preferred_element_type=F32).astype(BF16)

    ff_rows = (w_down.shape[0] * group * (heads_w // 128), width // n_rows * (2 * ff_w // 128))
    (ff_terms,) = call(
        ff_kernel,
        [shaped((n_rows, sum(ff_rows), 128), BF16)],
        hidden,
        d_z_all,
        f_in,
        d_gu,
        flops=6 * count * width * ff_w,
        grant=32,
    )
    d_f_in, ff_terms = team_scatter(d_f_in.reshape(group, clips, local, width), ff_terms)
    ff_sum = group_scatter(ff_terms)
    d_x_mid, d_y_one, d_g_two, d_gate_a, d_g_three, d_scale_f = mid_back((d_h_end, d_f_in))
    d_y_group, _ = team_gather(d_y_one.astype(BF16))
    d_y_group = d_y_group.reshape(count, width)
    d_attn = lax.dot_general(d_y_group, w_o, (((1,), (1,)), ((), ())), preferred_element_type=F32)

    d_pack, d_cross = call(
        split_kernel, [shaped((RING, 192, 128), BF16), shaped((count, heads_w), BF16)], d_attn, own_gate
    )
    d_got = lax.all_to_all(d_pack, PLANE, 0, 0)
    d_mix_gate = jnp.sum(d_attn * out_cross, axis=0) * (1.0 - own_gate[0] * own_gate[0])
    d_q_cross, d_k_cap, d_v_cap = cross_call(
        cross_back_kernel,
        [shaped(q_cap4.shape), shaped((heads_w, clips * caps)), shaped((heads_w, clips * caps))],
        ("toobt", "too"),
        q_cap4,
        k_cap_t,
        v_cap_t,
        bias,
        d_cross.reshape(q_cap4.shape),
    )
    d_got, (d_q_cross, d_k_cap, d_v_cap) = beside(d_got, (d_q_cross, d_k_cap, d_v_cap))
    back_scratch = [pltpu.VMEM((2, keys, 128), F32), pltpu.VMEM((2, 128, keys), BF16)]
    if n_far == 1:
        (d_send,) = call(
            functools.partial(self_back_kernel, True),
            [shaped((RING, 704, 128), BF16)],
            kv_all,
            got,
            d_got,
            o_t,
            lse,
            scratch=back_scratch,
            flops=5 * work,
            grant=32 if n_far == 1 else 60,
        )
    else:
        d_kv, d_q = call(
            functools.partial(self_back_kernel, False),
            [shaped((kv_all.shape[0], 512, 128), BF16), shaped((RING, 192, 128), BF16)],
            kv_all,
            got,
            d_got,
            o_t,
            lse,
            scratch=back_scratch,
            flops=5 * work,
            grant=32 if n_far == 1 else 60,
        )
        d_kv = lax.psum_scatter(d_kv, "far", scatter_dimension=0, tiled=True)
        d_send = jnp.concatenate([d_kv, d_q], axis=1)
    d_send, (above, below) = beside(d_send, (above, below))
    above, below = above.astype(F32), below.astype(F32)
    output = (y_grid + mix_coefs[1] * above + mix_coefs[2] * below).astype(BF16)
    d_above = jnp.sum(g_center * above, axis=(0, 1, 2, 3))
    d_below = jnp.sum(g_center * below, axis=(0, 1, 2, 3))
    cap_dot = team_sum(jnp.sum(d_k_cap * gain_cap * k_pre_t, axis=0, keepdims=True))
    wide = heads_w // n_rows
    tile = width // n_rows
    cut = (2 * wide + 16) * (clips * caps // 128)
    (out_terms,) = call(
        out_kernel,
        [shaped((n_rows, cut + tile * (heads_w // 128), 128), BF16)],
        attn_mix,
        d_y_group,
        d_k_cap,
        d_v_cap,
        cap_dot,
        flops=2 * count * width * heads_w,
    )

    def spread(block):
        return lax.dynamic_update_slice(jnp.zeros((width,), F32), block, (me * heads_w,))

    def owners_sum(mods, rows_in):
        first = mods.reshape(clips, -1, mod_cols).transpose(1, 0, 2).reshape(-1, clips * mod_cols)
        first = jnp.pad(first, ((0, n_all - first.shape[0]), (0, 0)))
        other = lax.optimization_barrier(jnp.stack(rows_in))
        other = other.reshape(len(rows_in), n_all, share).transpose(1, 0, 2).reshape(n_all, -1)
        both = jnp.concatenate([first, other], axis=1)
        both = jnp.pad(both, ((0, 0), (0, -both.shape[1] % 128))).reshape(n_all, -1, 128)
        both = jnp.sum(lax.all_to_all(both, ALL, 0, 0), axis=0).reshape(-1)
        cut = clips * mod_cols
        return both[:cut].reshape(clips, mod_cols), both[cut : cut + len(rows_in) * share].reshape(-1, share)

    d_recv, (output, out_terms, ff_sum) = beside(
        lax.all_to_all(d_send, PLANE, 0, 0), (output, out_terms, ff_sum)
    )
    out_sum = group_scatter(out_terms)
    d_qn, d_kn, d_v = call(
        back_kernel,
        [shaped((count, heads_w)), shaped((count, heads_w)), shaped((count, heads_w), BF16)],
        d_recv,
        d_q_cross.reshape(count, heads_w),
        cosine,
        sine,
    )
    rq, rk = rsq[:, 0:1], rsq[:, 1:2]
    d_g_query = jnp.sum(d_qn * q_zero * rq, axis=0)
    d_g_key = jnp.sum(d_kn * k_zero * rk, axis=0)
    a_q, a_k = d_qn * own_gains[0], d_kn * own_gains[1]
    dots = token_sum(jnp.stack([jnp.sum(a_q * q_zero, axis=1), jnp.sum(a_k * k_zero, axis=1)])).T / width
    d_q_low = (rq * a_q - q_zero * (rq * rq * rq * dots[:, 0:1])).astype(BF16)
    d_k_low = (rk * a_k - k_zero * (rk * rk * rk * dots[:, 1:2])).astype(BF16)
    d_qkv = jnp.concatenate([d_q_low, d_k_low, d_v], axis=1)
    d_h_in = lax.dot_general(d_qkv, w_qkv, (((1,), (1,)), ((), ())), preferred_element_type=F32)
    sum_down = to_owner(from_chunks(ff_sum[None, : ff_rows[0]], w_down.shape[0] * group))
    d_h_in, (term_qkv, out_sum, sum_down) = team_scatter(
        d_h_in.reshape(group, clips, local, width), (term(h_in, d_qkv), out_sum, sum_down)
    )
    qkv_sum = group_scatter(term_qkv)
    d_x_pre, d_g_zero, d_scale_a = pre_back(d_h_in)
    grad_tokens = (d_x_pre + d_x_mid).reshape(tokens.shape)

    d_mod, sums = owners_sum(
        jnp.concatenate([d_scale_a, d_gate_a, d_scale_f, d_gate_f], axis=1),
        [
            d_g_zero,
            d_g_two,
            d_g_three,
            d_g_four,
            spread(d_g_query),
            spread(d_g_key),
            spread(d_mix_gate),
            d_above,
            d_below,
        ],
    )
    d_w_mod = lax.dot_general(
        step_embed, d_mod.astype(BF16), (((0,), (0,)), ((), ())), preferred_element_type=F32
    )
    cap_sum = from_chunks(out_sum[None, :cut].astype(F32), 2 * wide + 16)
    d_k_own, d_v_own, cap_dot = cap_sum[:wide], cap_sum[wide : 2 * wide], cap_sum[2 * wide : 2 * wide + 1]
    k_own = lax.dynamic_slice(k_pre_t, (my_member * wide, 0), (wide, clips * caps))
    g_own = lax.dynamic_slice(gain_cap, (my_member * wide, 0), (wide, 1))
    d_g_cap = exchange(jnp.sum(d_k_own * k_own * r_cap, axis=1)[None])
    d_k_zero_cap = r_cap * g_own * d_k_own - k_own * (r_cap * r_cap * r_cap * cap_dot / width)
    d_caps = exchange(jnp.concatenate([d_k_zero_cap, d_v_own]).astype(BF16))
    sum_gu = exchange(ff_sum[ff_rows[0] :])
    sum_out = to_owner(from_chunks(out_sum[None, cut:], tile))
    d_w_mod, qkv_sum = beside(d_w_mod, exchange(qkv_sum))
    qkv_sum, sum_gu, sum_out, d_caps, d_g_cap = lax.optimization_barrier(
        (qkv_sum, sum_gu, sum_out, d_caps, d_g_cap)
    )
    qkv_sum = qkv_sum.astype(F32)
    sum_gate, sum_up = jnp.split(sum_gu, 2)

    def result(block):
        return from_chunks(block[None], tile).astype(F32)

    def cap_weight(d):
        return lax.dot_general(cap2, d, (((0,), (1,)), ((), ())), preferred_element_type=F32)

    d_w_cap_key = cap_weight(d_caps[:wide])
    d_w_cap_value = cap_weight(d_caps[wide:])
    d_gains = jnp.concatenate([sums[:6], d_g_cap], axis=0)
    d_mixes = sums[6:]

    return (
        output,
        grad_tokens,
        qkv_sum[:, :heads_w],
        qkv_sum[:, heads_w : 2 * heads_w],
        qkv_sum[:, 2 * heads_w :],
        sum_out.astype(F32),
        result(sum_gate),
        result(sum_up),
        sum_down.astype(F32),
        d_w_cap_key,
        d_w_cap_value,
        d_w_mod,
        d_gains,
        d_mixes,
    )


def solution(mesh):
    frame, row = mesh.shape["frame"], mesh.shape["row"]
    fine = Mesh(mesh.devices.reshape(frame // 2, 2, row // RING, RING // 2, 2), ALL)
    grid = P(None, FRAME, ROW, None, None)
    rows, columns = P(ALL, None), P(None, ALL)
    tile = P(ROW, FRAME)
    return jax.shard_map(
        body,
        mesh=fine,
        in_specs=(
            (grid,)
            + (rows,) * 7
            + (columns,) * 3
            + (P(),) * 6
            + (P(None, FRAME), P(ROW), P(), grid)
        ),
        out_specs=(grid, grid) + (tile,) * 7 + (columns,) * 5,
        check_vma=False,
    )
```

```python
import functools
import itertools
import math

import jax
import jax.numpy as jnp
from jax import lax
from jax.experimental import pallas as pl
from jax.experimental.pallas import tpu as pltpu
from jax.sharding import Mesh
from jax.sharding import PartitionSpec as P

HDIM = 64
EPS = 1e-05
THETA = 10000.0
NEG = -1000000000.0
F32 = jnp.float32
BF16 = jnp.bfloat16
RING = 8
TEAM = ("y", "x")
PLANE = ("z", "core")
GROUP = ("far", "z", "core")
FRAME = ("y", "core")
ROW = ("far", "z", "x")
ALL = ("y", "core", "far", "z", "x")


def swap(value, bits):
    return lax.ppermute(value, TEAM, [(i, i ^ bits) for i in range(4)])


def team_sum(value):
    one, two, three = (swap(value, k) for k in (1, 2, 3))
    return (value + one) + (two + three)


def token_sum(value):
    blocks = value.reshape(value.shape[0], 4, -1)
    one, two, three = (swap(blocks, k) for k in (1, 2, 3))
    pairs = one.reshape(value.shape[0], 2, 2, -1)[:, :, ::-1].reshape(blocks.shape)
    halves = jnp.concatenate([two[:, 2:], two[:, :2]], axis=1)
    return ((blocks + pairs) + (halves + three[:, ::-1])).reshape(value.shape)


def beside(moved, work):
    return (moved, None) if work is None else lax.optimization_barrier((moved, work))


def team_gather(value, work=None):
    others, work = beside([swap(value, k) for k in (3, 2, 1)], work)
    return jnp.stack([value, others[2], others[1], others[0]]), work


def team_scatter(terms, work=None):
    low = terms.astype(BF16)
    others, work = beside([swap(low[k], k) for k in (3, 2, 1)], work)
    return terms[0] + sum(other.astype(F32) for other in others), work


def relocate(block, target):
    sizes = [lax.axis_size(axis) for axis in ALL]
    pairs = []
    for index, where in enumerate(itertools.product(*(range(size) for size in sizes))):
        to = 0
        for size, at in zip(sizes, target(*where)):
            to = to * size + at
        if to != index:
            pairs.append((index, to))
    here = [lax.axis_index(axis) for axis in ALL]
    stays = functools.reduce(lambda a, b: a & b, [a == b for a, b in zip(here, target(*here))])
    return stays, block, lax.ppermute(block, ALL, pairs)


def settled(moved):
    stays, block, received = moved
    return jnp.where(stays, block, received)


def exchange(block):
    return relocate(block, lambda y, core, far, z, x: (y, x, far, z, core))


def piece_member(f, part, parts):
    if parts > 2:
        return f * parts + part
    core = f // 2
    return (f % 2 * 2 + (part ^ core)) * 2 + core


def to_owner(block):
    if lax.axis_size("far") == 1:
        return relocate(block, lambda y, core, far, z, x: (core, z // 2, 0, 2 * y + x, z % 2 ^ core))
    return relocate(block, lambda y, core, far, z, x: (far // 2, far % 2, 2 * y + x, z, core))


def group_gather(block):
    return lax.all_gather(block, GROUP, axis=0, tiled=True)


def group_scatter(terms):
    terms = terms.reshape(-1, terms.shape[-1])
    return lax.psum_scatter(terms, GROUP, scatter_dimension=0, tiled=True)


def row_neighbours(block):
    count = lax.axis_size(ROW)
    forward = [(i, i + 1) for i in range(count - 1)]
    above = lax.ppermute(block, ROW, forward)
    below = lax.ppermute(block, ROW, [(b, a) for a, b in forward])
    return above, below


def to_chunks(value, size):
    blocks, rows, columns = value.shape
    value = value.reshape(blocks, rows, columns // size, size).transpose(0, 2, 1, 3)
    return value.reshape(blocks, -1, size)


def from_chunks(value, rows):
    blocks, _, size = value.shape
    return value.reshape(blocks, -1, rows, size).transpose(0, 2, 1, 3).reshape(blocks * rows, -1)


def owners(pair):
    j, k = divmod(pair, 3)
    if k == 1:
        return [(2 * j, 1, (0, 1)), (2 * j + 1, 1, (2, 3))]
    return [(2 * j + k // 2, 0, (0, 1, 2, 3))]


def q_rows(slot, chunk):
    if slot == 0:
        return 64 * (chunk % 2), chunk // 2
    return 128, chunk % 2


def lanes(shape):
    return lax.broadcasted_iota(jnp.int32, shape, len(shape) - 1)


def half(value, source, target):
    return value if source == target else pltpu.roll(value, 64, 1)


def partner(value):
    lane = lanes(value.shape) % 64
    up8, dn8 = pltpu.roll(value, 120, 1), pltpu.roll(value, 8, 1)
    up12, dn12 = pltpu.roll(value, 116, 1), pltpu.roll(value, 12, 1)
    lower = ((lane >= 16) & (lane < 28)) | ((lane >= 40) & (lane < 52))
    return jnp.where(lane < 8, up8, jnp.where(lane < 16, dn8, jnp.where(lower, up12, dn12)))


def store_queries(out_ref, base, tile, clip, pair_of_heads):
    lane = lanes((64, 128))
    for e in range(2):
        pair = 6 * clip + 2 * pair_of_heads + e
        chunk = [tile[128 * k + 64 * clip : 128 * k + 64 * clip + 64] for k in range(4)]
        for dev, slot, chunks in owners(pair):
            for lo in chunks[: len(chunks) // 2]:
                row, _ = q_rows(slot, lo)
                hi = lo + len(chunks) // 2
                value = jnp.where(lane < 64, half(chunk[lo], e, 0), half(chunk[hi], e, 1))
                out_ref[dev, base + row : base + row + 64, :] = value.astype(out_ref.dtype)


def load_queries(in_ref, base, clip, pair_of_heads):
    lane = lanes((64, 128))
    parts = []
    for e in range(2):
        pair = 6 * clip + 2 * pair_of_heads + e
        found = [None] * 4
        for dev, slot, chunks in owners(pair):
            for c in chunks:
                row, source = q_rows(slot, c)
                value = in_ref[dev, base + row : base + row + 64, :].astype(F32)
                found[c] = half(value, source, e)
        parts.append(found)
    return [jnp.where(lane < 64, a, b) for a, b in zip(*parts)]


def send_kernel(qkv_ref, rs_ref, gain_ref, cos_ref, sin_ref, send_ref, qc_ref):
    lane = lanes((64, 128))
    cosine, sine = cos_ref[...], sin_ref[...]
    rq, rk = rs_ref[:, 0:1], rs_ref[:, 1:2]
    width = 384
    for hp in range(3):
        cut = slice(128 * hp, 128 * hp + 128)
        qn = qkv_ref[:, cut] * rq * gain_ref[0:1, cut]
        kn = qkv_ref[:, width + 128 * hp : width + 128 * hp + 128] * rk * gain_ref[1:2, cut]
        vv = qkv_ref[:, 2 * width + 128 * hp : 2 * width + 128 * hp + 128]
        qc_ref[:, cut] = qn.astype(BF16)
        qr = qn * cosine + partner(qn) * sine
        kr = kn * cosine + partner(kn) * sine
        for clip in range(2):
            store_queries(send_ref, 512, qr, clip, hp)
            for e in range(2):
                for k in range(4):
                    row = 128 * k + 64 * clip
                    kc, vc = kr[row : row + 64], vv[row : row + 64]
                    value = jnp.where(lane < 64, half(kc, e, 0), half(vc, e, 1)).astype(BF16)
                    for dev, slot, _ in owners(6 * clip + 2 * hp + e):
                        at = 256 * slot + 64 * k
                        send_ref[dev, at : at + 64, :] = value


def mix_kernel(o_ref, oc_ref, gate_ref, attn_ref):
    for hp in range(3):
        cut = slice(128 * hp, 128 * hp + 128)
        gate = gate_ref[0:1, cut]
        for clip in range(2):
            for k, chunk in enumerate(load_queries(o_ref, 0, clip, hp)):
                rows = slice(128 * k + 64 * clip, 128 * k + 64 * clip + 64)
                attn_ref[rows, cut] = (chunk + gate * oc_ref[rows, cut]).astype(BF16)


def split_kernel(d_ref, gate_ref, do_ref, doc_ref):
    for hp in range(3):
        cut = slice(128 * hp, 128 * hp + 128)
        tile = d_ref[:, cut]
        doc_ref[:, cut] = (tile * gate_ref[0:1, cut]).astype(BF16)
        for clip in range(2):
            store_queries(do_ref, 0, tile, clip, hp)


def back_kernel(d_ref, dqc_ref, cos_ref, sin_ref, dqn_ref, dkn_ref, dv_ref):
    lane = lanes((64, 128))
    for hp in range(3):
        cut = slice(128 * hp, 128 * hp + 128)
        for clip in range(2):
            queries = load_queries(d_ref, 512, clip, hp)
            for k in range(4):
                rows = slice(128 * k + 64 * clip, 128 * k + 64 * clip + 64)
                cosine, sine = cos_ref[rows, :], sin_ref[rows, :]
                heads = []
                for e in range(2):
                    total = None
                    for dev, slot, _ in owners(6 * clip + 2 * hp + e):
                        at = 256 * slot + 64 * k
                        term = d_ref[dev, at : at + 64, :].astype(F32)
                        total = term if total is None else total + term
                    heads.append(total)
                dk = jnp.where(lane < 64, heads[0], half(heads[1], 0, 1))
                dv = jnp.where(lane < 64, half(heads[0], 1, 0), heads[1])
                dq = queries[k]
                dqn_ref[rows, cut] = dq * cosine + partner(dq * sine) + dqc_ref[rows, cut]
                dkn_ref[rows, cut] = dk * cosine + partner(dk * sine)
                dv_ref[rows, cut] = dv.astype(BF16)


def dot_nt(a, b):
    return lax.dot_general(a, b, (((1,), (1,)), ((), ())), preferred_element_type=F32)


def dot_nn(a, b):
    return lax.dot_general(a, b, (((1,), (0,)), ((), ())), preferred_element_type=F32)


def turned(value):
    return value.astype(F32).T.astype(BF16)


def ff_kernel(hidden_ref, dz_ref, f_in_ref, dgu_ref, out_ref):
    n_rows = out_ref.shape[0]
    part = n_rows // 4
    left = turned(hidden_ref[...])
    tile = left.shape[0] // part

    for c in range(4):
        block = dot_nn(left, dz_ref[:, 384 * c : 384 * c + 384]).astype(BF16)
        for j in range(3):
            for h in range(part):
                out_ref[piece_member(c, h, part), tile * j : tile * j + tile, :] = block[
                    tile * h : tile * h + tile, 128 * j : 128 * j + 128
                ]
    base = 3 * tile
    left_f = turned(f_in_ref[...])
    tile_f = left_f.shape[0] // n_rows

    def gate_up(j, carry):
        block = dot_nn(left_f, dgu_ref[:, pl.ds(pl.multiple_of(256 * j, 128), 256)]).astype(BF16)
        for e in range(2):
            at = pl.multiple_of(base + tile_f * (2 * j + e), 16)
            for r in range(n_rows):
                out_ref[r, pl.ds(at, tile_f), :] = block[
                    tile_f * r : tile_f * r + tile_f, 128 * e : 128 * e + 128
                ]
        return carry

    lax.fori_loop(0, dgu_ref.shape[1] // 256, gate_up, 0)


def out_kernel(attn_ref, dy_ref, dk_ref, dv_ref, dot_ref, out_ref):
    n_rows = out_ref.shape[0]
    wide = dk_ref.shape[0] // n_rows
    tall = 2 * wide + 16
    chunks = dk_ref.shape[1] // 128
    for r in range(n_rows):
        for j in range(chunks):
            cut = slice(128 * j, 128 * j + 128)
            block = jnp.concatenate(
                [
                    dk_ref[wide * r : wide * r + wide, cut],
                    dv_ref[wide * r : wide * r + wide, cut],
                    jnp.broadcast_to(dot_ref[:, cut], (16, 128)),
                ]
            )
            out_ref[r, tall * j : tall * j + tall, :] = block.astype(BF16)
    base = tall * chunks
    left = turned(attn_ref[...])
    tile = left.shape[0] // (n_rows // 4)
    for f in range(4):
        block = dot_nn(left, dy_ref[:, 384 * f : 384 * f + 384]).astype(BF16)
        for part in range(n_rows // 4):
            member = piece_member(f, part, n_rows // 4)
            for j in range(3):
                out_ref[member, base + tile * j : base + tile * j + tile, :] = block[
                    tile * part : tile * part + tile, 128 * j : 128 * j + 128
                ]


def dot_tt(a, b):
    return lax.dot_general(a, b, (((0,), (1,)), ((), ())), preferred_element_type=F32)


def block_of(ref, i, base):
    at = pl.multiple_of(base + 64 * (i // 4), 64)
    return ref[pl.ds(2 * (i % 4), 2), pl.ds(at, 64), :].reshape(128, 128).astype(F32)


def put_block(ref, i, base, value):
    at = pl.multiple_of(base + 64 * (i // 4), 64)
    ref[pl.ds(2 * (i % 4), 2), pl.ds(at, 64), :] = value.reshape(2, 64, 128).astype(ref.dtype)


def slot_keys(kv_ref, slot):
    return kv_ref[:, pl.ds(pl.multiple_of(256 * slot, 256), 256), :].reshape(-1, 128)


def self_kernel(kv_ref, q_ref, o_ref, ot_ref, lse_ref, kvt_ref):
    lane = lanes((128, 128))
    for slot in range(2):
        kvt_ref[slot] = turned(slot_keys(kv_ref, slot))

    def step(i, carry):
        slot = i // 8
        q = block_of(q_ref, i, 512) * (HDIM ** (-0.5))
        qa = jnp.where(lane < 64, q, 0.0)
        qb = jnp.where(lane < 64, pltpu.roll(q, 64, 1), 0.0)
        q2 = jnp.concatenate([qa, qb], axis=0).astype(BF16)
        s = dot_nt(slot_keys(kv_ref, slot), q2)
        top = jnp.max(s, axis=0, keepdims=True)
        p = jnp.exp(s - top)
        total = jnp.sum(p, axis=0, keepdims=True)
        ot = dot_nn(kvt_ref[slot], p.astype(BF16)) / total
        o = ot.T
        put_block(o_ref, i, 0, jnp.where(lane < 64, pltpu.roll(o[:128], 64, 1), o[128:]))
        ot_ref[pl.ds(i, 1)] = ot[64:].reshape(1, 64, 256)
        lse_ref[pl.ds(i, 1)] = (top + jnp.log(total)).reshape(1, 1, 256)
        return carry

    lax.fori_loop(0, 12, step, 0)


def self_back_kernel(merged, kv_ref, q_ref, do_ref, ot_ref, lse_ref, *rest):
    if merged:
        dkv_ref, acc_ref, kvt_ref = rest
        dq_ref, base = dkv_ref, 512
    else:
        dkv_ref, dq_ref, acc_ref, kvt_ref = rest
        base = 0
    lane = lanes((128, 128))
    for slot in range(2):
        kvt_ref[slot] = turned(slot_keys(kv_ref, slot))
    acc_ref[...] = jnp.zeros_like(acc_ref)

    def step(i, carry):
        slot = i // 8
        q = block_of(q_ref, i, 512) * (HDIM ** (-0.5))
        d = block_of(do_ref, i, 0)
        qa = jnp.where(lane < 64, q, 0.0)
        qb = jnp.where(lane < 64, pltpu.roll(q, 64, 1), 0.0)
        q2 = jnp.concatenate([qa, qb], axis=0).astype(BF16)
        da = jnp.where(lane < 64, 0.0, pltpu.roll(d, 64, 1))
        db = jnp.where(lane < 64, 0.0, d)
        d2 = jnp.concatenate([da, db], axis=0)
        delta = jnp.sum(d2.T[64:] * ot_ref[pl.ds(i, 1)].reshape(64, 256), axis=0, keepdims=True)
        d2 = d2.astype(BF16)
        kv = slot_keys(kv_ref, slot)
        p = jnp.exp(dot_nt(kv, q2) - lse_ref[pl.ds(i, 1)].reshape(1, 256))
        ds = (p * (dot_nt(kv, d2) - delta)).astype(BF16)
        acc_ref[slot] += dot_nn(ds, q2) + dot_nn(p.astype(BF16), d2)
        dq = dot_nn(kvt_ref[slot], ds).T * (HDIM ** (-0.5))
        put_block(dq_ref, i, base, jnp.where(lane < 64, dq[:128], pltpu.roll(dq[128:], 64, 1)))
        return carry

    lax.fori_loop(0, 12, step, 0)
    for slot in range(2):
        dkv_ref[:, 256 * slot : 256 * slot + 256, :] = (
            acc_ref[slot].reshape(-1, 256, 128).astype(dkv_ref.dtype)
        )


def cross_probs(kc, q, bias, lane, e):
    qm = jnp.where((lane < 64) == (e == 0), q, jnp.zeros_like(q))
    s = jnp.where(bias > 0.0, dot_tt(kc, qm) * (HDIM ** (-0.5)), NEG)
    p = jnp.exp(s - jnp.max(s, axis=0, keepdims=True))
    return p / jnp.sum(p, axis=0, keepdims=True), qm


def cross_kernel(q_ref, kc_ref, vc_ref, bias_ref, o_ref):
    q = q_ref[...].reshape(256, 128)
    lane = lanes((256, 128))
    bias = bias_ref[...]
    outs = []
    for e in range(2):
        p, _ = cross_probs(kc_ref[...], q, bias, lane, e)
        outs.append(dot_tt(p.astype(BF16), vc_ref[...]))
    o_ref[...] = jnp.where(lane < 64, outs[0], outs[1]).reshape(4, 1, 64, 128)


def cross_back_kernel(q_ref, kc_ref, vc_ref, bias_ref, do_ref, dq_ref, dk_ref, dv_ref):
    q = q_ref[...].reshape(256, 128)
    d = do_ref[...].reshape(256, 128)
    lane = lanes((256, 128))
    bias = bias_ref[...]
    kc, vc = kc_ref[...], vc_ref[...]
    dqs, dk, dv = [], 0.0, 0.0
    for e in range(2):
        p, qm = cross_probs(kc, q, bias, lane, e)
        dm = jnp.where((lane < 64) == (e == 0), d, jnp.zeros_like(d))
        dp = dot_tt(vc, dm)
        dt = (p * (dp - jnp.sum(p * dp, axis=0, keepdims=True))).astype(BF16)
        dqs.append(dot_tt(dt, kc))
        dk = dk + dot_tt(qm, dt)
        dv = dv + dot_tt(dm, p.astype(BF16))
    dq = jnp.where(lane < 64, dqs[0], dqs[1]) * (HDIM ** (-0.5))
    dq_ref[...] = dq.reshape(4, 1, 64, 128)
    dk_ref[...] = dk * (HDIM ** (-0.5))
    dv_ref[...] = dv


def call(kernel, outs, *args, scratch=(), flops=0, grant=16):
    size = sum(math.prod(a.shape) * a.dtype.itemsize for a in (*args, *outs))
    spec = pl.BlockSpec(memory_space=pltpu.VMEM)
    return pl.pallas_call(
        kernel,
        out_shape=outs,
        in_specs=[spec] * len(args),
        out_specs=[spec] * len(outs),
        scratch_shapes=list(scratch),
        compiler_params=pltpu.CompilerParams(vmem_limit_bytes=grant << 20),
        cost_estimate=pl.CostEstimate(flops=flops, bytes_accessed=size, transcendentals=flops // 256),
    )(*args)


def cross_call(kernel, outs, specs, *args):
    token = pl.BlockSpec((4, 1, 64, 128), lambda c, h: (0, c, 0, h))
    bias = pl.BlockSpec((256, 1), lambda c, h: (c, 0))
    back = pl.BlockSpec((128, 256), lambda c, h: (h, c))
    kinds = {"t": token, "b": bias, "o": back}
    return pl.pallas_call(
        kernel,
        grid=(2, 3),
        out_shape=outs,
        in_specs=[kinds[c] for c in specs[0]],
        out_specs=[kinds[c] for c in specs[1]],
        compiler_params=pltpu.CompilerParams(vmem_limit_bytes=16 << 20),
        cost_estimate=pl.CostEstimate(
            flops=12 * len(args) * 256 * 256 * 128, bytes_accessed=4 << 20, transcendentals=12 << 16
        ),
    )(*args)


def feed_kernel(f_in_ref, w_gu_ref, w_dn_ref, gu_ref, hidden_ref, z_ref):
    half_w = hidden_ref.shape[1]
    z_ref[...] = jnp.zeros_like(z_ref)

    def step(j, carry):
        at = pl.multiple_of(256 * j, 256)
        up_at = pl.multiple_of(half_w + 256 * j, 256)
        gate = dot_nn(f_in_ref[...], w_gu_ref[:, pl.ds(at, 256)])
        up = dot_nn(f_in_ref[...], w_gu_ref[:, pl.ds(up_at, 256)])
        gu_ref[:, pl.ds(at, 256)] = gate
        gu_ref[:, pl.ds(up_at, 256)] = up
        hidden = (gate * jax.nn.sigmoid(gate) * up).astype(BF16)
        hidden_ref[:, pl.ds(at, 256)] = hidden
        z_ref[...] += dot_nn(hidden, w_dn_ref[pl.ds(at, 256), :])
        return carry

    lax.fori_loop(0, half_w // 256, step, 0)


def feed_back_kernel(dz_ref, w_dn_ref, gu_ref, w_gu_ref, dgu_ref, df_ref):
    half_w = w_dn_ref.shape[0]
    df_ref[...] = jnp.zeros_like(df_ref)

    def step(j, carry):
        at = pl.multiple_of(256 * j, 256)
        up_at = pl.multiple_of(half_w + 256 * j, 256)
        d_hidden = dot_nt(dz_ref[...], w_dn_ref[pl.ds(at, 256), :])
        gate, up = gu_ref[:, pl.ds(at, 256)], gu_ref[:, pl.ds(up_at, 256)]
        sigma = jax.nn.sigmoid(gate)
        d_gate = (d_hidden * up * (sigma * (1.0 + gate * (1.0 - sigma)))).astype(BF16)
        d_up = (d_hidden * (gate * sigma)).astype(BF16)
        dgu_ref[:, pl.ds(at, 256)] = d_gate
        dgu_ref[:, pl.ds(up_at, 256)] = d_up
        df_ref[...] += dot_nt(d_gate, w_gu_ref[:, pl.ds(at, 256)])
        df_ref[...] += dot_nt(d_up, w_gu_ref[:, pl.ds(up_at, 256)])
        return carry

    lax.fori_loop(0, half_w // 256, step, 0)


def shaped(shape, dtype=F32):
    return jax.ShapeDtypeStruct(shape, dtype)


def rms_norm(tensor, gain):
    return tensor * lax.rsqrt(jnp.mean(tensor * tensor, axis=-1, keepdims=True) + EPS) * gain


def rotary_lanes():
    parts = ((0, 16), (1, 24), (2, 24))
    freqs = [[], [], []]
    signs = []
    for which, size in parts:
        for upper in range(2):
            for i in range(size // 2):
                for p in range(3):
                    freqs[p].append(math.exp(-math.log(THETA) * 2.0 * i / size) if p == which else 0.0)
                signs.append(1.0 if upper else -1.0)
    return [jnp.array(f, F32) for f in freqs], jnp.array(signs, F32)


def mm(a, b):
    return jnp.dot(a, b, preferred_element_type=F32)


def body(
    tokens,
    w_query,
    w_key,
    w_value,
    w_out,
    w_gate,
    w_up,
    w_down,
    w_cap_key,
    w_cap_value,
    w_mod,
    norm_gains,
    mix_coefs,
    caption,
    cap_len,
    cap_mask,
    timesteps,
    frame_pos,
    row_pos,
    col_pos,
    grad_out,
):
    clips, frames, rows_here, cols, width = tokens.shape
    local = frames * rows_here * cols
    group = lax.axis_size("y") * lax.axis_size("x")
    n_rows = lax.axis_size(ROW)
    n_far = lax.axis_size("far")
    n_all = group * n_rows
    me = lax.axis_index(TEAM)
    my_member = lax.axis_index(GROUP)
    heads_w = width // group
    ff_w = w_gate.shape[1] // group
    count = group * clips * local
    caps = caption.shape[1]
    share = width // n_all

    rows = w_query.shape[0]
    cap2 = caption.reshape(clips * caps, width)

    def by_columns(parts):
        cut = jnp.concatenate([w.reshape(rows, group, -1) for w in parts], axis=2)
        cut = lax.all_to_all(cut.transpose(1, 0, 2), TEAM, 0, 0)
        return cut.reshape(group * rows, -1)

    def in_order(gathered):
        full = gathered.reshape(n_far, RING // 2, 2, 2, 2, rows, -1).transpose(3, 2, 0, 1, 4, 5, 6)
        return full.reshape(width, -1)

    def cap_columns(weight):
        return lax.dot_general(weight, cap2, (((0,), (1,)), ((), ())), preferred_element_type=F32).astype(BF16)

    cut_qkv = by_columns([w_query, w_key, w_value])

    half_width = width // 2
    frequencies = jnp.exp(-math.log(THETA) * jnp.arange(half_width, dtype=F32) / half_width)
    phases = timesteps.astype(F32)[:, None] * frequencies[None, :]
    step_embed = jax.nn.silu(jnp.concatenate([jnp.cos(phases), jnp.sin(phases)], axis=1)).astype(BF16)
    mod_local = mm(step_embed, w_mod).astype(BF16).astype(F32)
    mod_cols = mod_local.shape[1]
    note = jnp.concatenate([mod_local.reshape(-1), frame_pos.astype(F32).reshape(-1), row_pos.astype(F32)])
    used = note.shape[0]
    note = jnp.pad(note, (0, -used % 512)).reshape(1, -1, 128)
    note = lax.all_to_all(jnp.broadcast_to(note, (n_all,) + note.shape[1:]), ALL, 0, 0)
    note, (w_gate, w_up) = beside(note, (w_gate, w_up))
    cut_gu = by_columns([w_gate, w_up])
    note = note.reshape(n_all, -1)
    x_own = tokens.reshape(clips, local, width)
    x_flat = x_own.astype(F32)
    x_group, _ = team_gather(x_own)
    w_qkv = in_order(group_gather(cut_qkv))
    tokens_c = clips * caps
    blank = jnp.zeros((rows, width - 2 * tokens_c), BF16)
    cap_rows = jnp.concatenate([cap_columns(w_cap_key), cap_columns(w_cap_value), blank], axis=1)
    side = group_gather(settled(exchange(jnp.concatenate([w_out, cap_rows]))))
    down_rows = settled(exchange(w_down))
    mod_full = note[:, : clips * mod_cols].reshape(n_all, clips, mod_cols)
    mod_full = mod_full.transpose(1, 0, 2).reshape(clips, 4, width)
    scale_a, gate_a, scale_f, gate_f = (mod_full[:, i] for i in range(4))
    positions = note[:, clips * mod_cols : used].reshape(2, 2, n_far, RING // 2, 2, -1)
    here = [lax.axis_index(axis) for axis in ("core", "far", "z")]
    positions = lax.dynamic_slice(positions, (0, *here, 0, 0), (2, 1, 1, 1, 2, positions.shape[-1]))
    order = jnp.arange(group)
    chosen = (order[None, :] == (me ^ order)[:, None]).astype(F32)
    positions = jnp.sum(chosen[:, :, None] * positions.reshape(1, group, -1), axis=1)

    gains = norm_gains
    own_gains = lax.dynamic_slice(gains, (4, me * heads_w), (3, heads_w))
    own_gate = jnp.tanh(lax.dynamic_slice(mix_coefs, (0, me * heads_w), (1, heads_w)))

    full = (group, clips, frames, cols)
    frame_at = positions[:, :-1].reshape(group, clips, frames) + cap_len.astype(F32)[None, :, None]
    pos_a = jnp.broadcast_to(frame_at[..., None], full)
    pos_b = jnp.broadcast_to(positions[:, -1:, None, None], full)
    pos_e = jnp.broadcast_to(col_pos.astype(F32), full)
    (fa, fb, fe), sign = rotary_lanes()
    angle = (
        pos_a.reshape(count, 1) * fa + pos_b.reshape(count, 1) * fb + pos_e.reshape(count, 1) * fe
    )
    cosine = jnp.tile(jnp.cos(angle), (1, 2))
    sine = jnp.tile(jnp.sin(angle) * sign, (1, 2))

    def pre_piece(x_in, gain, scale_in):
        return rms_norm(x_in, gain) * (1.0 + scale_in[:, None, :])

    h_in = pre_piece(x_group.astype(F32), gains[0], scale_a).astype(BF16).reshape(count, width)
    h_in = lax.optimization_barrier(h_in)
    _, pre_back = jax.vjp(pre_piece, x_flat, gains[0], scale_a)
    qkv = mm(h_in, w_qkv)
    q_zero, k_zero = qkv[:, :heads_w], qkv[:, heads_w : 2 * heads_w]
    squares = jnp.stack([jnp.sum(q_zero * q_zero, axis=1), jnp.sum(k_zero * k_zero, axis=1)])
    rsq = lax.rsqrt(token_sum(squares) / width + EPS).T
    send, q_cap = call(
        send_kernel,
        [shaped((RING, 704, 128), BF16), shaped((count, heads_w), BF16)],
        qkv,
        rsq,
        own_gains,
        cosine,
        sine,
    )
    side = side.reshape(n_rows, -1, width)
    w_o = side[:, :rows].reshape(-1, width)
    k_pre_t = side[:, rows:, :tokens_c].reshape(-1, tokens_c)
    v_cap_t = side[:, rows:, tokens_c : 2 * tokens_c].reshape(-1, tokens_c)

    usable = (jnp.arange(caps)[None, :] < cap_len[:, None]) & (cap_mask > 0)
    bias = usable.astype(F32).reshape(clips * caps, 1)
    k_pre_t = k_pre_t.astype(F32)
    gain_cap = own_gains[2][:, None]
    r_cap = lax.rsqrt(team_sum(jnp.sum(k_pre_t * k_pre_t, axis=0, keepdims=True)) / width + EPS)
    k_cap_t = (k_pre_t * r_cap * gain_cap).astype(BF16)
    got, (k_pre_t, r_cap, k_cap_t, v_cap_t, w_o, cut_gu, down_rows, (above_g, below_g)) = beside(
        lax.all_to_all(send, PLANE, 0, 0),
        (k_pre_t, r_cap, k_cap_t, v_cap_t, w_o, cut_gu, down_rows, row_neighbours(grad_out)),
    )
    w_gu = group_gather(cut_gu)
    kv_all = got
    if n_far > 1:
        kv_all = lax.all_gather(got, "far", axis=0, tiled=True)
    keys = kv_all.shape[0] * 256
    work = 12 * keys * 256 * 128 * 2
    o_pack, o_t, lse = call(
        self_kernel,
        [shaped((RING, 192, 128), BF16), shaped((12, 64, 256)), shaped((12, 1, 256))],
        kv_all,
        got,
        scratch=[pltpu.VMEM((2, 128, keys), BF16)],
        flops=2 * work,
        grant=24 if n_far == 1 else 56,
    )
    o_back = lax.all_to_all(o_pack, PLANE, 0, 0)

    q_cap4 = q_cap.reshape(group, clips, local, heads_w)
    (out_cross,) = cross_call(
        cross_kernel, [shaped(q_cap4.shape)], ("toob", "t"), q_cap4, k_cap_t, v_cap_t, bias
    )
    o_back, out_cross = beside(o_back, out_cross)
    out_cross = out_cross.reshape(count, heads_w)
    (attn_mix,) = call(mix_kernel, [shaped((count, heads_w), BF16)], o_back, out_cross, own_gate)

    y_one, (w_gu, down_rows) = team_scatter(
        mm(attn_mix, w_o).reshape(group, clips, local, width), (w_gu, down_rows)
    )
    w_dn = group_gather(down_rows)

    def mid_piece(x_in, y_in, gain_two, gate_in, gain_three, scale_in):
        h_mid = x_in + jnp.tanh(gate_in)[:, None, :] * rms_norm(y_in, gain_two)
        return (h_mid, rms_norm(h_mid, gain_three) * (1.0 + scale_in[:, None, :]))

    (h_mid, f_in32), mid_back = jax.vjp(mid_piece, x_flat, y_one, gains[1], gate_a, gains[2], scale_f)
    f_in, w_gu = team_gather(f_in32.astype(BF16), in_order(w_gu))
    f_in = f_in.reshape(count, width)
    gate_up, hidden, z_terms = call(
        feed_kernel,
        [shaped((count, 2 * ff_w)), shaped((count, ff_w), BF16), shaped((count, width))],
        f_in,
        w_gu,
        w_dn,
        flops=6 * count * width * ff_w,
        grant=32,
    )
    z_out, _ = team_scatter(z_terms.reshape(group, clips, local, width))

    def end_piece(h_in_mid, z_in, gain_four, gate_in):
        return h_in_mid + jnp.tanh(gate_in)[:, None, :] * rms_norm(z_in, gain_four)

    y_all, end_back = jax.vjp(end_piece, h_mid, z_out, gains[3], gate_f)
    y_grid = y_all.reshape(tokens.shape)
    above, below = row_neighbours(y_grid.astype(BF16))
    g_center = grad_out.astype(F32)
    d_y = g_center + mix_coefs[1] * below_g.astype(F32) + mix_coefs[2] * above_g.astype(F32)
    d_h_end, d_z, d_g_four, d_gate_f = end_back(d_y.reshape(clips, local, width))
    d_z_all, _ = team_gather(d_z.astype(BF16))
    d_z_all = d_z_all.reshape(count, width)
    d_gu, d_f_in = call(
        feed_back_kernel,
        [shaped((count, 2 * ff_w), BF16), shaped((count, width))],
        d_z_all,
        w_dn,
        gate_up,
        w_gu,
        flops=6 * count * width * ff_w,
        grant=32,
    )

    def term(left, right):
        return lax.dot_general(left, right, (((0,), (0,)), ((), ())), preferred_element_type=F32).astype(BF16)

    ff_rows = (w_down.shape[0] * group * (heads_w // 128), width // n_rows * (2 * ff_w // 128))
    (ff_terms,) = call(
        ff_kernel,
        [shaped((n_rows, sum(ff_rows), 128), BF16)],
        hidden,
        d_z_all,
        f_in,
        d_gu,
        flops=6 * count * width * ff_w,
        grant=32,
    )
    d_f_in, ff_terms = team_scatter(d_f_in.reshape(group, clips, local, width), ff_terms)
    ff_sum = group_scatter(ff_terms)
    d_x_mid, d_y_one, d_g_two, d_gate_a, d_g_three, d_scale_f = mid_back((d_h_end, d_f_in))
    d_y_group, _ = team_gather(d_y_one.astype(BF16))
    d_y_group = d_y_group.reshape(count, width)
    d_attn = lax.dot_general(d_y_group, w_o, (((1,), (1,)), ((), ())), preferred_element_type=F32)

    d_pack, d_cross = call(
        split_kernel, [shaped((RING, 192, 128), BF16), shaped((count, heads_w), BF16)], d_attn, own_gate
    )
    d_got = lax.all_to_all(d_pack, PLANE, 0, 0)
    d_mix_gate = jnp.sum(d_attn * out_cross, axis=0) * (1.0 - own_gate[0] * own_gate[0])
    back_scratch = [pltpu.VMEM((2, keys, 128), F32), pltpu.VMEM((2, 128, keys), BF16)]
    if n_far == 1:
        (d_send,) = call(
            functools.partial(self_back_kernel, True),
            [shaped((RING, 704, 128), BF16)],
            kv_all,
            got,
            d_got,
            o_t,
            lse,
            scratch=back_scratch,
            flops=5 * work,
            grant=32 if n_far == 1 else 60,
        )
    else:
        d_kv, d_q = call(
            functools.partial(self_back_kernel, False),
            [shaped((kv_all.shape[0], 512, 128), BF16), shaped((RING, 192, 128), BF16)],
            kv_all,
            got,
            d_got,
            o_t,
            lse,
            scratch=back_scratch,
            flops=5 * work,
            grant=32 if n_far == 1 else 60,
        )
        d_kv = lax.psum_scatter(d_kv, "far", scatter_dimension=0, tiled=True)
        d_send = jnp.concatenate([d_kv, d_q], axis=1)
    d_send, (above, below, d_cross) = beside(d_send, (above, below, d_cross))
    d_q_cross, d_k_cap, d_v_cap = cross_call(
        cross_back_kernel,
        [shaped(q_cap4.shape), shaped((heads_w, clips * caps)), shaped((heads_w, clips * caps))],
        ("toobt", "too"),
        q_cap4,
        k_cap_t,
        v_cap_t,
        bias,
        d_cross.reshape(q_cap4.shape),
    )
    above, below = above.astype(F32), below.astype(F32)
    output = (y_grid + mix_coefs[1] * above + mix_coefs[2] * below).astype(BF16)
    d_above = jnp.sum(g_center * above, axis=(0, 1, 2, 3))
    d_below = jnp.sum(g_center * below, axis=(0, 1, 2, 3))
    cap_dot = team_sum(jnp.sum(d_k_cap * gain_cap * k_pre_t, axis=0, keepdims=True))
    wide = heads_w // n_rows
    tile = width // n_rows
    cut = (2 * wide + 16) * (clips * caps // 128)
    (out_terms,) = call(
        out_kernel,
        [shaped((n_rows, cut + tile * (heads_w // 128), 128), BF16)],
        attn_mix,
        d_y_group,
        d_k_cap,
        d_v_cap,
        cap_dot,
        flops=2 * count * width * heads_w,
    )

    def spread(block):
        return lax.dynamic_update_slice(jnp.zeros((width,), F32), block, (me * heads_w,))

    def owners_sum(mods, rows_in):
        first = mods.reshape(clips, -1, mod_cols).transpose(1, 0, 2).reshape(-1, clips * mod_cols)
        first = jnp.pad(first, ((0, n_all - first.shape[0]), (0, 0)))
        other = lax.optimization_barrier(jnp.stack(rows_in))
        other = other.reshape(len(rows_in), n_all, share).transpose(1, 0, 2).reshape(n_all, -1)
        both = jnp.concatenate([first, other], axis=1)
        both = jnp.pad(both, ((0, 0), (0, -both.shape[1] % 128))).reshape(n_all, -1, 128)
        both = jnp.sum(lax.all_to_all(both, ALL, 0, 0), axis=0).reshape(-1)
        cut = clips * mod_cols
        return both[:cut].reshape(clips, mod_cols), both[cut : cut + len(rows_in) * share].reshape(-1, share)

    d_recv, (output, out_terms, ff_sum, d_q_cross) = beside(
        lax.all_to_all(d_send, PLANE, 0, 0), (output, out_terms, ff_sum, d_q_cross)
    )
    out_sum = group_scatter(out_terms)
    d_qn, d_kn, d_v = call(
        back_kernel,
        [shaped((count, heads_w)), shaped((count, heads_w)), shaped((count, heads_w), BF16)],
        d_recv,
        d_q_cross.reshape(count, heads_w),
        cosine,
        sine,
    )
    rq, rk = rsq[:, 0:1], rsq[:, 1:2]
    d_g_query = jnp.sum(d_qn * q_zero * rq, axis=0)
    d_g_key = jnp.sum(d_kn * k_zero * rk, axis=0)
    a_q, a_k = d_qn * own_gains[0], d_kn * own_gains[1]
    dots = token_sum(jnp.stack([jnp.sum(a_q * q_zero, axis=1), jnp.sum(a_k * k_zero, axis=1)])).T / width
    d_q_low = (rq * a_q - q_zero * (rq * rq * rq * dots[:, 0:1])).astype(BF16)
    d_k_low = (rk * a_k - k_zero * (rk * rk * rk * dots[:, 1:2])).astype(BF16)
    d_qkv = jnp.concatenate([d_q_low, d_k_low, d_v], axis=1)
    d_h_in = lax.dot_general(d_qkv, w_qkv, (((1,), (1,)), ((), ())), preferred_element_type=F32)
    d_h_in, (term_qkv, out_sum) = team_scatter(
        d_h_in.reshape(group, clips, local, width), (term(h_in, d_qkv), out_sum)
    )
    qkv_sum = group_scatter(term_qkv)
    d_x_pre, d_g_zero, d_scale_a = pre_back(d_h_in)
    grad_tokens = (d_x_pre + d_x_mid).reshape(tokens.shape)
    d_g_zero, (ff_sum, out_sum) = beside(d_g_zero, (ff_sum, out_sum))

    d_mod, sums = owners_sum(
        jnp.concatenate([d_scale_a, d_gate_a, d_scale_f, d_gate_f], axis=1),
        [
            d_g_zero,
            d_g_two,
            d_g_three,
            d_g_four,
            spread(d_g_query),
            spread(d_g_key),
            spread(d_mix_gate),
            d_above,
            d_below,
        ],
    )
    cap_sum = from_chunks(out_sum[None, :cut].astype(F32), 2 * wide + 16)
    d_k_own, d_v_own, cap_dot = cap_sum[:wide], cap_sum[wide : 2 * wide], cap_sum[2 * wide : 2 * wide + 1]
    k_own = lax.dynamic_slice(k_pre_t, (my_member * wide, 0), (wide, clips * caps))
    g_own = lax.dynamic_slice(gain_cap, (my_member * wide, 0), (wide, 1))
    caps_gain = exchange(jnp.sum(d_k_own * k_own * r_cap, axis=1)[None])
    d_k_zero_cap = r_cap * g_own * d_k_own - k_own * (r_cap * r_cap * r_cap * cap_dot / width)
    moved = [
        caps_gain,
        exchange(jnp.concatenate([d_k_zero_cap, d_v_own]).astype(BF16)),
        exchange(ff_sum[ff_rows[0] :]),
    ]
    d_mod, received = beside(d_mod, [m[2] for m in moved])
    d_g_cap, d_caps, sum_gu = (settled((*m[:2], r)) for m, r in zip(moved, received))
    d_w_mod = lax.dot_general(
        step_embed, d_mod.astype(BF16), (((0,), (0,)), ((), ())), preferred_element_type=F32
    )
    sum_gate, sum_up = jnp.split(sum_gu, 2)

    def result(block):
        return from_chunks(block[None], tile).astype(F32)

    def cap_weight(d):
        return lax.dot_general(cap2, d, (((0,), (1,)), ((), ())), preferred_element_type=F32)

    d_w_cap_key = cap_weight(d_caps[:wide])
    d_w_cap_value = cap_weight(d_caps[wide:])
    d_gains = jnp.concatenate([sums[:6], d_g_cap], axis=0)
    mine = w_down.shape[0] * group
    owned = jnp.concatenate(
        [from_chunks(ff_sum[None, : ff_rows[0]], mine), from_chunks(out_sum[None, cut:], tile)]
    )
    ready = (
        result(sum_gate),
        result(sum_up),
        d_w_cap_key,
        d_w_cap_value,
        d_w_mod,
        d_gains,
        sums[6:],
    )
    owned, qkv_sum = beside(owned, qkv_sum)
    moved = to_owner(owned), exchange(qkv_sum)
    received, ready = beside([m[2] for m in moved], ready)
    owned, qkv_sum = (settled((*m[:2], r)).astype(F32) for m, r in zip(moved, received))
    gate_grad, up_grad, *ready = ready
    return (
        output,
        grad_tokens,
        qkv_sum[:, :heads_w],
        qkv_sum[:, heads_w : 2 * heads_w],
        qkv_sum[:, 2 * heads_w :],
        owned[mine:],
        gate_grad,
        up_grad,
        owned[:mine],
        *ready,
    )


def solution(mesh):
    frame, row = mesh.shape["frame"], mesh.shape["row"]
    fine = Mesh(mesh.devices.reshape(frame // 2, 2, row // RING, RING // 2, 2), ALL)
    grid = P(None, FRAME, ROW, None, None)
    rows, columns = P(ALL, None), P(None, ALL)
    tile = P(ROW, FRAME)
    return jax.shard_map(
        body,
        mesh=fine,
        in_specs=(
            (grid,)
            + (rows,) * 7
            + (columns,) * 3
            + (P(),) * 6
            + (P(None, FRAME), P(ROW), P(), grid)
        ),
        out_specs=(grid, grid) + (tile,) * 7 + (columns,) * 5,
        check_vma=False,
    )
```

```python
import functools
import itertools
import math

import jax
import jax.numpy as jnp
from jax import lax
from jax.experimental import pallas as pl
from jax.experimental.pallas import tpu as pltpu
from jax.sharding import Mesh
from jax.sharding import PartitionSpec as P

HDIM = 64
EPS = 1e-05
THETA = 10000.0
NEG = -1000000000.0
F32 = jnp.float32
BF16 = jnp.bfloat16
RING = 8
TEAM = ("y", "x")
PLANE = ("z", "core")
GROUP = ("far", "z", "core")
FRAME = ("y", "core")
ROW = ("far", "z", "x")
ALL = ("y", "core", "far", "z", "x")


def swap(value, bits):
    return lax.ppermute(value, TEAM, [(i, i ^ bits) for i in range(4)])


def team_sum(value):
    one, two, three = (swap(value, k) for k in (1, 2, 3))
    return (value + one) + (two + three)


def token_sum(value):
    blocks = value.reshape(value.shape[0], 4, -1)
    one, two, three = (swap(blocks, k) for k in (1, 2, 3))
    pairs = one.reshape(value.shape[0], 2, 2, -1)[:, :, ::-1].reshape(blocks.shape)
    halves = jnp.concatenate([two[:, 2:], two[:, :2]], axis=1)
    return ((blocks + pairs) + (halves + three[:, ::-1])).reshape(value.shape)


def beside(moved, work):
    return (moved, None) if work is None else lax.optimization_barrier((moved, work))


def team_gather(value, work=None):
    others, work = beside([swap(value, k) for k in (3, 2, 1)], work)
    return jnp.stack([value, others[2], others[1], others[0]]), work


def team_scatter(terms, work=None):
    low = terms.astype(BF16)
    others, work = beside([swap(low[k], k) for k in (3, 2, 1)], work)
    return terms[0] + sum(other.astype(F32) for other in others), work


def relocate(block, target):
    sizes = [lax.axis_size(axis) for axis in ALL]
    pairs = []
    for index, where in enumerate(itertools.product(*(range(size) for size in sizes))):
        to = 0
        for size, at in zip(sizes, target(*where)):
            to = to * size + at
        if to != index:
            pairs.append((index, to))
    here = [lax.axis_index(axis) for axis in ALL]
    stays = functools.reduce(lambda a, b: a & b, [a == b for a, b in zip(here, target(*here))])
    return stays, block, lax.ppermute(block, ALL, pairs)


def settled(moved):
    stays, block, received = moved
    return jnp.where(stays, block, received)


def exchange(block):
    return relocate(block, lambda y, core, far, z, x: (y, x, far, z, core))


def piece_member(f, part, parts):
    if parts > 2:
        return f * parts + part
    core = f // 2
    return (f % 2 * 2 + (part ^ core)) * 2 + core


def to_owner(block):
    if lax.axis_size("far") == 1:
        return relocate(block, lambda y, core, far, z, x: (core, z // 2, 0, 2 * y + x, z % 2 ^ core))
    return relocate(block, lambda y, core, far, z, x: (far // 2, far % 2, 2 * y + x, z, core))


def group_gather(block):
    return lax.all_gather(block, GROUP, axis=0, tiled=True)


def group_scatter(terms):
    terms = terms.reshape(-1, terms.shape[-1])
    return lax.psum_scatter(terms, GROUP, scatter_dimension=0, tiled=True)


def row_neighbours(block):
    count = lax.axis_size(ROW)
    forward = [(i, i + 1) for i in range(count - 1)]
    above = lax.ppermute(block, ROW, forward)
    below = lax.ppermute(block, ROW, [(b, a) for a, b in forward])
    return above, below


def to_chunks(value, size):
    blocks, rows, columns = value.shape
    value = value.reshape(blocks, rows, columns // size, size).transpose(0, 2, 1, 3)
    return value.reshape(blocks, -1, size)


def from_chunks(value, rows):
    blocks, _, size = value.shape
    return value.reshape(blocks, -1, rows, size).transpose(0, 2, 1, 3).reshape(blocks * rows, -1)


def owners(pair):
    j, k = divmod(pair, 3)
    if k == 1:
        return [(2 * j, 1, (0, 1)), (2 * j + 1, 1, (2, 3))]
    return [(2 * j + k // 2, 0, (0, 1, 2, 3))]


def q_rows(slot, chunk):
    if slot == 0:
        return 64 * (chunk % 2), chunk // 2
    return 128, chunk % 2


def lanes(shape):
    return lax.broadcasted_iota(jnp.int32, shape, len(shape) - 1)


def half(value, source, target):
    return value if source == target else pltpu.roll(value, 64, 1)


def partner(value):
    lane = lanes(value.shape) % 64
    up8, dn8 = pltpu.roll(value, 120, 1), pltpu.roll(value, 8, 1)
    up12, dn12 = pltpu.roll(value, 116, 1), pltpu.roll(value, 12, 1)
    lower = ((lane >= 16) & (lane < 28)) | ((lane >= 40) & (lane < 52))
    return jnp.where(lane < 8, up8, jnp.where(lane < 16, dn8, jnp.where(lower, up12, dn12)))


def store_queries(out_ref, base, tile, clip, pair_of_heads):
    lane = lanes((64, 128))
    for e in range(2):
        pair = 6 * clip + 2 * pair_of_heads + e
        chunk = [tile[128 * k + 64 * clip : 128 * k + 64 * clip + 64] for k in range(4)]
        for dev, slot, chunks in owners(pair):
            for lo in chunks[: len(chunks) // 2]:
                row, _ = q_rows(slot, lo)
                hi = lo + len(chunks) // 2
                value = jnp.where(lane < 64, half(chunk[lo], e, 0), half(chunk[hi], e, 1))
                out_ref[dev, base + row : base + row + 64, :] = value.astype(out_ref.dtype)


def load_queries(in_ref, base, clip, pair_of_heads):
    lane = lanes((64, 128))
    parts = []
    for e in range(2):
        pair = 6 * clip + 2 * pair_of_heads + e
        found = [None] * 4
        for dev, slot, chunks in owners(pair):
            for c in chunks:
                row, source = q_rows(slot, c)
                value = in_ref[dev, base + row : base + row + 64, :].astype(F32)
                found[c] = half(value, source, e)
        parts.append(found)
    return [jnp.where(lane < 64, a, b) for a, b in zip(*parts)]


def send_kernel(qkv_ref, rs_ref, gain_ref, cos_ref, sin_ref, send_ref, qc_ref):
    lane = lanes((64, 128))
    cosine, sine = cos_ref[...], sin_ref[...]
    rq, rk = rs_ref[:, 0:1], rs_ref[:, 1:2]
    width = 384
    for hp in range(3):
        cut = slice(128 * hp, 128 * hp + 128)
        qn = qkv_ref[:, cut] * rq * gain_ref[0:1, cut]
        kn = qkv_ref[:, width + 128 * hp : width + 128 * hp + 128] * rk * gain_ref[1:2, cut]
        vv = qkv_ref[:, 2 * width + 128 * hp : 2 * width + 128 * hp + 128]
        qc_ref[:, cut] = qn.astype(BF16)
        qr = qn * cosine + partner(qn) * sine
        kr = kn * cosine + partner(kn) * sine
        for clip in range(2):
            store_queries(send_ref, 512, qr, clip, hp)
            for e in range(2):
                for k in range(4):
                    row = 128 * k + 64 * clip
                    kc, vc = kr[row : row + 64], vv[row : row + 64]
                    value = jnp.where(lane < 64, half(kc, e, 0), half(vc, e, 1)).astype(BF16)
                    for dev, slot, _ in owners(6 * clip + 2 * hp + e):
                        at = 256 * slot + 64 * k
                        send_ref[dev, at : at + 64, :] = value


def mix_kernel(o_ref, oc_ref, gate_ref, attn_ref):
    for hp in range(3):
        cut = slice(128 * hp, 128 * hp + 128)
        gate = gate_ref[0:1, cut]
        for clip in range(2):
            for k, chunk in enumerate(load_queries(o_ref, 0, clip, hp)):
                rows = slice(128 * k + 64 * clip, 128 * k + 64 * clip + 64)
                attn_ref[rows, cut] = (chunk + gate * oc_ref[rows, cut]).astype(BF16)


def split_kernel(d_ref, gate_ref, do_ref, doc_ref):
    for hp in range(3):
        cut = slice(128 * hp, 128 * hp + 128)
        tile = d_ref[:, cut]
        doc_ref[:, cut] = (tile * gate_ref[0:1, cut]).astype(BF16)
        for clip in range(2):
            store_queries(do_ref, 0, tile, clip, hp)


def back_kernel(d_ref, dqc_ref, cos_ref, sin_ref, dqn_ref, dkn_ref, dv_ref):
    lane = lanes((64, 128))
    for hp in range(3):
        cut = slice(128 * hp, 128 * hp + 128)
        for clip in range(2):
            queries = load_queries(d_ref, 512, clip, hp)
            for k in range(4):
                rows = slice(128 * k + 64 * clip, 128 * k + 64 * clip + 64)
                cosine, sine = cos_ref[rows, :], sin_ref[rows, :]
                heads = []
                for e in range(2):
                    total = None
                    for dev, slot, _ in owners(6 * clip + 2 * hp + e):
                        at = 256 * slot + 64 * k
                        term = d_ref[dev, at : at + 64, :].astype(F32)
                        total = term if total is None else total + term
                    heads.append(total)
                dk = jnp.where(lane < 64, heads[0], half(heads[1], 0, 1))
                dv = jnp.where(lane < 64, half(heads[0], 1, 0), heads[1])
                dq = queries[k]
                dqn_ref[rows, cut] = dq * cosine + partner(dq * sine) + dqc_ref[rows, cut]
                dkn_ref[rows, cut] = dk * cosine + partner(dk * sine)
                dv_ref[rows, cut] = dv.astype(BF16)


def dot_nt(a, b):
    return lax.dot_general(a, b, (((1,), (1,)), ((), ())), preferred_element_type=F32)


def dot_nn(a, b):
    return lax.dot_general(a, b, (((1,), (0,)), ((), ())), preferred_element_type=F32)


def turned(value):
    return value.astype(F32).T.astype(BF16)


def ff_kernel(hidden_ref, dz_ref, f_in_ref, dgu_ref, out_ref):
    n_rows = out_ref.shape[0]
    part = n_rows // 4
    left = turned(hidden_ref[...])
    tile = left.shape[0] // part

    for c in range(4):
        block = dot_nn(left, dz_ref[:, 384 * c : 384 * c + 384]).astype(BF16)
        for j in range(3):
            for h in range(part):
                out_ref[piece_member(c, h, part), tile * j : tile * j + tile, :] = block[
                    tile * h : tile * h + tile, 128 * j : 128 * j + 128
                ]
    base = 3 * tile
    left_f = turned(f_in_ref[...])
    tile_f = left_f.shape[0] // n_rows

    def gate_up(j, carry):
        block = dot_nn(left_f, dgu_ref[:, pl.ds(pl.multiple_of(256 * j, 128), 256)]).astype(BF16)
        for e in range(2):
            at = pl.multiple_of(base + tile_f * (2 * j + e), 16)
            for r in range(n_rows):
                out_ref[r, pl.ds(at, tile_f), :] = block[
                    tile_f * r : tile_f * r + tile_f, 128 * e : 128 * e + 128
                ]
        return carry

    lax.fori_loop(0, dgu_ref.shape[1] // 256, gate_up, 0)


def out_kernel(attn_ref, dy_ref, dk_ref, dv_ref, dot_ref, out_ref):
    n_rows = out_ref.shape[0]
    wide = dk_ref.shape[0] // n_rows
    tall = 2 * wide + 16
    chunks = dk_ref.shape[1] // 128
    for r in range(n_rows):
        for j in range(chunks):
            cut = slice(128 * j, 128 * j + 128)
            block = jnp.concatenate(
                [
                    dk_ref[wide * r : wide * r + wide, cut],
                    dv_ref[wide * r : wide * r + wide, cut],
                    jnp.broadcast_to(dot_ref[:, cut], (16, 128)),
                ]
            )
            out_ref[r, tall * j : tall * j + tall, :] = block.astype(BF16)
    base = tall * chunks
    left = turned(attn_ref[...])
    tile = left.shape[0] // (n_rows // 4)
    for f in range(4):
        block = dot_nn(left, dy_ref[:, 384 * f : 384 * f + 384]).astype(BF16)
        for part in range(n_rows // 4):
            member = piece_member(f, part, n_rows // 4)
            for j in range(3):
                out_ref[member, base + tile * j : base + tile * j + tile, :] = block[
                    tile * part : tile * part + tile, 128 * j : 128 * j + 128
                ]


def dot_tt(a, b):
    return lax.dot_general(a, b, (((0,), (1,)), ((), ())), preferred_element_type=F32)


def block_of(ref, i, base):
    at = pl.multiple_of(base + 64 * (i // 4), 64)
    return ref[pl.ds(2 * (i % 4), 2), pl.ds(at, 64), :].reshape(128, 128).astype(F32)


def put_block(ref, i, base, value):
    at = pl.multiple_of(base + 64 * (i // 4), 64)
    ref[pl.ds(2 * (i % 4), 2), pl.ds(at, 64), :] = value.reshape(2, 64, 128).astype(ref.dtype)


def slot_keys(kv_ref, slot):
    return kv_ref[:, pl.ds(pl.multiple_of(256 * slot, 256), 256), :].reshape(-1, 128)


def self_kernel(kv_ref, q_ref, o_ref, ot_ref, lse_ref, kvt_ref):
    lane = lanes((128, 128))
    for slot in range(2):
        kvt_ref[slot] = turned(slot_keys(kv_ref, slot))

    def step(i, carry):
        slot = i // 8
        q = block_of(q_ref, i, 512) * (HDIM ** (-0.5))
        qa = jnp.where(lane < 64, q, 0.0)
        qb = jnp.where(lane < 64, pltpu.roll(q, 64, 1), 0.0)
        q2 = jnp.concatenate([qa, qb], axis=0).astype(BF16)
        s = dot_nt(slot_keys(kv_ref, slot), q2)
        top = jnp.max(s, axis=0, keepdims=True)
        p = jnp.exp(s - top)
        total = jnp.sum(p, axis=0, keepdims=True)
        ot = dot_nn(kvt_ref[slot], p.astype(BF16)) / total
        o = ot.T
        put_block(o_ref, i, 0, jnp.where(lane < 64, pltpu.roll(o[:128], 64, 1), o[128:]))
        ot_ref[pl.ds(i, 1)] = ot[64:].reshape(1, 64, 256)
        lse_ref[pl.ds(i, 1)] = (top + jnp.log(total)).reshape(1, 1, 256)
        return carry

    lax.fori_loop(0, 12, step, 0)


def self_back_kernel(merged, kv_ref, q_ref, do_ref, ot_ref, lse_ref, *rest):
    if merged:
        dkv_ref, acc_ref, kvt_ref = rest
        dq_ref, base = dkv_ref, 512
    else:
        dkv_ref, dq_ref, acc_ref, kvt_ref = rest
        base = 0
    lane = lanes((128, 128))
    for slot in range(2):
        kvt_ref[slot] = turned(slot_keys(kv_ref, slot))
    acc_ref[...] = jnp.zeros_like(acc_ref)

    def step(i, carry):
        slot = i // 8
        q = block_of(q_ref, i, 512) * (HDIM ** (-0.5))
        d = block_of(do_ref, i, 0)
        qa = jnp.where(lane < 64, q, 0.0)
        qb = jnp.where(lane < 64, pltpu.roll(q, 64, 1), 0.0)
        q2 = jnp.concatenate([qa, qb], axis=0).astype(BF16)
        da = jnp.where(lane < 64, 0.0, pltpu.roll(d, 64, 1))
        db = jnp.where(lane < 64, 0.0, d)
        d2 = jnp.concatenate([da, db], axis=0)
        delta = jnp.sum(d2.T[64:] * ot_ref[pl.ds(i, 1)].reshape(64, 256), axis=0, keepdims=True)
        d2 = d2.astype(BF16)
        kv = slot_keys(kv_ref, slot)
        p = jnp.exp(dot_nt(kv, q2) - lse_ref[pl.ds(i, 1)].reshape(1, 256))
        ds = (p * (dot_nt(kv, d2) - delta)).astype(BF16)
        acc_ref[slot] += dot_nn(ds, q2) + dot_nn(p.astype(BF16), d2)
        dq = dot_nn(kvt_ref[slot], ds).T * (HDIM ** (-0.5))
        put_block(dq_ref, i, base, jnp.where(lane < 64, dq[:128], pltpu.roll(dq[128:], 64, 1)))
        return carry

    lax.fori_loop(0, 12, step, 0)
    for slot in range(2):
        dkv_ref[:, 256 * slot : 256 * slot + 256, :] = (
            acc_ref[slot].reshape(-1, 256, 128).astype(dkv_ref.dtype)
        )


def cross_probs(kc, q, bias, lane, e):
    qm = jnp.where((lane < 64) == (e == 0), q, jnp.zeros_like(q))
    s = jnp.where(bias > 0.0, dot_tt(kc, qm) * (HDIM ** (-0.5)), NEG)
    p = jnp.exp(s - jnp.max(s, axis=0, keepdims=True))
    return p / jnp.sum(p, axis=0, keepdims=True), qm


def cross_kernel(q_ref, kc_ref, vc_ref, bias_ref, o_ref):
    q = q_ref[...].reshape(256, 128)
    lane = lanes((256, 128))
    bias = bias_ref[...]
    outs = []
    for e in range(2):
        p, _ = cross_probs(kc_ref[...], q, bias, lane, e)
        outs.append(dot_tt(p.astype(BF16), vc_ref[...]))
    o_ref[...] = jnp.where(lane < 64, outs[0], outs[1]).reshape(4, 1, 64, 128)


def cross_back_kernel(q_ref, kc_ref, vc_ref, bias_ref, do_ref, dq_ref, dk_ref, dv_ref):
    q = q_ref[...].reshape(256, 128)
    d = do_ref[...].reshape(256, 128)
    lane = lanes((256, 128))
    bias = bias_ref[...]
    kc, vc = kc_ref[...], vc_ref[...]
    dqs, dk, dv = [], 0.0, 0.0
    for e in range(2):
        p, qm = cross_probs(kc, q, bias, lane, e)
        dm = jnp.where((lane < 64) == (e == 0), d, jnp.zeros_like(d))
        dp = dot_tt(vc, dm)
        dt = (p * (dp - jnp.sum(p * dp, axis=0, keepdims=True))).astype(BF16)
        dqs.append(dot_tt(dt, kc))
        dk = dk + dot_tt(qm, dt)
        dv = dv + dot_tt(dm, p.astype(BF16))
    dq = jnp.where(lane < 64, dqs[0], dqs[1]) * (HDIM ** (-0.5))
    dq_ref[...] = dq.reshape(4, 1, 64, 128)
    dk_ref[...] = dk * (HDIM ** (-0.5))
    dv_ref[...] = dv


def call(kernel, outs, *args, scratch=(), flops=0, grant=16):
    size = sum(math.prod(a.shape) * a.dtype.itemsize for a in (*args, *outs))
    spec = pl.BlockSpec(memory_space=pltpu.VMEM)
    return pl.pallas_call(
        kernel,
        out_shape=outs,
        in_specs=[spec] * len(args),
        out_specs=[spec] * len(outs),
        scratch_shapes=list(scratch),
        compiler_params=pltpu.CompilerParams(vmem_limit_bytes=grant << 20),
        cost_estimate=pl.CostEstimate(flops=flops, bytes_accessed=size, transcendentals=flops // 256),
    )(*args)


def cross_call(kernel, outs, specs, *args):
    token = pl.BlockSpec((4, 1, 64, 128), lambda c, h: (0, c, 0, h))
    bias = pl.BlockSpec((256, 1), lambda c, h: (c, 0))
    back = pl.BlockSpec((128, 256), lambda c, h: (h, c))
    kinds = {"t": token, "b": bias, "o": back}
    return pl.pallas_call(
        kernel,
        grid=(2, 3),
        out_shape=outs,
        in_specs=[kinds[c] for c in specs[0]],
        out_specs=[kinds[c] for c in specs[1]],
        compiler_params=pltpu.CompilerParams(vmem_limit_bytes=16 << 20),
        cost_estimate=pl.CostEstimate(
            flops=12 * len(args) * 256 * 256 * 128, bytes_accessed=4 << 20, transcendentals=12 << 16
        ),
    )(*args)


def feed_kernel(f_in_ref, w_gu_ref, w_dn_ref, gu_ref, hidden_ref, z_ref):
    half_w = hidden_ref.shape[1]
    z_ref[...] = jnp.zeros_like(z_ref)

    def step(j, carry):
        at = pl.multiple_of(256 * j, 256)
        up_at = pl.multiple_of(half_w + 256 * j, 256)
        gate = dot_nn(f_in_ref[...], w_gu_ref[:, pl.ds(at, 256)])
        up = dot_nn(f_in_ref[...], w_gu_ref[:, pl.ds(up_at, 256)])
        gu_ref[:, pl.ds(at, 256)] = gate
        gu_ref[:, pl.ds(up_at, 256)] = up
        hidden = (gate * jax.nn.sigmoid(gate) * up).astype(BF16)
        hidden_ref[:, pl.ds(at, 256)] = hidden
        z_ref[...] += dot_nn(hidden, w_dn_ref[pl.ds(at, 256), :])
        return carry

    lax.fori_loop(0, half_w // 256, step, 0)


def feed_back_kernel(dz_ref, w_dn_ref, gu_ref, w_gu_ref, dgu_ref, df_ref):
    half_w = w_dn_ref.shape[0]
    df_ref[...] = jnp.zeros_like(df_ref)

    def step(j, carry):
        at = pl.multiple_of(256 * j, 256)
        up_at = pl.multiple_of(half_w + 256 * j, 256)
        d_hidden = dot_nt(dz_ref[...], w_dn_ref[pl.ds(at, 256), :])
        gate, up = gu_ref[:, pl.ds(at, 256)], gu_ref[:, pl.ds(up_at, 256)]
        sigma = jax.nn.sigmoid(gate)
        d_gate = (d_hidden * up * (sigma * (1.0 + gate * (1.0 - sigma)))).astype(BF16)
        d_up = (d_hidden * (gate * sigma)).astype(BF16)
        dgu_ref[:, pl.ds(at, 256)] = d_gate
        dgu_ref[:, pl.ds(up_at, 256)] = d_up
        df_ref[...] += dot_nt(d_gate, w_gu_ref[:, pl.ds(at, 256)])
        df_ref[...] += dot_nt(d_up, w_gu_ref[:, pl.ds(up_at, 256)])
        return carry

    lax.fori_loop(0, half_w // 256, step, 0)


def shaped(shape, dtype=F32):
    return jax.ShapeDtypeStruct(shape, dtype)


def rms_norm(tensor, gain):
    return tensor * lax.rsqrt(jnp.mean(tensor * tensor, axis=-1, keepdims=True) + EPS) * gain


def rotary_lanes():
    parts = ((0, 16), (1, 24), (2, 24))
    freqs = [[], [], []]
    signs = []
    for which, size in parts:
        for upper in range(2):
            for i in range(size // 2):
                for p in range(3):
                    freqs[p].append(math.exp(-math.log(THETA) * 2.0 * i / size) if p == which else 0.0)
                signs.append(1.0 if upper else -1.0)
    return [jnp.array(f, F32) for f in freqs], jnp.array(signs, F32)


def mm(a, b):
    return jnp.dot(a, b, preferred_element_type=F32)


def body(
    tokens,
    w_query,
    w_key,
    w_value,
    w_out,
    w_gate,
    w_up,
    w_down,
    w_cap_key,
    w_cap_value,
    w_mod,
    norm_gains,
    mix_coefs,
    caption,
    cap_len,
    cap_mask,
    timesteps,
    frame_pos,
    row_pos,
    col_pos,
    grad_out,
):
    clips, frames, rows_here, cols, width = tokens.shape
    local = frames * rows_here * cols
    group = lax.axis_size("y") * lax.axis_size("x")
    n_rows = lax.axis_size(ROW)
    n_far = lax.axis_size("far")
    n_all = group * n_rows
    me = lax.axis_index(TEAM)
    my_member = lax.axis_index(GROUP)
    heads_w = width // group
    ff_w = w_gate.shape[1] // group
    count = group * clips * local
    caps = caption.shape[1]
    share = width // n_all

    rows = w_query.shape[0]
    cap2 = caption.reshape(clips * caps, width)

    def by_columns(parts):
        cut = jnp.concatenate([w.reshape(rows, group, -1) for w in parts], axis=2)
        cut = lax.all_to_all(cut.transpose(1, 0, 2), TEAM, 0, 0)
        return cut.reshape(group * rows, -1)

    def in_order(gathered):
        full = gathered.reshape(n_far, RING // 2, 2, 2, 2, rows, -1).transpose(3, 2, 0, 1, 4, 5, 6)
        return full.reshape(width, -1)

    def cap_columns(weight):
        return lax.dot_general(weight, cap2, (((0,), (1,)), ((), ())), preferred_element_type=F32).astype(BF16)

    cut_qkv = by_columns([w_query, w_key, w_value])

    half_width = width // 2
    frequencies = jnp.exp(-math.log(THETA) * jnp.arange(half_width, dtype=F32) / half_width)
    phases = timesteps.astype(F32)[:, None] * frequencies[None, :]
    step_embed = jax.nn.silu(jnp.concatenate([jnp.cos(phases), jnp.sin(phases)], axis=1)).astype(BF16)
    mod_local = mm(step_embed, w_mod).astype(BF16).astype(F32)
    mod_cols = mod_local.shape[1]
    note = jnp.concatenate([mod_local.reshape(-1), frame_pos.astype(F32).reshape(-1), row_pos.astype(F32)])
    used = note.shape[0]
    note = jnp.pad(note, (0, -used % 512)).reshape(1, -1, 128)
    note = lax.all_to_all(jnp.broadcast_to(note, (n_all,) + note.shape[1:]), ALL, 0, 0)
    note, (w_gate, w_up) = beside(note, (w_gate, w_up))
    cut_gu = by_columns([w_gate, w_up])
    note = note.reshape(n_all, -1)
    x_own = tokens.reshape(clips, local, width)
    x_flat = x_own.astype(F32)
    x_group, _ = team_gather(x_own)
    w_qkv = in_order(group_gather(cut_qkv))
    tokens_c = clips * caps
    blank = jnp.zeros((rows, width - 2 * tokens_c), BF16)
    cap_rows = jnp.concatenate([cap_columns(w_cap_key), cap_columns(w_cap_value), blank], axis=1)
    side = group_gather(settled(exchange(jnp.concatenate([w_out, cap_rows]))))
    down_rows = settled(exchange(w_down))
    mod_full = note[:, : clips * mod_cols].reshape(n_all, clips, mod_cols)
    mod_full = mod_full.transpose(1, 0, 2).reshape(clips, 4, width)
    scale_a, gate_a, scale_f, gate_f = (mod_full[:, i] for i in range(4))
    positions = note[:, clips * mod_cols : used].reshape(2, 2, n_far, RING // 2, 2, -1)
    here = [lax.axis_index(axis) for axis in ("core", "far", "z")]
    positions = lax.dynamic_slice(positions, (0, *here, 0, 0), (2, 1, 1, 1, 2, positions.shape[-1]))
    order = jnp.arange(group)
    chosen = (order[None, :] == (me ^ order)[:, None]).astype(F32)
    positions = jnp.sum(chosen[:, :, None] * positions.reshape(1, group, -1), axis=1)

    gains = norm_gains
    own_gains = lax.dynamic_slice(gains, (4, me * heads_w), (3, heads_w))
    own_gate = jnp.tanh(lax.dynamic_slice(mix_coefs, (0, me * heads_w), (1, heads_w)))

    full = (group, clips, frames, cols)
    frame_at = positions[:, :-1].reshape(group, clips, frames) + cap_len.astype(F32)[None, :, None]
    pos_a = jnp.broadcast_to(frame_at[..., None], full)
    pos_b = jnp.broadcast_to(positions[:, -1:, None, None], full)
    pos_e = jnp.broadcast_to(col_pos.astype(F32), full)
    (fa, fb, fe), sign = rotary_lanes()
    angle = (
        pos_a.reshape(count, 1) * fa + pos_b.reshape(count, 1) * fb + pos_e.reshape(count, 1) * fe
    )
    cosine = jnp.tile(jnp.cos(angle), (1, 2))
    sine = jnp.tile(jnp.sin(angle) * sign, (1, 2))

    def pre_piece(x_in, gain, scale_in):
        return rms_norm(x_in, gain) * (1.0 + scale_in[:, None, :])

    h_in = pre_piece(x_group.astype(F32), gains[0], scale_a).astype(BF16).reshape(count, width)
    h_in = lax.optimization_barrier(h_in)
    _, pre_back = jax.vjp(pre_piece, x_flat, gains[0], scale_a)
    qkv = mm(h_in, w_qkv)
    q_zero, k_zero = qkv[:, :heads_w], qkv[:, heads_w : 2 * heads_w]
    squares = jnp.stack([jnp.sum(q_zero * q_zero, axis=1), jnp.sum(k_zero * k_zero, axis=1)])
    rsq = lax.rsqrt(token_sum(squares) / width + EPS).T
    send, q_cap = call(
        send_kernel,
        [shaped((RING, 704, 128), BF16), shaped((count, heads_w), BF16)],
        qkv,
        rsq,
        own_gains,
        cosine,
        sine,
    )
    side = side.reshape(n_rows, -1, width)
    w_o = side[:, :rows].reshape(-1, width)
    k_pre_t = side[:, rows:, :tokens_c].reshape(-1, tokens_c)
    v_cap_t = side[:, rows:, tokens_c : 2 * tokens_c].reshape(-1, tokens_c)

    usable = (jnp.arange(caps)[None, :] < cap_len[:, None]) & (cap_mask > 0)
    bias = usable.astype(F32).reshape(clips * caps, 1)
    k_pre_t = k_pre_t.astype(F32)
    gain_cap = own_gains[2][:, None]
    r_cap = lax.rsqrt(team_sum(jnp.sum(k_pre_t * k_pre_t, axis=0, keepdims=True)) / width + EPS)
    k_cap_t = (k_pre_t * r_cap * gain_cap).astype(BF16)
    got, (k_pre_t, r_cap, k_cap_t, v_cap_t, w_o, cut_gu, down_rows, (above_g, below_g)) = beside(
        lax.all_to_all(send, PLANE, 0, 0),
        (k_pre_t, r_cap, k_cap_t, v_cap_t, w_o, cut_gu, down_rows, row_neighbours(grad_out)),
    )
    w_gu = group_gather(cut_gu)
    kv_all = got
    if n_far > 1:
        kv_all = lax.all_gather(got, "far", axis=0, tiled=True)
    keys = kv_all.shape[0] * 256
    work = 12 * keys * 256 * 128 * 2
    o_pack, o_t, lse = call(
        self_kernel,
        [shaped((RING, 192, 128), BF16), shaped((12, 64, 256)), shaped((12, 1, 256))],
        kv_all,
        got,
        scratch=[pltpu.VMEM((2, 128, keys), BF16)],
        flops=2 * work,
        grant=24 if n_far == 1 else 56,
    )
    o_back = lax.all_to_all(o_pack, PLANE, 0, 0)

    q_cap4 = q_cap.reshape(group, clips, local, heads_w)
    (out_cross,) = cross_call(
        cross_kernel, [shaped(q_cap4.shape)], ("toob", "t"), q_cap4, k_cap_t, v_cap_t, bias
    )
    o_back, out_cross = beside(o_back, out_cross)
    out_cross = out_cross.reshape(count, heads_w)
    (attn_mix,) = call(mix_kernel, [shaped((count, heads_w), BF16)], o_back, out_cross, own_gate)

    y_one, (w_gu, down_rows) = team_scatter(
        mm(attn_mix, w_o).reshape(group, clips, local, width), (w_gu, down_rows)
    )
    w_dn = group_gather(down_rows)

    def mid_piece(x_in, y_in, gain_two, gate_in, gain_three, scale_in):
        h_mid = x_in + jnp.tanh(gate_in)[:, None, :] * rms_norm(y_in, gain_two)
        return (h_mid, rms_norm(h_mid, gain_three) * (1.0 + scale_in[:, None, :]))

    (h_mid, f_in32), mid_back = jax.vjp(mid_piece, x_flat, y_one, gains[1], gate_a, gains[2], scale_f)
    f_in, w_gu = team_gather(f_in32.astype(BF16), in_order(w_gu))
    f_in = f_in.reshape(count, width)
    gate_up, hidden, z_terms = call(
        feed_kernel,
        [shaped((count, 2 * ff_w)), shaped((count, ff_w), BF16), shaped((count, width))],
        f_in,
        w_gu,
        w_dn,
        flops=6 * count * width * ff_w,
        grant=24,
    )
    z_out, _ = team_scatter(z_terms.reshape(group, clips, local, width))

    def end_piece(h_in_mid, z_in, gain_four, gate_in):
        return h_in_mid + jnp.tanh(gate_in)[:, None, :] * rms_norm(z_in, gain_four)

    y_all, end_back = jax.vjp(end_piece, h_mid, z_out, gains[3], gate_f)
    y_grid = y_all.reshape(tokens.shape)
    above, below = row_neighbours(y_grid.astype(BF16))
    g_center = grad_out.astype(F32)
    d_y = g_center + mix_coefs[1] * below_g.astype(F32) + mix_coefs[2] * above_g.astype(F32)
    d_h_end, d_z, d_g_four, d_gate_f = end_back(d_y.reshape(clips, local, width))
    d_z_all, _ = team_gather(d_z.astype(BF16))
    d_z_all = d_z_all.reshape(count, width)
    d_gu, d_f_in = call(
        feed_back_kernel,
        [shaped((count, 2 * ff_w), BF16), shaped((count, width))],
        d_z_all,
        w_dn,
        gate_up,
        w_gu,
        flops=6 * count * width * ff_w,
        grant=24,
    )

    def term(left, right):
        return lax.dot_general(left, right, (((0,), (0,)), ((), ())), preferred_element_type=F32).astype(BF16)

    ff_rows = (w_down.shape[0] * group * (heads_w // 128), width // n_rows * (2 * ff_w // 128))
    (ff_terms,) = call(
        ff_kernel,
        [shaped((n_rows, sum(ff_rows), 128), BF16)],
        hidden,
        d_z_all,
        f_in,
        d_gu,
        flops=6 * count * width * ff_w,
        grant=24,
    )
    d_f_in, ff_terms = team_scatter(d_f_in.reshape(group, clips, local, width), ff_terms)
    ff_sum = group_scatter(ff_terms)
    d_x_mid, d_y_one, d_g_two, d_gate_a, d_g_three, d_scale_f = mid_back((d_h_end, d_f_in))
    d_y_group, _ = team_gather(d_y_one.astype(BF16))
    d_y_group = d_y_group.reshape(count, width)
    d_attn = lax.dot_general(d_y_group, w_o, (((1,), (1,)), ((), ())), preferred_element_type=F32)

    d_pack, d_cross = call(
        split_kernel, [shaped((RING, 192, 128), BF16), shaped((count, heads_w), BF16)], d_attn, own_gate
    )
    d_got = lax.all_to_all(d_pack, PLANE, 0, 0)
    d_mix_gate = jnp.sum(d_attn * out_cross, axis=0) * (1.0 - own_gate[0] * own_gate[0])
    back_scratch = [pltpu.VMEM((2, keys, 128), F32), pltpu.VMEM((2, 128, keys), BF16)]
    if n_far == 1:
        (d_send,) = call(
            functools.partial(self_back_kernel, True),
            [shaped((RING, 704, 128), BF16)],
            kv_all,
            got,
            d_got,
            o_t,
            lse,
            scratch=back_scratch,
            flops=5 * work,
            grant=26 if n_far == 1 else 60,
        )
    else:
        d_kv, d_q = call(
            functools.partial(self_back_kernel, False),
            [shaped((kv_all.shape[0], 512, 128), BF16), shaped((RING, 192, 128), BF16)],
            kv_all,
            got,
            d_got,
            o_t,
            lse,
            scratch=back_scratch,
            flops=5 * work,
            grant=26 if n_far == 1 else 60,
        )
        d_kv = lax.psum_scatter(d_kv, "far", scatter_dimension=0, tiled=True)
        d_send = jnp.concatenate([d_kv, d_q], axis=1)
    d_send, (above, below, d_cross) = beside(d_send, (above, below, d_cross))
    d_q_cross, d_k_cap, d_v_cap = cross_call(
        cross_back_kernel,
        [shaped(q_cap4.shape), shaped((heads_w, clips * caps)), shaped((heads_w, clips * caps))],
        ("toobt", "too"),
        q_cap4,
        k_cap_t,
        v_cap_t,
        bias,
        d_cross.reshape(q_cap4.shape),
    )
    above, below = above.astype(F32), below.astype(F32)
    output = (y_grid + mix_coefs[1] * above + mix_coefs[2] * below).astype(BF16)
    d_above = jnp.sum(g_center * above, axis=(0, 1, 2, 3))
    d_below = jnp.sum(g_center * below, axis=(0, 1, 2, 3))
    cap_dot = team_sum(jnp.sum(d_k_cap * gain_cap * k_pre_t, axis=0, keepdims=True))
    wide = heads_w // n_rows
    tile = width // n_rows
    cut = (2 * wide + 16) * (clips * caps // 128)
    (out_terms,) = call(
        out_kernel,
        [shaped((n_rows, cut + tile * (heads_w // 128), 128), BF16)],
        attn_mix,
        d_y_group,
        d_k_cap,
        d_v_cap,
        cap_dot,
        flops=2 * count * width * heads_w,
    )

    def spread(block):
        return lax.dynamic_update_slice(jnp.zeros((width,), F32), block, (me * heads_w,))

    def owners_sum(mods, rows_in):
        first = mods.reshape(clips, -1, mod_cols).transpose(1, 0, 2).reshape(-1, clips * mod_cols)
        first = jnp.pad(first, ((0, n_all - first.shape[0]), (0, 0)))
        other = lax.optimization_barrier(jnp.stack(rows_in))
        other = other.reshape(len(rows_in), n_all, share).transpose(1, 0, 2).reshape(n_all, -1)
        both = jnp.concatenate([first, other], axis=1)
        both = jnp.pad(both, ((0, 0), (0, -both.shape[1] % 128))).reshape(n_all, -1, 128)
        both = jnp.sum(lax.all_to_all(both, ALL, 0, 0), axis=0).reshape(-1)
        cut = clips * mod_cols
        return both[:cut].reshape(clips, mod_cols), both[cut : cut + len(rows_in) * share].reshape(-1, share)

    d_recv, (output, out_terms, ff_sum, d_q_cross) = beside(
        lax.all_to_all(d_send, PLANE, 0, 0), (output, out_terms, ff_sum, d_q_cross)
    )
    out_sum = group_scatter(out_terms)
    d_qn, d_kn, d_v = call(
        back_kernel,
        [shaped((count, heads_w)), shaped((count, heads_w)), shaped((count, heads_w), BF16)],
        d_recv,
        d_q_cross.reshape(count, heads_w),
        cosine,
        sine,
    )
    rq, rk = rsq[:, 0:1], rsq[:, 1:2]
    d_g_query = jnp.sum(d_qn * q_zero * rq, axis=0)
    d_g_key = jnp.sum(d_kn * k_zero * rk, axis=0)
    a_q, a_k = d_qn * own_gains[0], d_kn * own_gains[1]
    dots = token_sum(jnp.stack([jnp.sum(a_q * q_zero, axis=1), jnp.sum(a_k * k_zero, axis=1)])).T / width
    d_q_low = (rq * a_q - q_zero * (rq * rq * rq * dots[:, 0:1])).astype(BF16)
    d_k_low = (rk * a_k - k_zero * (rk * rk * rk * dots[:, 1:2])).astype(BF16)
    d_qkv = jnp.concatenate([d_q_low, d_k_low, d_v], axis=1)
    d_h_in = lax.dot_general(d_qkv, w_qkv, (((1,), (1,)), ((), ())), preferred_element_type=F32)
    d_h_in, (term_qkv, out_sum) = team_scatter(
        d_h_in.reshape(group, clips, local, width), (term(h_in, d_qkv), out_sum)
    )
    qkv_sum = group_scatter(term_qkv)
    d_x_pre, d_g_zero, d_scale_a = pre_back(d_h_in)
    grad_tokens = (d_x_pre + d_x_mid).reshape(tokens.shape)
    d_g_zero, (ff_sum, out_sum) = beside(d_g_zero, (ff_sum, out_sum))

    d_mod, sums = owners_sum(
        jnp.concatenate([d_scale_a, d_gate_a, d_scale_f, d_gate_f], axis=1),
        [
            d_g_zero,
            d_g_two,
            d_g_three,
            d_g_four,
            spread(d_g_query),
            spread(d_g_key),
            spread(d_mix_gate),
            d_above,
            d_below,
        ],
    )
    cap_sum = from_chunks(out_sum[None, :cut].astype(F32), 2 * wide + 16)
    d_k_own, d_v_own, cap_dot = cap_sum[:wide], cap_sum[wide : 2 * wide], cap_sum[2 * wide : 2 * wide + 1]
    k_own = lax.dynamic_slice(k_pre_t, (my_member * wide, 0), (wide, clips * caps))
    g_own = lax.dynamic_slice(gain_cap, (my_member * wide, 0), (wide, 1))
    caps_gain = exchange(jnp.sum(d_k_own * k_own * r_cap, axis=1)[None])
    d_k_zero_cap = r_cap * g_own * d_k_own - k_own * (r_cap * r_cap * r_cap * cap_dot / width)
    moved = [
        caps_gain,
        exchange(jnp.concatenate([d_k_zero_cap, d_v_own]).astype(BF16)),
        exchange(ff_sum[ff_rows[0] :]),
    ]
    d_mod, received = beside(d_mod, [m[2] for m in moved])
    d_g_cap, d_caps, sum_gu = (settled((*m[:2], r)) for m, r in zip(moved, received))
    d_w_mod = lax.dot_general(
        step_embed, d_mod.astype(BF16), (((0,), (0,)), ((), ())), preferred_element_type=F32
    )
    sum_gate, sum_up = jnp.split(sum_gu, 2)

    def result(block):
        return from_chunks(block[None], tile).astype(F32)

    def cap_weight(d):
        return lax.dot_general(cap2, d, (((0,), (1,)), ((), ())), preferred_element_type=F32)

    d_w_cap_key = cap_weight(d_caps[:wide])
    d_w_cap_value = cap_weight(d_caps[wide:])
    d_gains = jnp.concatenate([sums[:6], d_g_cap], axis=0)
    mine = w_down.shape[0] * group
    owned = jnp.concatenate(
        [from_chunks(ff_sum[None, : ff_rows[0]], mine), from_chunks(out_sum[None, cut:], tile)]
    )
    ready = (
        result(sum_gate),
        result(sum_up),
        d_w_cap_key,
        d_w_cap_value,
        d_w_mod,
        d_gains,
        sums[6:],
    )
    owned, qkv_sum = beside(owned, qkv_sum)
    moved = to_owner(owned), exchange(qkv_sum)
    received, ready = beside([m[2] for m in moved], ready)
    owned, qkv_sum = (settled((*m[:2], r)).astype(F32) for m, r in zip(moved, received))
    gate_grad, up_grad, *ready = ready
    return (
        output,
        grad_tokens,
        qkv_sum[:, :heads_w],
        qkv_sum[:, heads_w : 2 * heads_w],
        qkv_sum[:, 2 * heads_w :],
        owned[mine:],
        gate_grad,
        up_grad,
        owned[:mine],
        *ready,
    )


def solution(mesh):
    frame, row = mesh.shape["frame"], mesh.shape["row"]
    fine = Mesh(mesh.devices.reshape(frame // 2, 2, row // RING, RING // 2, 2), ALL)
    grid = P(None, FRAME, ROW, None, None)
    rows, columns = P(ALL, None), P(None, ALL)
    tile = P(ROW, FRAME)
    return jax.shard_map(
        body,
        mesh=fine,
        in_specs=(
            (grid,)
            + (rows,) * 7
            + (columns,) * 3
            + (P(),) * 6
            + (P(None, FRAME), P(ROW), P(), grid)
        ),
        out_specs=(grid, grid) + (tile,) * 7 + (columns,) * 5,
        check_vma=False,
    )
```
